32 devices in a mesh: groups: 2 (over x), tm: 16 (over z, y, core).
Axes of the slice: x: 2, y: 2, z: 4, core: 2. Of those that a mesh axis runs over, the one named last changes fastest.
Arguments:
- token_ids: int32 [4096, 8], P(('groups', 'tm')), parts along dimension 0, may hold values from 0 to 127
- field_offsets: int32 [16], P('groups'), parts along dimension 0, may hold values from 0 to 896
- embed_table: bfloat16 [1024, 1024], replicated, may hold values from -2.09375 to 2.09375
- w_in: bfloat16 [1024, 3072], P('tm'), may hold values from -0.1875 to 0.1875
- short_taps: float32 [3, 3072], replicated, may hold values from -1 to 1
- filters: bfloat16 [2, 1024, 2048], P(None, 'tm'), may hold values from -1.1 to 1.1
- cotangent: bfloat16 [4096, 1024], P(('groups', 'tm')), parts along dimension 0, may hold values from -0.125 to 0.125
Outputs:
- mixer_out: bfloat16 [4096, 1024], P(('groups', 'tm')), parts along dimension 0
- weight_grads: float32 [2048, 3072], P(('groups', 'tm')), parts along dimension 0
- tap_grads: float32 [6, 3072], P('groups'), parts along dimension 0
- filter_grads: float32 [4, 1024, 2048], P('groups', 'tm'), parts along dimension 0
The draws below stay inside these ranges and needn't reach their ends.
There are 2 independent parts, one for each index of `groups`. The reference program is written for one: setup_inputs(seed, part) draws one part's arguments, and reference() takes and returns one part's arrays. A program takes and returns all parts, laid end to end along the dimension named above; an argument that names none is the same for every part. Nothing has to cross between parts.
All inputs are finite; a program needn't handle non-finite values.
Results may differ from the reference program's by a relative error of at most 0.035.
Values may be sent and summed in bfloat16 or wider, within the bound.
A program may use at most 128 MiB of HBM per device.

```python
import jax
import jax.numpy as jnp

D = 1024
S = 8
K = 128
V = 1024
TOKENS = 2048


def draw_filters(key, part):
    key_rate, key_noise = jax.random.split(key)
    length = TOKENS
    low = jnp.log(0.25 / length)
    high = jnp.log(1.0 / 30.0)
    rate = jnp.exp(jax.random.uniform(key_rate, (2, D, 1), jnp.float32, low, high))
    lag = jnp.arange(length, dtype=jnp.float32)[None, None, :]
    envelope = jnp.sqrt(2.0 * rate) * jnp.exp(-rate * lag)
    noise = jnp.clip(jax.random.normal(key_noise, (2, D, length), jnp.float32), -4.0, 4.0)
    return (envelope * noise).astype(jnp.bfloat16)


def with_ends(array, stream_key, smallest, high):
    longest = array.shape.index(max(array.shape))
    spots = []
    for shift in (0, 1):
        where = [jax.random.randint(jax.random.fold_in(stream_key, axis), (), 0, length) for axis, length in enumerate(array.shape)]
        where[longest] = (where[longest] + shift) % array.shape[longest]
        spots.append(tuple(where))
    return array.at[spots[0]].set(smallest).at[spots[1]].set(high)


def levels(key, shape, cuts, smallest, largest):
    factor_of, own = 1.0, jax.random.fold_in(key, 6)
    for position, blocks in cuts:
        steps = jnp.exp(jax.random.uniform(jax.random.fold_in(own, position), (blocks,), jnp.float32, smallest / len(cuts), largest / len(cuts)))
        factor_of = factor_of * jnp.repeat(steps, shape[position] // blocks).reshape([-1 if axis == position else 1 for axis in range(len(shape))])
    return factor_of


def gaussian(rng, dims, width, limit, shards=(), kind=jnp.bfloat16):
    array = jax.random.normal(rng, dims, jnp.float32) * width
    if len(shards) > 0:
        array = levels(rng, dims, shards, -0.22, 0.18) * array
    return jnp.clip(array, min=-limit, max=limit).astype(kind)


def setup_inputs(seed: int = 0, part: int = 0) -> dict:
    splits = jax.random.split(jax.random.key(seed), 8)
    part_keys = jax.random.split(jax.random.fold_in(splits[7], part), 8)
    return {
        "token_ids": with_ends(jax.random.randint(part_keys[0], (TOKENS, S), 0, K), jax.random.fold_in(part_keys[0], 1), 0, K - 1).astype(jnp.int32),
        "field_offsets": with_ends(jax.random.randint(part_keys[1], (S,), 0, V - K + 1), jax.random.fold_in(part_keys[1], 1), 0, V - K).astype(jnp.int32),
        "embed_table": gaussian(splits[2], (V, D), 0.35, 2.09375),
        "w_in": gaussian(splits[3], (D, 3 * D), D ** -0.5, 0.1875, ((0, 16),)),
        "short_taps": jnp.clip(jax.random.uniform(splits[4], (3, 3 * D), jnp.float32, -1.0, 1.0), -1.0, 1.0),
        "filters": draw_filters(jax.random.fold_in(splits[7], 71), part),
        "cotangent": gaussian(part_keys[6], (TOKENS, D), (TOKENS ** -0.5), 0.125, ((0, 16),)),
    }


def reference(token_ids, field_offsets, embed_table, w_in, short_taps, filters, cotangent):
    row_index = (token_ids + field_offsets[None, :]).astype(jnp.int32)
    embedded = jnp.sum(jnp.take(embed_table, row_index, axis=0).astype(jnp.float32), axis=1).astype(jnp.bfloat16)
    proj = jnp.dot(embedded, w_in, preferred_element_type=jnp.float32).astype(jnp.bfloat16)
    length = proj.shape[0]
    total = 2 * length
    proj_wide = proj.astype(jnp.float32)
    padded = jnp.concatenate([jnp.zeros((2, proj.shape[1]), jnp.float32), proj_wide], axis=0)
    mixed = (short_taps[0] * padded[2:] + short_taps[1] * padded[1:length + 1] + short_taps[2] * padded[:length]).astype(jnp.bfloat16)
    values = mixed[:, :D].astype(jnp.float32)
    first_gate = mixed[:, D:2 * D].astype(jnp.float32)
    second_gate = mixed[:, 2 * D:].astype(jnp.float32)

    def spectrum(series):
        return jnp.fft.rfft(series.T, n=total, axis=-1)

    def signal(spec):
        return jnp.fft.irfft(spec, n=total, axis=-1)[:, :length]

    first_spec = jnp.fft.rfft(filters[0].astype(jnp.float32), n=total, axis=-1)
    second_spec = jnp.fft.rfft(filters[1].astype(jnp.float32), n=total, axis=-1)
    value_spec = spectrum(values)
    first_conv = signal(value_spec * first_spec).T.astype(jnp.bfloat16).astype(jnp.float32)
    first_mix = (first_gate * first_conv).astype(jnp.bfloat16).astype(jnp.float32)
    mix_spec = spectrum(first_mix)
    second_conv = signal(mix_spec * second_spec).T.astype(jnp.bfloat16).astype(jnp.float32)
    mixer_out = (second_gate * second_conv).astype(jnp.bfloat16)
    upstream = cotangent.astype(jnp.float32)
    grad_conv2 = (upstream * second_gate).astype(jnp.bfloat16).astype(jnp.float32)
    grad_gate2 = (upstream * second_conv).astype(jnp.bfloat16)
    grad_spec2 = spectrum(grad_conv2)
    grad_mix = signal(grad_spec2 * jnp.conj(second_spec)).T.astype(jnp.bfloat16).astype(jnp.float32)
    filter_two = signal(grad_spec2 * jnp.conj(mix_spec))
    grad_gate1 = (grad_mix * first_conv).astype(jnp.bfloat16)
    grad_conv1 = (grad_mix * first_gate).astype(jnp.bfloat16).astype(jnp.float32)
    grad_spec1 = spectrum(grad_conv1)
    grad_values = signal(grad_spec1 * jnp.conj(first_spec)).T.astype(jnp.bfloat16)
    filter_one = signal(grad_spec1 * jnp.conj(value_spec))
    filter_grads = jnp.stack([filter_one, filter_two], axis=0)
    grad_mixed = jnp.concatenate([grad_values, grad_gate1, grad_gate2], axis=1).astype(jnp.float32)
    grad_padded = jnp.concatenate([grad_mixed, jnp.zeros((2, grad_mixed.shape[1]), jnp.float32)], axis=0)
    grad_proj = (short_taps[0] * grad_mixed + short_taps[1] * grad_padded[1:length + 1] + short_taps[2] * grad_padded[2:]).astype(jnp.bfloat16)
    tap_grads = jnp.stack([
        jnp.sum(grad_mixed * padded[2:], axis=0),
        jnp.sum(grad_mixed * padded[1:length + 1], axis=0),
        jnp.sum(grad_mixed * padded[:length], axis=0)], axis=0)
    weight_grads = jnp.dot(embedded.T, grad_proj, preferred_element_type=jnp.float32)
    return mixer_out, weight_grads, tap_grads, filter_grads
```

```python
import math

import jax
import jax.numpy as jnp
import ml_dtypes
import numpy as np
from jax import lax
from jax.experimental import pallas as pl
from jax.experimental.pallas import tpu as pltpu
from jax.sharding import PartitionSpec as P

DENSE_LIMIT = 4096
CODES = 128
LANES = 128
VMEM = 56 << 20


def widen(array):
    return array.astype(jnp.float32)


def narrow(array):
    return array.astype(jnp.bfloat16)


def local(token_ids, field_offsets, embed_table, w_in, short_taps, filters, cotangent):
    peers = lax.axis_size("tm")
    rows, width = cotangent.shape
    dense = 2 * rows * peers <= DENSE_LIMIT
    fits = width == peers * LANES // 2 and rows == LANES and peers & (peers - 1) == 0
    plan = fast_local if dense and fits and token_ids.shape[1] == 8 else wide_local
    return plan(token_ids, field_offsets, embed_table, w_in, short_taps, filters, cotangent)


def basis(quarter):
    total = 8 * quarter
    k = np.arange(quarter)
    angle = np.outer(k, k) % (2 * quarter) * (np.pi / quarter)
    cos, sin = np.cos(angle), -np.sin(angle)
    forward = np.concatenate([cos, sin], axis=0)
    forward[quarter] = 1.0 - 2.0 * (k % 2)
    inverse = forward.T * (2.0 / total)
    inverse[:, 0] *= 0.5
    inverse[:, quarter] *= 0.5
    turn = np.arange(quarter + 8)
    turn[quarter:] = quarter
    twist = []
    for step in (1, 2, 3):
        twist += [np.cos(turn * step * (2 * np.pi / total)), np.sin(turn * step * (2 * np.pi / total))]
    twist = np.broadcast_to(np.stack(twist)[:, :, None], (6, quarter + 8, LANES))
    bf16 = ml_dtypes.bfloat16
    return (forward.astype(bf16), inverse.astype(bf16), twist.astype(np.float32))


def dot(left, right):
    return jnp.dot(left, right, preferred_element_type=jnp.float32)


def swap(value):
    return pltpu.roll(value, LANES // 2, 1)


def left_lanes(rows):
    return lax.broadcasted_iota(jnp.int32, (rows, LANES), 1) < LANES // 2


def pick_quarter(count):
    row = lax.broadcasted_iota(jnp.int32, (count, count), 0)
    col = lax.broadcasted_iota(jnp.int32, (count, count), 1)
    block = count // 4
    return narrow(jnp.where(col == 4 * (row % block) + row // block, 1.0, 0.0))


def spin(real, imag, twist, rows):
    re, im = [real[0]], [imag[0]]
    for p in (1, 2, 3):
        cos, sin = twist[2 * p - 2, rows, :], twist[2 * p - 1, rows, :]
        re.append(real[p] * cos + imag[p] * sin)
        im.append(imag[p] * cos - real[p] * sin)
    er, ei, fr, fi = re[0] + re[2], im[0] + im[2], re[0] - re[2], im[0] - im[2]
    gr, gi, hr, hi = re[1] + re[3], im[1] + im[3], re[1] - re[3], im[1] - im[3]
    return [er + gr, fr + hi, er - gr, fr - hi], [ei + gi, fi - hr, ei - gi, fi + hr]


def unspin(real, imag, twist, rows):
    er, ei, fr, fi = real[0] + real[2], imag[0] + imag[2], real[0] - real[2], imag[0] - imag[2]
    gr, gi, hr, hi = real[1] + real[3], imag[1] + imag[3], real[1] - real[3], imag[1] - imag[3]
    re, im = [er + gr, fr - hi, er - gr, fr + hi], [ei + gi, fi + hr, ei - gi, fi - hr]
    for p in (1, 2, 3):
        cos, sin = twist[2 * p - 2, rows, :], twist[2 * p - 1, rows, :]
        re[p], im[p] = re[p] * cos - im[p] * sin, im[p] * cos + re[p] * sin
    return re, im


def matmul_rows(left, right, out):
    rows = left.shape[0]
    chunk = min(256, rows)

    def body(step, carry):
        own = pl.ds(pl.multiple_of(step * chunk, chunk), chunk)
        out[own, :] = dot(left[own, :], right[...])
        return carry

    lax.fori_loop(0, rows // chunk, body, 0)


def lanes_of(p):
    return slice(p * LANES, (p + 1) * LANES)


def each_bin(bins, twist, visit):
    quarter = bins.shape[0] // 2
    last = pl.ds(quarter, 8)
    zero = jnp.zeros((8, LANES), jnp.float32)
    nyquist = [jnp.broadcast_to(bins[quarter : quarter + 1, lanes_of(p)], (8, LANES)) for p in range(4)]
    kept = visit(last, *spin(nyquist, [zero] * 4, twist, last), True)
    bins[quarter : quarter + 1, :] = jnp.zeros((1, bins.shape[1]), jnp.float32)
    chunk = 32

    def body(step, carry):
        start = pl.multiple_of(step * chunk, chunk)
        rows = pl.ds(start, chunk)
        lower = pl.ds(pl.multiple_of(quarter + start, chunk), chunk)
        real = [bins[rows, lanes_of(p)] for p in range(4)]
        imag = [bins[lower, lanes_of(p)] for p in range(4)]
        visit(rows, *spin(real, imag, twist, rows), False)
        return carry

    lax.fori_loop(0, quarter // chunk, body, 0)
    return kept


def put_back(packed, ends):
    quarter = packed.shape[0] // 2
    own = slice(quarter, quarter + 16)
    first = lax.broadcasted_iota(jnp.int32, (16, LANES), 0) == 0
    for p in range(4):
        here = widen(packed[own, lanes_of(p)])
        there = jnp.broadcast_to(ends[p][:1], (16, LANES))
        packed[own, lanes_of(p)] = narrow(jnp.where(first, there, here))


def keep(packed, rows, real, imag, twist, ends):
    re, im = unspin(real, imag, twist, rows)
    if ends:
        return re
    quarter = packed.shape[0] // 2
    lower = pl.ds(pl.multiple_of(rows.start + quarter, 16), rows.size)
    for p in range(4):
        packed[rows, lanes_of(p)] = narrow(re[p])
        packed[lower, lanes_of(p)] = narrow(im[p])
    return None


def sides(rows):
    return jnp.where(left_lanes(rows), 1.0, -1.0)


def filter_spectrum(filters, forward, twist, series, bins, spec_re, spec_im):
    length = filters.shape[2]
    both = filters.shape[0] * filters.shape[1]
    block = length // 4
    pick = pick_quarter(block)
    part = block // 4
    for b in range(4):
        chunk = filters[:, :, b * block : (b + 1) * block].reshape(both, block)
        turned = lax.dot_general(
            pick, chunk, (((1,), (1,)), ((), ())), preferred_element_type=jnp.float32
        )
        for p in range(4):
            series[b * part : (b + 1) * part, lanes_of(p)] = narrow(turned[p * part : (p + 1) * part])
    matmul_rows(forward, series, bins)

    def visit(rows, re, im, ends):
        sign = sides(rows.size)
        for m in range(4):
            spec_re[m, rows, :] = re[m]
            spec_im[m, rows, :] = im[m] * sign

    each_bin(bins, twist, visit)


def first_product(bins, twist, filt_re, filt_im, spec_re, spec_im, packed):
    def visit(rows, re, im, ends):
        out_re, out_im = [], []
        for m in range(4):
            spec_re[m, rows, :] = re[m]
            spec_im[m, rows, :] = im[m]
            fr, fi = filt_re[m, rows, :], filt_im[m, rows, :]
            out_re.append(re[m] * fr - im[m] * fi)
            out_im.append(re[m] * fi + im[m] * fr)
        return keep(packed, rows, out_re, out_im, twist, ends)

    put_back(packed, each_bin(bins, twist, visit))


def second_product(bins, twist, filt_re, filt_im, spec_re, spec_im, packed, lagged):
    def visit(rows, re, im, ends):
        out_re, out_im, lag_re, lag_im = [], [], [], []
        sign = sides(rows.size)
        for m in range(4):
            fr, fi = filt_re[m, rows, :], filt_im[m, rows, :]
            out_re.append(re[m] * fr + im[m] * fi)
            out_im.append(im[m] * fr - re[m] * fi)
            sr, si = spec_re[m, rows, :], spec_im[m, rows, :]
            lag_re.append(re[m] * sr + im[m] * si)
            lag_im.append((im[m] * sr - re[m] * si) * sign)
        conv = keep(packed, rows, out_re, out_im, twist, ends)
        lags = keep(lagged, rows, lag_re, lag_im, twist, ends)
        return (conv, lags)

    conv, lags = each_bin(bins, twist, visit)
    put_back(packed, conv)
    put_back(lagged, lags)


def shifted(value, step):
    rows = value.shape[0]
    row = lax.broadcasted_iota(jnp.int32, value.shape, 0)
    edge = 0 if step == 1 else rows - 1
    return jnp.where(row == edge, 0.0, pltpu.roll(value, step % rows, 0))


def exchange(send, got, send_sems, recv_sems, d):
    me = lax.axis_index("tm")
    peer = me ^ d
    return pltpu.make_async_remote_copy(
        src_ref=send.at[peer],
        dst_ref=got.at[me],
        send_sem=send_sems.at[d],
        recv_sem=recv_sems.at[d],
        device_id=(lax.axis_index("groups"), peer),
        device_id_type=pl.DeviceIdType.MESH,
    )


def share(source, got, send_sems, recv_sems, d):
    me = lax.axis_index("tm")
    return pltpu.make_async_remote_copy(
        src_ref=source,
        dst_ref=got.at[me],
        send_sem=send_sems.at[d],
        recv_sem=recv_sems.at[d],
        device_id=(lax.axis_index("groups"), me ^ d),
        device_id_type=pl.DeviceIdType.MESH,
    )


def greet(peers):
    me = lax.axis_index("tm")
    barrier = pltpu.get_barrier_semaphore()
    for d in range(1, peers):
        pl.semaphore_signal(
            barrier,
            inc=1,
            device_id=(lax.axis_index("groups"), me ^ d),
            device_id_type=pl.DeviceIdType.MESH,
        )
    pl.semaphore_wait(barrier, peers - 1)


def window_kernel(
    tok_ref, w_ref, cot_ref, offsets, taps_ref, table_hbm, filters_hbm, forward_hbm, inverse_hbm, twist_hbm,
    mixer_out, weight_out, tap_out, filter_out,
    table, filters, forward, inverse, twist,
    tok_own, tok_got, send, got, mix_back, mix_home, back, home, tap_own, tap_got,
    used, emb, emb_t, w_own, proj, gates, first_gate, upstream,
    series, bins, filt_re, filt_im, spec_re, spec_im, packed, lagged, wave, grad_b, grad_a, grad_proj,
    load_sems, tok_send, tok_recv, in_send, in_recv, mix_send, mix_recv, out_send, out_recv, tap_send, tap_recv,
):
    peers, _, _ = got.shape
    rows, width = cot_ref.shape
    half = LANES // 2
    quarter = inverse.shape[0]
    block = rows // 4
    fields = tok_ref.shape[0]
    me = lax.axis_index("tm")
    others = range(1, peers)

    loads = [
        pltpu.make_async_copy(source, target, load_sems.at[i])
        for i, (source, target) in enumerate(
            [(table_hbm, table), (filters_hbm, filters), (forward_hbm, forward), (twist_hbm, twist), (inverse_hbm, inverse)]
        )
    ]
    for load in loads:
        load.start()

    pick = pick_quarter(rows)
    tokens = lax.dot_general(
        narrow(tok_ref[...].astype(jnp.float32)), pick, (((1,), (1,)), ((), ())), preferred_element_type=jnp.float32
    )
    tok_own[...] = tokens
    tok_got[me] = tokens
    turned = narrow(dot(pick, cot_ref[...]))
    for q in range(0, peers, 2):
        own = [slice(j * width + q * half, j * width + (q + 2) * half) for j in range(3)]
        value, gate1, gate2 = [w_ref[:, s] for s in own]
        steps = [turned[p * block : (p + 1) * block, own[0]] for p in range(4)]
        for side in range(2):
            mine = slice(side * half, (side + 1) * half)
            pairs = [(value, gate2), (gate1[: half // 2], gate1[half // 2 :]), (steps[0], steps[1]), (steps[2], steps[3])]
            send[q + side] = jnp.concatenate(
                [jnp.concatenate([a[:, mine], b[:, mine]], axis=1) for a, b in pairs], axis=0
            )
    got[me] = send[me]

    greet(peers)
    for d in others:
        share(tok_own, tok_got, tok_send, tok_recv, d).start()
    for d in others:
        exchange(send, got, in_send, in_recv, d).start()

    loads[0].wait()
    code = lax.broadcasted_iota(jnp.int32, (CODES, table.shape[0]), 1)
    code = code - lax.broadcasted_iota(jnp.int32, (CODES, table.shape[0]), 0)
    for field in range(fields):
        chosen = narrow(jnp.where(code == offsets[field], 1.0, 0.0))
        used[field * CODES : (field + 1) * CODES, :] = narrow(dot(chosen, table[...]))
    for load in loads[1:4]:
        load.wait()
    filter_spectrum(filters, forward, twist, series, bins, filt_re, filt_im)

    for d in others:
        share(tok_own, tok_got, tok_send, tok_recv, d).wait_recv()
    lanes = lax.broadcasted_iota(jnp.int32, (rows, CODES), 1).astype(jnp.float32)

    def embed(i, carry):
        hot = []
        for s in range(2):
            steps = tok_got[2 * i + s].T
            hot.append(
                jnp.concatenate(
                    [
                        narrow(jnp.where(steps[:, field : field + 1] == lanes, 1.0, 0.0))
                        for field in range(fields)
                    ],
                    axis=1,
                )
            )
        summed = dot(jnp.concatenate(hot, axis=0), used[...])
        rounded = narrow(summed)
        emb_t[:, pl.ds(pl.multiple_of(i * 2 * rows, 2 * rows), 2 * rows)] = rounded.T
        for s in range(2):
            for p in range(4):
                start = s * rows + p * block
                emb[p, 2 * i + s] = rounded[start : start + block]
        return carry

    lax.fori_loop(0, peers // 2, embed, 0)
    loads[4].wait()

    for d in others:
        exchange(send, got, in_send, in_recv, d).wait_recv()
    near = left_lanes(half // 2)
    for peer in range(peers):
        own = slice(peer * half, (peer + 1) * half)
        w_own[own, :LANES] = got[peer, :half]
        gate = widen(got[peer, half : half + half // 2])
        other = swap(gate)
        both = jnp.concatenate([jnp.where(near, gate, other), jnp.where(near, other, gate)], axis=0)
        w_own[own, LANES:] = narrow(both)
    left = left_lanes(quarter)
    for p in range(0, 4, 2):
        start = half + half // 2 + p // 2 * block
        steps = widen(got[:, start : start + block, :].reshape(quarter, LANES))
        upstream[p] = jnp.where(left, 1.0, swap(steps))
        upstream[p + 1] = jnp.where(left, 1.0, steps)

    pair = taps_ref[...]
    place = pl.multiple_of(me // 2 * LANES, LANES)
    odd = me % 2 == 1
    near3 = left_lanes(3)
    own_taps = []
    for j in range(3):
        piece = taps_ref[:, pl.ds(pl.multiple_of(place + j * width, LANES), LANES)]
        own_taps.append(jnp.where(odd, swap(piece), piece))
    taps = jnp.concatenate(
        [jnp.where(near3, own_taps[0], swap(own_taps[2])), jnp.where(near3, own_taps[1], swap(own_taps[1]))], axis=1
    )
    tap = [taps[j : j + 1] for j in range(3)]

    for p in range(4):
        proj[p] = widen(narrow(dot(emb[p].reshape(quarter, width), w_own[...])))

    def back_by(p, steps):
        return proj[p - steps] if p >= steps else shifted(proj[p - steps + 4], 1)

    for p in range(4):
        mixed = widen(narrow(tap[0] * proj[p] + tap[1] * back_by(p, 1) + tap[2] * back_by(p, 2)))
        gates[p] = mixed[:, :LANES]
        first_gate[p] = mixed[:, LANES:]
        series[:, lanes_of(p)] = narrow(mixed[:, :LANES] * upstream[p])

    matmul_rows(forward, series, bins)
    first_product(bins, twist, filt_re, filt_im, spec_re, spec_im, packed)
    matmul_rows(inverse, packed, wave)
    for p in range(4):
        out = widen(narrow(wave[:, lanes_of(p)]))
        flipped = swap(out)
        series[:, lanes_of(p)] = narrow(flipped * first_gate[p])
        grad_b[p] = widen(narrow(out * flipped))

    matmul_rows(forward, series, bins)
    second_product(bins, twist, filt_re, filt_im, spec_re, spec_im, packed, lagged)
    matmul_rows(inverse, packed, wave)
    mixed = []
    for p in range(4):
        out = widen(narrow(wave[:, lanes_of(p)]))
        mixed.append(gates[p] * out)
        grad_a[p] = widen(narrow(upstream[p] * out))
    for p in range(0, 4, 2):
        start = p // 2 * block
        both = narrow(jnp.where(left, swap(mixed[p]), mixed[p + 1]))
        mix_back[:, start : start + block, :] = both.reshape(peers, block, LANES)
    mix_home[me] = mix_back[me]
    for d in others:
        exchange(mix_back, mix_home, mix_send, mix_recv, d).start()

    def ahead(grad, p, steps):
        return grad[p + steps] if p + steps < 4 else shifted(grad[p + steps - 4], -1)

    sums = []
    for grad, own in ((grad_a, slice(0, LANES)), (grad_b, slice(LANES, 2 * LANES))):
        total = [jnp.zeros((1, LANES), jnp.float32)] * 3
        for p in range(4):
            here = grad[p]
            out = tap[0][:, own] * here + tap[1][:, own] * ahead(grad, p, 1) + tap[2][:, own] * ahead(grad, p, 2)
            grad_proj[:, p, :, own] = narrow(out).reshape(peers, block, LANES)
            for j in range(3):
                lag = proj[p - j, :, own] if p >= j else shifted(proj[p - j + 4, :, own], 1)
                total[j] = total[j] + jnp.sum(here * lag, axis=0, keepdims=True)
        sums += total
    tap_own[...] = jnp.concatenate(sums + [jnp.zeros((2, LANES), jnp.float32)], axis=0)
    tap_got[me] = tap_own[...]
    for d in others:
        share(tap_own, tap_got, tap_send, tap_recv, d).start()

    group = 4

    def weights(step, carry):
        own = pl.ds(pl.multiple_of(step * group * half, group * half), group * half)
        terms = dot(emb_t[own, :], grad_proj[...].reshape(peers * rows, 2 * LANES))
        for s in range(group):
            here = terms[s * half : (s + 1) * half]
            back[step * group + s, :half, :] = narrow(here[:, :LANES])
            twin = here[:, LANES:]
            back[step * group + s, half:, :] = narrow(jnp.where(near, twin[: half // 2], twin[half // 2 :]))
        return carry

    lax.fori_loop(0, peers // group, weights, 0)
    home[me] = back[me]
    for d in others:
        exchange(back, home, out_send, out_recv, d).start()

    matmul_rows(inverse, lagged, wave)
    part = quarter // 4
    order = pick_quarter(quarter)
    for b in range(4):
        lags = jnp.concatenate(
            [wave[b * part : (b + 1) * part, lanes_of(p)].T for p in range(4)], axis=1
        )
        high = narrow(lags)
        rest = narrow(lags - widen(high))
        out = dot(high, order) + dot(rest, order)
        place = slice(b * quarter, (b + 1) * quarter)
        filter_out[0, :, place] = out[:half]
        filter_out[1, :, place] = out[half:]

    for d in others:
        exchange(mix_back, mix_home, mix_send, mix_recv, d).wait_recv()
    columns = []
    for q in range(0, peers, 2):
        one, two = mix_home[q], mix_home[q + 1]
        pieces = []
        for p in range(4):
            start = p // 2 * block
            mine = slice(p % 2 * half, (p % 2 + 1) * half)
            pieces.append(
                jnp.concatenate([one[start : start + block, mine], two[start : start + block, mine]], axis=1)
            )
        columns.append(jnp.concatenate(pieces, axis=0))
    gathered = jnp.concatenate(columns, axis=1)
    mixer_out[...] = narrow(
        lax.dot_general(pick, gathered, (((0,), (0,)), ((), ())), preferred_element_type=jnp.float32)
    )
    for d in others:
        share(tap_own, tap_got, tap_send, tap_recv, d).wait_recv()
    for q in range(0, peers, 2):
        one, two = tap_got[q], tap_got[q + 1]
        for j, (row, side) in enumerate(((0, 0), (3, 0), (0, 1))):
            mine = slice(side * half, (side + 1) * half)
            start = j * width + q * half
            tap_out[:, start : start + LANES] = jnp.concatenate(
                [one[row : row + 3, mine], two[row : row + 3, mine]], axis=1
            )
    for d in others:
        exchange(back, home, out_send, out_recv, d).wait_recv()
    for q in range(0, peers, 2):
        one, two = widen(home[q]), widen(home[q + 1])
        first = [one[:half, :half], one[half:, :half], one[half:, half:], one[:half, half:]]
        second = [two[:half, :half], two[half:, :half], two[half:, half:], two[:half, half:]]
        whole = [jnp.concatenate(pair, axis=1) for pair in zip(first, second)]
        start = q * half
        weight_out[:, start : start + LANES] = whole[0]
        weight_out[: half // 2, width + start : width + start + LANES] = whole[1]
        weight_out[half // 2 :, width + start : width + start + LANES] = whole[2]
        weight_out[:, 2 * width + start : 2 * width + start + LANES] = whole[3]

    for d in others:
        share(tok_own, tok_got, tok_send, tok_recv, d).wait_send()
        exchange(send, got, in_send, in_recv, d).wait_send()
        exchange(mix_back, mix_home, mix_send, mix_recv, d).wait_send()
        share(tap_own, tap_got, tap_send, tap_recv, d).wait_send()
        exchange(back, home, out_send, out_recv, d).wait_send()


def fast_local(token_ids, field_offsets, embed_table, w_in, short_taps, filters, cotangent):
    rows, width = cotangent.shape
    fields = token_ids.shape[1]
    peers = lax.axis_size("tm")
    length = rows * peers
    quarter = length // 4
    forward, inverse, twist = basis(quarter)
    whole = pl.BlockSpec(memory_space=pltpu.VMEM)
    anywhere = pl.BlockSpec(memory_space=pl.ANY)
    f32, bf16 = jnp.float32, jnp.bfloat16
    payload = rows + LANES // 4
    sems = pltpu.SemaphoreType.DMA((peers,))
    wide = 4 * LANES
    scratch = [
        pltpu.VMEM(embed_table.shape, bf16),
        pltpu.VMEM(filters.shape, bf16),
        pltpu.VMEM(forward.shape, bf16),
        pltpu.VMEM(inverse.shape, bf16),
        pltpu.VMEM(twist.shape, f32),
        pltpu.VMEM((fields, rows), f32),
        pltpu.VMEM((peers, fields, rows), f32),
        pltpu.VMEM((peers, payload, LANES), bf16),
        pltpu.VMEM((peers, payload, LANES), bf16),
        pltpu.VMEM((peers, rows // 2, LANES), bf16),
        pltpu.VMEM((peers, rows // 2, LANES), bf16),
        pltpu.VMEM((peers, payload - rows // 2, LANES), bf16),
        pltpu.VMEM((peers, payload - rows // 2, LANES), bf16),
        pltpu.VMEM((8, LANES), f32),
        pltpu.VMEM((peers, 8, LANES), f32),
        pltpu.VMEM((fields * CODES, width), bf16),
        pltpu.VMEM((4, peers, rows // 4, width), bf16),
        pltpu.VMEM((width, length), bf16),
        pltpu.VMEM((width, 2 * LANES), bf16),
        pltpu.VMEM((4, quarter, 2 * LANES), f32),
        pltpu.VMEM((4, quarter, LANES), f32),
        pltpu.VMEM((4, quarter, LANES), f32),
        pltpu.VMEM((4, quarter, LANES), f32),
        pltpu.VMEM((quarter, wide), bf16),
        pltpu.VMEM((2 * quarter, wide), f32),
        pltpu.VMEM((4, quarter + 8, LANES), f32),
        pltpu.VMEM((4, quarter + 8, LANES), f32),
        pltpu.VMEM((4, quarter + 8, LANES), f32),
        pltpu.VMEM((4, quarter + 8, LANES), f32),
        pltpu.VMEM((2 * quarter, wide), bf16),
        pltpu.VMEM((2 * quarter, wide), bf16),
        pltpu.VMEM((quarter, wide), f32),
        pltpu.VMEM((4, quarter, LANES), f32),
        pltpu.VMEM((4, quarter, LANES), f32),
        pltpu.VMEM((peers, 4, rows // 4, 2 * LANES), bf16),
        pltpu.SemaphoreType.DMA((5,)),
    ] + [sems] * 10
    return tuple(
        pl.pallas_call(
            window_kernel,
            out_shape=(
                jax.ShapeDtypeStruct((rows, width), bf16),
                jax.ShapeDtypeStruct((width // peers, 3 * width), f32),
                jax.ShapeDtypeStruct((3, 3 * width), f32),
                jax.ShapeDtypeStruct(filters.shape, f32),
            ),
            in_specs=[whole, whole, whole, pl.BlockSpec(memory_space=pltpu.SMEM), whole] + [anywhere] * 5,
            out_specs=(whole,) * 4,
            scratch_shapes=scratch,
            compiler_params=pltpu.CompilerParams(
                vmem_limit_bytes=VMEM, collective_id=0, has_side_effects=True
            ),
            name="window",
        )(
            token_ids.T,
            w_in,
            cotangent,
            field_offsets,
            short_taps,
            embed_table,
            filters,
            jnp.asarray(forward),
            jnp.asarray(inverse),
            jnp.asarray(twist),
        )
    )


def cis_tables(count_a, count_b, modulus):
    left = jnp.arange(count_a, dtype=jnp.int32)[:, None]
    right = jnp.arange(count_b, dtype=jnp.int32)[None, :]
    angle = 2.0 * math.pi / modulus * (left * right % modulus).astype(jnp.float32)
    return (jnp.cos(angle), jnp.sin(angle))


class Factored:
    def __init__(self, total):
        bits = total.bit_length() - 1
        first_len = 1 << (bits + 1) // 2
        second_len = total // first_len
        first_cos, first_sin = cis_tables(first_len, first_len // 2, first_len)
        second_cos, second_sin = cis_tables(second_len, second_len, second_len)
        self.total = total
        self.second_len = second_len
        self.twist_cos, self.twist_sin = cis_tables(first_len, second_len, total)
        self.first_both = jnp.concatenate([first_cos, -first_sin], axis=0)
        self.forward = jnp.block([[second_cos, -second_sin], [second_sin, second_cos]])
        self.inverse = jnp.block([[second_cos, second_sin], [-second_sin, second_cos]])

    def spectrum(self, series):
        series = widen(series)
        channels, length = series.shape
        rows_k = self.twist_cos.shape[0]
        half = self.first_both.shape[1]
        blocks = series.reshape(channels, half, length // half)
        part = jnp.einsum("ka,cab->ckb", self.first_both, blocks)
        part_re = part[:, :rows_k]
        part_im = part[:, rows_k:]
        turn_re = part_re * self.twist_cos + part_im * self.twist_sin
        turn_im = part_im * self.twist_cos - part_re * self.twist_sin
        turned = jnp.concatenate([turn_re, turn_im], axis=2)
        result = jnp.einsum("ckb,bm->ckm", turned, self.forward)
        return (result[:, :, : self.second_len], result[:, :, self.second_len :])

    def product(self, left, right, conjugate):
        left_re, left_im = left
        right_re, right_im = right
        if conjugate:
            right_im = -right_im
        return (left_re * right_re - left_im * right_im, left_re * right_im + left_im * right_re)

    def signal(self, pair):
        joined = jnp.concatenate(pair, axis=2)
        back = jnp.einsum("ckm,mb->ckb", joined, self.inverse)
        back_re = back[:, :, : self.second_len]
        back_im = back[:, :, self.second_len :]
        turn_re = back_re * self.twist_cos - back_im * self.twist_sin
        turn_im = back_im * self.twist_cos + back_re * self.twist_sin
        turned = jnp.concatenate([turn_re, turn_im], axis=1)
        blocks = jnp.einsum("ka,ckb->cab", self.first_both, turned)
        return blocks.reshape(joined.shape[0], -1) * (1.0 / self.total)


def delayed(array, steps):
    length = array.shape[1]
    return jnp.pad(array, ((0, 0), (steps, 0)))[:, :length]


def advanced(array, steps):
    return jnp.pad(array, ((0, 0), (0, steps)))[:, steps:]


def wide_local(token_ids, field_offsets, embed_table, w_in, short_taps, filters, cotangent):
    rows, width = cotangent.shape
    fields = token_ids.shape[1]
    peers = lax.axis_size("tm")
    me = lax.axis_index("tm")
    chans = width // peers
    length = rows * peers
    vocab = embed_table.shape[0]

    w_part = w_in.reshape(chans, 3, peers, chans).transpose(2, 0, 1, 3).reshape(peers, chans, 3 * chans)
    cot_part = cotangent.reshape(rows, peers, chans).transpose(1, 2, 0)
    tok_part = narrow(token_ids).T.reshape(1, chans, -1)
    tok_part = jnp.broadcast_to(tok_part, (peers,) + tok_part.shape[1:])
    sent = jnp.concatenate([w_part, cot_part, tok_part], axis=2)
    got = lax.all_to_all(sent, "tm", split_axis=0, concat_axis=0, tiled=True)
    w_own = got[:, :, : 3 * chans].reshape(width, 3 * chans)
    upstream = widen(got[:, :, 3 * chans : 3 * chans + rows].transpose(1, 0, 2).reshape(chans, length))
    tokens = got[:, :, 3 * chans + rows :].reshape(peers, fields, rows)
    tokens = tokens.transpose(1, 0, 2).reshape(fields, length).astype(jnp.int32)
    row_index = tokens + field_offsets[:, None]

    codes = lax.broadcasted_iota(jnp.int32, (vocab, length), 0)
    counts = jnp.zeros((vocab, length), jnp.float32)
    for field in range(fields):
        counts = counts + jnp.where(codes == row_index[field][None, :], 1.0, 0.0)
    embedded = narrow(
        jnp.einsum("vr,vt->rt", embed_table, narrow(counts), preferred_element_type=jnp.float32)
    )
    proj = narrow(jnp.einsum("rc,rt->ct", w_own, embedded, preferred_element_type=jnp.float32))
    taps = lax.dynamic_index_in_dim(short_taps.reshape(3, 3, peers, chans), me, 2, keepdims=False)
    taps = taps.reshape(3, 3 * chans, 1)
    proj_wide = widen(proj)
    lags = (proj_wide, delayed(proj_wide, 1), delayed(proj_wide, 2))
    mixed = narrow(taps[0] * lags[0] + taps[1] * lags[1] + taps[2] * lags[2])
    values = mixed[:chans]
    first_gate = widen(mixed[chans : 2 * chans])
    second_gate = widen(mixed[2 * chans :])

    transform = Factored(2 * length)

    def spectra(*series):
        whole = transform.spectrum(jnp.concatenate(series, axis=0))
        return [
            tuple(part[i * chans : (i + 1) * chans] for part in whole) for i in range(len(series))
        ]

    def signals(*pairs):
        whole = transform.signal(tuple(jnp.concatenate(parts, axis=0) for parts in zip(*pairs)))
        return [whole[i * chans : (i + 1) * chans] for i in range(len(pairs))]

    grad_conv2 = narrow(upstream * second_gate)
    first_spec, second_spec, value_spec, grad_spec2 = spectra(
        filters[0], filters[1], values, grad_conv2
    )
    first_conv, grad_mix = signals(
        transform.product(value_spec, first_spec, False),
        transform.product(grad_spec2, second_spec, True),
    )
    first_conv = widen(narrow(first_conv))
    grad_mix = widen(narrow(grad_mix))
    first_mix = narrow(first_gate * first_conv)
    grad_gate1 = narrow(grad_mix * first_conv)
    grad_conv1 = narrow(grad_mix * first_gate)
    mix_spec, grad_spec1 = spectra(first_mix, grad_conv1)
    second_conv, grad_values, filter_one, filter_two = signals(
        transform.product(mix_spec, second_spec, False),
        transform.product(grad_spec1, first_spec, True),
        transform.product(grad_spec1, value_spec, True),
        transform.product(grad_spec2, mix_spec, True),
    )
    second_conv = widen(narrow(second_conv))
    mixer_out = narrow(second_gate * second_conv)
    grad_gate2 = narrow(upstream * second_conv)
    filter_grads = jnp.stack([filter_one, filter_two], axis=0)
    grad_mixed = jnp.concatenate([narrow(grad_values), grad_gate1, grad_gate2], axis=0)
    grad_wide = widen(grad_mixed)
    grad_proj = narrow(
        taps[0] * grad_wide + taps[1] * advanced(grad_wide, 1) + taps[2] * advanced(grad_wide, 2)
    )
    tap_terms = jnp.stack([jnp.sum(grad_wide * lag, axis=1) for lag in lags], axis=0)
    weight_terms = narrow(
        jnp.einsum("rt,ct->rc", embedded, grad_proj, preferred_element_type=jnp.float32)
    )

    weight_part = weight_terms.reshape(peers, chans, 3 * chans)
    mixer_part = mixer_out.reshape(chans, peers, rows).transpose(1, 0, 2)
    tap_part = narrow(tap_terms).reshape(1, chans, -1)
    tap_part = jnp.broadcast_to(tap_part, (peers,) + tap_part.shape[1:])
    back = lax.all_to_all(
        jnp.concatenate([weight_part, mixer_part, tap_part], axis=2),
        "tm",
        split_axis=0,
        concat_axis=0,
        tiled=True,
    )
    weight_grads = widen(
        back[:, :, : 3 * chans].reshape(peers, chans, 3, chans).transpose(1, 2, 0, 3)
    ).reshape(chans, 3 * width)
    mixer_rows = back[:, :, 3 * chans : 3 * chans + rows].reshape(width, rows).T
    tap_grads = widen(
        back[:, :, 3 * chans + rows :].reshape(peers, 3, 3, chans).transpose(1, 2, 0, 3)
    ).reshape(3, 3 * width)
    return (mixer_rows, weight_grads, tap_grads, filter_grads)


def solution(mesh):
    return jax.shard_map(
        local,
        mesh=mesh,
        in_specs=(
            P(("groups", "tm"), None),
            P("groups"),
            P(),
            P("tm", None),
            P(),
            P(None, "tm", None),
            P(("groups", "tm"), None),
        ),
        out_specs=(
            P(("groups", "tm"), None),
            P(("groups", "tm"), None),
            P("groups", None),
            P("groups", "tm", None),
        ),
        check_vma=False,
    )
```

```python
import math

import jax
import jax.numpy as jnp
import ml_dtypes
import numpy as np
from jax import lax
from jax.experimental import pallas as pl
from jax.experimental.pallas import tpu as pltpu
from jax.sharding import PartitionSpec as P

DENSE_LIMIT = 4096
CODES = 128
LANES = 128
VMEM = 56 << 20


def widen(array):
    return array.astype(jnp.float32)


def narrow(array):
    return array.astype(jnp.bfloat16)


def local(token_ids, field_offsets, embed_table, w_in, short_taps, filters, cotangent):
    peers = lax.axis_size("tm")
    rows, width = cotangent.shape
    dense = 2 * rows * peers <= DENSE_LIMIT
    fits = width == peers * LANES // 2 and rows == LANES and peers & (peers - 1) == 0
    plan = fast_local if dense and fits and token_ids.shape[1] == 8 else wide_local
    return plan(token_ids, field_offsets, embed_table, w_in, short_taps, filters, cotangent)


def basis(quarter):
    total = 8 * quarter
    k = np.arange(quarter)
    angle = np.outer(k, k) % (2 * quarter) * (np.pi / quarter)
    cos, sin = np.cos(angle), -np.sin(angle)
    forward = np.concatenate([cos, sin], axis=0)
    forward[quarter] = 1.0 - 2.0 * (k % 2)
    inverse = forward.T * (2.0 / total)
    inverse[:, 0] *= 0.5
    inverse[:, quarter] *= 0.5
    turn = np.arange(quarter + 8)
    turn[quarter:] = quarter
    twist = []
    for step in (1, 2, 3):
        twist += [np.cos(turn * step * (2 * np.pi / total)), np.sin(turn * step * (2 * np.pi / total))]
    twist = np.broadcast_to(np.stack(twist)[:, :, None], (6, quarter + 8, LANES))
    bf16 = ml_dtypes.bfloat16
    return (forward.astype(bf16), inverse.astype(bf16), twist.astype(np.float32))


def dot(left, right):
    return jnp.dot(left, right, preferred_element_type=jnp.float32)


def swap(value):
    return pltpu.roll(value, LANES // 2, 1)


def left_lanes(rows):
    return lax.broadcasted_iota(jnp.int32, (rows, LANES), 1) < LANES // 2


def pick_quarter(count):
    row = lax.broadcasted_iota(jnp.int32, (count, count), 0)
    col = lax.broadcasted_iota(jnp.int32, (count, count), 1)
    block = count // 4
    return narrow(jnp.where(col == 4 * (row % block) + row // block, 1.0, 0.0))


def spin(real, imag, twist, rows):
    re, im = [real[0]], [imag[0]]
    for p in (1, 2, 3):
        cos, sin = twist[2 * p - 2, rows, :], twist[2 * p - 1, rows, :]
        re.append(real[p] * cos + imag[p] * sin)
        im.append(imag[p] * cos - real[p] * sin)
    er, ei, fr, fi = re[0] + re[2], im[0] + im[2], re[0] - re[2], im[0] - im[2]
    gr, gi, hr, hi = re[1] + re[3], im[1] + im[3], re[1] - re[3], im[1] - im[3]
    return [er + gr, fr + hi, er - gr, fr - hi], [ei + gi, fi - hr, ei - gi, fi + hr]


def unspin(real, imag, twist, rows):
    er, ei, fr, fi = real[0] + real[2], imag[0] + imag[2], real[0] - real[2], imag[0] - imag[2]
    gr, gi, hr, hi = real[1] + real[3], imag[1] + imag[3], real[1] - real[3], imag[1] - imag[3]
    re, im = [er + gr, fr - hi, er - gr, fr + hi], [ei + gi, fi + hr, ei - gi, fi - hr]
    for p in (1, 2, 3):
        cos, sin = twist[2 * p - 2, rows, :], twist[2 * p - 1, rows, :]
        re[p], im[p] = re[p] * cos - im[p] * sin, im[p] * cos + re[p] * sin
    return re, im


def matmul_rows(left, right, out):
    rows = left.shape[0]
    chunk = min(256, rows)

    def body(step, carry):
        own = pl.ds(pl.multiple_of(step * chunk, chunk), chunk)
        out[own, :] = dot(left[own, :], right[...])
        return carry

    lax.fori_loop(0, rows // chunk, body, 0)


def lanes_of(p):
    return slice(p * LANES, (p + 1) * LANES)


def each_bin(bins, twist, visit):
    quarter = bins.shape[0] // 2
    last = pl.ds(quarter, 8)
    zero = jnp.zeros((8, LANES), jnp.float32)
    nyquist = [jnp.broadcast_to(bins[quarter : quarter + 1, lanes_of(p)], (8, LANES)) for p in range(4)]
    kept = visit(last, *spin(nyquist, [zero] * 4, twist, last), True)
    bins[quarter : quarter + 1, :] = jnp.zeros((1, bins.shape[1]), jnp.float32)
    chunk = 32

    def body(step, carry):
        start = pl.multiple_of(step * chunk, chunk)
        rows = pl.ds(start, chunk)
        lower = pl.ds(pl.multiple_of(quarter + start, chunk), chunk)
        real = [bins[rows, lanes_of(p)] for p in range(4)]
        imag = [bins[lower, lanes_of(p)] for p in range(4)]
        visit(rows, *spin(real, imag, twist, rows), False)
        return carry

    lax.fori_loop(0, quarter // chunk, body, 0)
    return kept


def put_back(packed, ends):
    quarter = packed.shape[0] // 2
    own = slice(quarter, quarter + 16)
    first = lax.broadcasted_iota(jnp.int32, (16, LANES), 0) == 0
    for p in range(4):
        here = widen(packed[own, lanes_of(p)])
        there = jnp.broadcast_to(ends[p][:1], (16, LANES))
        packed[own, lanes_of(p)] = narrow(jnp.where(first, there, here))


def keep(packed, rows, real, imag, twist, ends):
    re, im = unspin(real, imag, twist, rows)
    if ends:
        return re
    quarter = packed.shape[0] // 2
    lower = pl.ds(pl.multiple_of(rows.start + quarter, 16), rows.size)
    for p in range(4):
        packed[rows, lanes_of(p)] = narrow(re[p])
        packed[lower, lanes_of(p)] = narrow(im[p])
    return None


def sides(rows):
    return jnp.where(left_lanes(rows), 1.0, -1.0)


def filter_spectrum(filters, forward, twist, series, bins, spec_re, spec_im):
    length = filters.shape[2]
    both = filters.shape[0] * filters.shape[1]
    block = length // 4
    pick = pick_quarter(block)
    part = block // 4
    for b in range(4):
        chunk = filters[:, :, b * block : (b + 1) * block].reshape(both, block)
        turned = lax.dot_general(
            pick, chunk, (((1,), (1,)), ((), ())), preferred_element_type=jnp.float32
        )
        for p in range(4):
            series[b * part : (b + 1) * part, lanes_of(p)] = narrow(turned[p * part : (p + 1) * part])
    matmul_rows(forward, series, bins)

    def visit(rows, re, im, ends):
        sign = sides(rows.size)
        for m in range(4):
            spec_re[m, rows, :] = re[m]
            spec_im[m, rows, :] = im[m] * sign

    each_bin(bins, twist, visit)


def first_product(bins, twist, filt_re, filt_im, spec_re, spec_im, packed):
    def visit(rows, re, im, ends):
        out_re, out_im = [], []
        for m in range(4):
            spec_re[m, rows, :] = re[m]
            spec_im[m, rows, :] = im[m]
            fr, fi = filt_re[m, rows, :], filt_im[m, rows, :]
            out_re.append(re[m] * fr - im[m] * fi)
            out_im.append(re[m] * fi + im[m] * fr)
        return keep(packed, rows, out_re, out_im, twist, ends)

    put_back(packed, each_bin(bins, twist, visit))


def second_product(bins, twist, filt_re, filt_im, spec_re, spec_im, packed, lagged):
    def visit(rows, re, im, ends):
        out_re, out_im, lag_re, lag_im = [], [], [], []
        sign = sides(rows.size)
        for m in range(4):
            fr, fi = filt_re[m, rows, :], filt_im[m, rows, :]
            out_re.append(re[m] * fr + im[m] * fi)
            out_im.append(im[m] * fr - re[m] * fi)
            sr, si = spec_re[m, rows, :], spec_im[m, rows, :]
            lag_re.append(re[m] * sr + im[m] * si)
            lag_im.append((im[m] * sr - re[m] * si) * sign)
        conv = keep(packed, rows, out_re, out_im, twist, ends)
        lags = keep(lagged, rows, lag_re, lag_im, twist, ends)
        return (conv, lags)

    conv, lags = each_bin(bins, twist, visit)
    put_back(packed, conv)
    put_back(lagged, lags)


def shifted(value, step):
    rows = value.shape[0]
    row = lax.broadcasted_iota(jnp.int32, value.shape, 0)
    edge = 0 if step == 1 else rows - 1
    return jnp.where(row == edge, 0.0, pltpu.roll(value, step % rows, 0))


def remote(source, target, send_sems, recv_sems, d):
    return pltpu.make_async_remote_copy(
        src_ref=source,
        dst_ref=target,
        send_sem=send_sems.at[d],
        recv_sem=recv_sems.at[d],
        device_id=(lax.axis_index("groups"), lax.axis_index("tm") ^ d),
        device_id_type=pl.DeviceIdType.MESH,
    )


class Exchange:
    def __init__(self, send, got, sems, peers, same=False):
        self.send, self.got, self.sems, self.peers, self.same = send, got, sems, peers, same

    def copies(self):
        me = lax.axis_index("tm")
        for d in range(1, self.peers):
            source = self.send if self.same else self.send.at[me ^ d]
            yield remote(source, self.got.at[me], self.sems.at[0], self.sems.at[1], d)

    def own(self):
        me = lax.axis_index("tm")
        source = self.send if self.same else self.send.at[me]
        return pltpu.make_async_copy(source, self.got.at[me], self.sems.at[0, 0])

    def start(self):
        for copy in self.copies():
            copy.start()
        self.own().start()

    def wait_recv(self):
        self.own().wait()
        for copy in self.copies():
            copy.wait_recv()

    def wait_send(self):
        for copy in self.copies():
            copy.wait_send()


def window_kernel(
    tok_ref, offsets, taps_ref, w_hbm, cot_hbm, table_hbm, filters_hbm, forward_hbm, inverse_hbm, twist_hbm,
    mix_home, home, tap_home, lag_out,
    w_ref, cot_ref, table, filters, forward, inverse, twist,
    tok_own, tok_got, w_send, w_got, cot_send, cot_got, mix_back, back, tap_own,
    used, emb, emb_t, w_own, proj, gates, first_gate, upstream,
    series, bins, filt_re, filt_im, spec_re, spec_im, packed, lagged, wave, grad_b, grad_a, grad_proj, lags_by_channel,
    load_sems, lag_sem, tok_sems, w_sems, cot_sems, mix_sems, out_sems, tap_sems,
):
    peers, _, _ = w_got.shape
    rows, width = cot_ref.shape
    half = LANES // 2
    quarter = inverse.shape[0]
    block = rows // 4
    fields = tok_ref.shape[0]
    me = lax.axis_index("tm")
    others = range(1, peers)

    loads = [
        pltpu.make_async_copy(source, target, load_sems.at[i])
        for i, (source, target) in enumerate(
            [
                (w_hbm, w_ref), (cot_hbm, cot_ref), (table_hbm, table), (filters_hbm, filters),
                (forward_hbm, forward), (twist_hbm, twist), (inverse_hbm, inverse),
            ]
        )
    ]
    for load in loads:
        load.start()
    barrier = pltpu.get_barrier_semaphore()
    for d in others:
        pl.semaphore_signal(
            barrier,
            inc=1,
            device_id=(lax.axis_index("groups"), me ^ d),
            device_id_type=pl.DeviceIdType.MESH,
        )

    to_tok = Exchange(tok_own, tok_got, tok_sems, peers, same=True)
    to_w = Exchange(w_send, w_got, w_sems, peers)
    to_cot = Exchange(cot_send, cot_got, cot_sems, peers)
    to_mix = Exchange(mix_back, mix_home, mix_sems, peers)
    to_out = Exchange(back, home, out_sems, peers)
    to_tap = Exchange(tap_own, tap_home, tap_sems, peers, same=True)

    pick = pick_quarter(rows)
    tok_own[...] = lax.dot_general(
        narrow(tok_ref[...].astype(jnp.float32)), pick, (((1,), (1,)), ((), ())), preferred_element_type=jnp.float32
    )

    def fill(send, q, pairs):
        for side in range(2):
            mine = slice(side * half, (side + 1) * half)
            send[q + side] = jnp.concatenate(
                [jnp.concatenate([a[:, mine], b[:, mine]], axis=1) for a, b in pairs], axis=0
            )

    loads[0].wait()
    for q in range(0, peers, 2):
        value, gate1, gate2 = [w_ref[:, j * width + q * half : j * width + (q + 2) * half] for j in range(3)]
        fill(w_send, q, [(value, gate2), (gate1[: half // 2], gate1[half // 2 :])])
    pl.semaphore_wait(barrier, peers - 1)
    to_tok.start()
    to_w.start()
    loads[1].wait()
    turned = narrow(dot(pick, cot_ref[...]))
    for q in range(0, peers, 2):
        steps = [turned[p * block : (p + 1) * block, q * half : (q + 2) * half] for p in range(4)]
        fill(cot_send, q, [(steps[0], steps[1]), (steps[2], steps[3])])
    to_cot.start()

    loads[2].wait()
    col = lax.broadcasted_iota(jnp.int32, (CODES, table.shape[0]), 1)
    col = col - lax.broadcasted_iota(jnp.int32, (CODES, table.shape[0]), 0)
    group = 4
    for field in range(0, fields, group):
        chosen = [narrow(jnp.where(col == offsets[field + s], 1.0, 0.0)) for s in range(group)]
        found = dot(jnp.concatenate(chosen, axis=0), table[...])
        used[field * CODES : (field + group) * CODES, :] = narrow(found)
    for load in loads[3:6]:
        load.wait()
    filter_spectrum(filters, forward, twist, series, bins, filt_re, filt_im)

    to_tok.wait_recv()
    lanes = lax.broadcasted_iota(jnp.int32, (rows, CODES), 1).astype(jnp.float32)

    def embed(i, carry):
        hot = []
        for s in range(2):
            steps = tok_got[2 * i + s].T
            hot.append(
                jnp.concatenate(
                    [
                        narrow(jnp.where(steps[:, field : field + 1] == lanes, 1.0, 0.0))
                        for field in range(fields)
                    ],
                    axis=1,
                )
            )
        summed = dot(jnp.concatenate(hot, axis=0), used[...])
        rounded = narrow(summed)
        emb_t[:, pl.ds(pl.multiple_of(i * 2 * rows, 2 * rows), 2 * rows)] = rounded.T
        for s in range(2):
            for p in range(4):
                start = s * rows + p * block
                emb[p, 2 * i + s] = rounded[start : start + block]
        return carry

    lax.fori_loop(0, peers // 2, embed, 0)
    loads[6].wait()

    to_w.wait_recv()
    near = left_lanes(half // 2)
    for peer in range(peers):
        own = slice(peer * half, (peer + 1) * half)
        w_own[own, :LANES] = w_got[peer, :half]
        gate = widen(w_got[peer, half:])
        other = swap(gate)
        both = jnp.concatenate([jnp.where(near, gate, other), jnp.where(near, other, gate)], axis=0)
        w_own[own, LANES:] = narrow(both)
    place = pl.multiple_of(me // 2 * LANES, LANES)
    odd = me % 2 == 1
    near3 = left_lanes(3)
    own_taps = []
    for j in range(3):
        piece = taps_ref[:, pl.ds(pl.multiple_of(place + j * width, LANES), LANES)]
        own_taps.append(jnp.where(odd, swap(piece), piece))
    taps = jnp.concatenate(
        [jnp.where(near3, own_taps[0], swap(own_taps[2])), jnp.where(near3, own_taps[1], swap(own_taps[1]))], axis=1
    )
    tap = [taps[j : j + 1] for j in range(3)]

    for p in range(4):
        proj[p] = widen(narrow(dot(emb[p].reshape(quarter, width), w_own[...])))

    def back_by(p, steps):
        return proj[p - steps] if p >= steps else shifted(proj[p - steps + 4], 1)

    for p in range(4):
        mixed = widen(narrow(tap[0] * proj[p] + tap[1] * back_by(p, 1) + tap[2] * back_by(p, 2)))
        gates[p] = mixed[:, :LANES]
        first_gate[p] = mixed[:, LANES:]
    to_cot.wait_recv()
    left = left_lanes(quarter)
    for p in range(0, 4, 2):
        steps = widen(cot_got[:, p // 2 * block : (p // 2 + 1) * block, :].reshape(quarter, LANES))
        upstream[p] = jnp.where(left, 1.0, swap(steps))
        upstream[p + 1] = jnp.where(left, 1.0, steps)
    for p in range(4):
        series[:, lanes_of(p)] = narrow(gates[p] * upstream[p])

    matmul_rows(forward, series, bins)
    first_product(bins, twist, filt_re, filt_im, spec_re, spec_im, packed)
    matmul_rows(inverse, packed, wave)
    for p in range(4):
        out = widen(narrow(wave[:, lanes_of(p)]))
        flipped = swap(out)
        series[:, lanes_of(p)] = narrow(flipped * first_gate[p])
        grad_b[p] = widen(narrow(out * flipped))

    matmul_rows(forward, series, bins)
    second_product(bins, twist, filt_re, filt_im, spec_re, spec_im, packed, lagged)
    matmul_rows(inverse, packed, wave)
    mixed = []
    for p in range(4):
        out = widen(narrow(wave[:, lanes_of(p)]))
        mixed.append(gates[p] * out)
        grad_a[p] = widen(narrow(upstream[p] * out))
    for p in range(0, 4, 2):
        start = p // 2 * block
        both = narrow(jnp.where(left, swap(mixed[p]), mixed[p + 1]))
        mix_back[:, start : start + block, :] = both.reshape(peers, block, LANES)
    to_mix.start()

    def ahead(grad, p, steps):
        return grad[p + steps] if p + steps < 4 else shifted(grad[p + steps - 4], -1)

    sums = []
    for grad, own in ((grad_a, slice(0, LANES)), (grad_b, slice(LANES, 2 * LANES))):
        total = [jnp.zeros((1, LANES), jnp.float32)] * 3
        for p in range(4):
            here = grad[p]
            out = tap[0][:, own] * here + tap[1][:, own] * ahead(grad, p, 1) + tap[2][:, own] * ahead(grad, p, 2)
            grad_proj[:, p, :, own] = narrow(out).reshape(peers, block, LANES)
            for j in range(3):
                lag = proj[p - j, :, own] if p >= j else shifted(proj[p - j + 4, :, own], 1)
                total[j] = total[j] + jnp.sum(here * lag, axis=0, keepdims=True)
        sums += total
    tap_own[...] = jnp.concatenate(sums + [jnp.zeros((2, LANES), jnp.float32)], axis=0)
    to_tap.start()

    group = 4
    sends = list(to_out.copies())
    for step in (1, 2, 3, 0):
        first = (me // group ^ step) * group
        own = pl.ds(pl.multiple_of(first * half, group * half), group * half)
        terms = dot(emb_t[own, :], grad_proj[...].reshape(peers * rows, 2 * LANES))
        for s in range(group):
            here = terms[s * half : (s + 1) * half]
            back[first + s, :half, :] = narrow(here[:, :LANES])
            twin = here[:, LANES:]
            back[first + s, half:, :] = narrow(jnp.where(near, twin[: half // 2], twin[half // 2 :]))
        for d in range(max(1, step * group), (step + 1) * group):
            sends[d - 1].start()
    to_out.own().start()

    matmul_rows(inverse, lagged, wave)
    part = quarter // 4
    order = pick_quarter(quarter)
    for b in range(4):
        lags = jnp.concatenate(
            [wave[b * part : (b + 1) * part, lanes_of(p)].T for p in range(4)], axis=1
        )
        high = narrow(lags)
        rest = narrow(lags - widen(high))
        out = dot(high, order) + dot(rest, order)
        span = slice(b * quarter, (b + 1) * quarter)
        lags_by_channel[0, :, span] = out[:half]
        lags_by_channel[1, :, span] = out[half:]
    leave = pltpu.make_async_copy(lags_by_channel, lag_out, lag_sem)
    leave.start()

    for exchange in (to_mix, to_tap, to_out):
        exchange.wait_recv()
    for exchange in (to_tok, to_w, to_cot, to_mix, to_tap, to_out):
        exchange.wait_send()
    leave.wait()


def unpack_kernel(
    mix_hbm, hbm, tap_hbm, lags, mixer_out, weight_out, tap_out, filter_out, mix_home, home, tap_home, sems
):
    peers, block, _ = mix_home.shape
    block = block // 2
    half = LANES // 2
    width = peers * half
    loads = [
        pltpu.make_async_copy(source, target, sems.at[i])
        for i, (source, target) in enumerate(
            [(mix_hbm, mix_home), (tap_hbm, tap_home), (hbm, home), (lags, filter_out)]
        )
    ]
    for load in loads:
        load.start()
    loads[0].wait()
    columns = []
    for q in range(0, peers, 2):
        one, two = mix_home[q], mix_home[q + 1]
        pieces = []
        for p in range(4):
            at = slice(p // 2 * block, (p // 2 + 1) * block)
            mine = slice(p % 2 * half, (p % 2 + 1) * half)
            pieces.append(jnp.concatenate([one[at, mine], two[at, mine]], axis=1))
        columns.append(jnp.concatenate(pieces, axis=0))
    mixer_out[...] = narrow(
        lax.dot_general(
            pick_quarter(4 * block),
            jnp.concatenate(columns, axis=1),
            (((0,), (0,)), ((), ())),
            preferred_element_type=jnp.float32,
        )
    )
    loads[1].wait()
    loads[2].wait()
    for q in range(0, peers, 2):
        start = q * half
        one, two = tap_home[q], tap_home[q + 1]
        for j, (row, side) in enumerate(((0, 0), (3, 0), (0, 1))):
            mine = slice(side * half, (side + 1) * half)
            tap_out[:, j * width + start : j * width + start + LANES] = jnp.concatenate(
                [one[row : row + 3, mine], two[row : row + 3, mine]], axis=1
            )
        one, two = home[q], home[q + 1]
        for side in range(2):
            mine = slice(side * half, (side + 1) * half)
            column = 2 * side * width + start
            weight_out[:, column : column + LANES] = widen(
                jnp.concatenate([one[:half, mine], two[:half, mine]], axis=1)
            )
            at = slice(side * half // 2, (side + 1) * half // 2)
            weight_out[at, width + start : width + start + LANES] = widen(
                jnp.concatenate([one[half:, mine], two[half:, mine]], axis=1)
            )
    loads[3].wait()


def fast_local(token_ids, field_offsets, embed_table, w_in, short_taps, filters, cotangent):
    rows, width = cotangent.shape
    fields = token_ids.shape[1]
    peers = lax.axis_size("tm")
    length = rows * peers
    quarter = length // 4
    forward, inverse, twist = basis(quarter)
    whole = pl.BlockSpec(memory_space=pltpu.VMEM)
    anywhere = pl.BlockSpec(memory_space=pl.ANY)
    f32, bf16 = jnp.float32, jnp.bfloat16
    half = LANES // 2
    sems = pltpu.SemaphoreType.DMA((2, peers))
    wide = 4 * LANES
    scratch = [
        pltpu.VMEM(w_in.shape, bf16),
        pltpu.VMEM(cotangent.shape, bf16),
        pltpu.VMEM(embed_table.shape, bf16),
        pltpu.VMEM(filters.shape, bf16),
        pltpu.VMEM(forward.shape, bf16),
        pltpu.VMEM(inverse.shape, bf16),
        pltpu.VMEM(twist.shape, f32),
        pltpu.VMEM((fields, rows), f32),
        pltpu.VMEM((peers, fields, rows), f32),
        pltpu.VMEM((peers, half + half // 2, LANES), bf16),
        pltpu.VMEM((peers, half + half // 2, LANES), bf16),
        pltpu.VMEM((peers, rows // 2, LANES), bf16),
        pltpu.VMEM((peers, rows // 2, LANES), bf16),
        pltpu.VMEM((peers, rows // 2, LANES), bf16),
        pltpu.VMEM((peers, half + half // 2, LANES), bf16),
        pltpu.VMEM((8, LANES), f32),
        pltpu.VMEM((fields * CODES, width), bf16),
        pltpu.VMEM((4, peers, rows // 4, width), bf16),
        pltpu.VMEM((width, length), bf16),
        pltpu.VMEM((width, 2 * LANES), bf16),
        pltpu.VMEM((4, quarter, 2 * LANES), f32),
        pltpu.VMEM((4, quarter, LANES), f32),
        pltpu.VMEM((4, quarter, LANES), f32),
        pltpu.VMEM((4, quarter, LANES), f32),
        pltpu.VMEM((quarter, wide), bf16),
        pltpu.VMEM((2 * quarter, wide), f32),
        pltpu.VMEM((4, quarter + 8, LANES), f32),
        pltpu.VMEM((4, quarter + 8, LANES), f32),
        pltpu.VMEM((4, quarter + 8, LANES), f32),
        pltpu.VMEM((4, quarter + 8, LANES), f32),
        pltpu.VMEM((2 * quarter, wide), bf16),
        pltpu.VMEM((2 * quarter, wide), bf16),
        pltpu.VMEM((quarter, wide), f32),
        pltpu.VMEM((4, quarter, LANES), f32),
        pltpu.VMEM((4, quarter, LANES), f32),
        pltpu.VMEM((peers, 4, rows // 4, 2 * LANES), bf16),
        pltpu.VMEM(filters.shape, f32),
        pltpu.SemaphoreType.DMA((7,)),
        pltpu.SemaphoreType.DMA,
    ] + [sems] * 6
    homes = pl.pallas_call(
        window_kernel,
        out_shape=(
            jax.ShapeDtypeStruct((peers, rows // 2, LANES), bf16),
            jax.ShapeDtypeStruct((peers, half + half // 2, LANES), bf16),
            jax.ShapeDtypeStruct((peers, 8, LANES), f32),
            jax.ShapeDtypeStruct(filters.shape, f32),
        ),
        in_specs=[whole, pl.BlockSpec(memory_space=pltpu.SMEM), whole] + [anywhere] * 7,
        out_specs=(anywhere,) * 4,
        scratch_shapes=scratch,
        compiler_params=pltpu.CompilerParams(
            vmem_limit_bytes=VMEM, collective_id=0, has_side_effects=True
        ),
        name="window",
    )(
        token_ids.T,
        field_offsets,
        short_taps,
        w_in,
        cotangent,
        embed_table,
        filters,
        jnp.asarray(forward),
        jnp.asarray(inverse),
        jnp.asarray(twist),
    )
    return tuple(
        pl.pallas_call(
            unpack_kernel,
            out_shape=(
                jax.ShapeDtypeStruct((rows, width), bf16),
                jax.ShapeDtypeStruct((half, 3 * width), f32),
                jax.ShapeDtypeStruct((3, 3 * width), f32),
                jax.ShapeDtypeStruct(filters.shape, f32),
            ),
            in_specs=[anywhere] * 4,
            out_specs=(whole,) * 4,
            scratch_shapes=[pltpu.VMEM(home.shape, home.dtype) for home in homes[:3]]
            + [pltpu.SemaphoreType.DMA((4,))],
            compiler_params=pltpu.CompilerParams(vmem_limit_bytes=VMEM),
            name="unpack",
        )(*homes)
    )


def cis_tables(count_a, count_b, modulus):
    left = jnp.arange(count_a, dtype=jnp.int32)[:, None]
    right = jnp.arange(count_b, dtype=jnp.int32)[None, :]
    angle = 2.0 * math.pi / modulus * (left * right % modulus).astype(jnp.float32)
    return (jnp.cos(angle), jnp.sin(angle))


class Factored:
    def __init__(self, total):
        bits = total.bit_length() - 1
        first_len = 1 << (bits + 1) // 2
        second_len = total // first_len
        first_cos, first_sin = cis_tables(first_len, first_len // 2, first_len)
        second_cos, second_sin = cis_tables(second_len, second_len, second_len)
        self.total = total
        self.second_len = second_len
        self.twist_cos, self.twist_sin = cis_tables(first_len, second_len, total)
        self.first_both = jnp.concatenate([first_cos, -first_sin], axis=0)
        self.forward = jnp.block([[second_cos, -second_sin], [second_sin, second_cos]])
        self.inverse = jnp.block([[second_cos, second_sin], [-second_sin, second_cos]])

    def spectrum(self, series):
        series = widen(series)
        channels, length = series.shape
        rows_k = self.twist_cos.shape[0]
        half = self.first_both.shape[1]
        blocks = series.reshape(channels, half, length // half)
        part = jnp.einsum("ka,cab->ckb", self.first_both, blocks)
        part_re = part[:, :rows_k]
        part_im = part[:, rows_k:]
        turn_re = part_re * self.twist_cos + part_im * self.twist_sin
        turn_im = part_im * self.twist_cos - part_re * self.twist_sin
        turned = jnp.concatenate([turn_re, turn_im], axis=2)
        result = jnp.einsum("ckb,bm->ckm", turned, self.forward)
        return (result[:, :, : self.second_len], result[:, :, self.second_len :])

    def product(self, left, right, conjugate):
        left_re, left_im = left
        right_re, right_im = right
        if conjugate:
            right_im = -right_im
        return (left_re * right_re - left_im * right_im, left_re * right_im + left_im * right_re)

    def signal(self, pair):
        joined = jnp.concatenate(pair, axis=2)
        back = jnp.einsum("ckm,mb->ckb", joined, self.inverse)
        back_re = back[:, :, : self.second_len]
        back_im = back[:, :, self.second_len :]
        turn_re = back_re * self.twist_cos - back_im * self.twist_sin
        turn_im = back_im * self.twist_cos + back_re * self.twist_sin
        turned = jnp.concatenate([turn_re, turn_im], axis=1)
        blocks = jnp.einsum("ka,ckb->cab", self.first_both, turned)
        return blocks.reshape(joined.shape[0], -1) * (1.0 / self.total)


def delayed(array, steps):
    length = array.shape[1]
    return jnp.pad(array, ((0, 0), (steps, 0)))[:, :length]


def advanced(array, steps):
    return jnp.pad(array, ((0, 0), (0, steps)))[:, steps:]


def wide_local(token_ids, field_offsets, embed_table, w_in, short_taps, filters, cotangent):
    rows, width = cotangent.shape
    fields = token_ids.shape[1]
    peers = lax.axis_size("tm")
    me = lax.axis_index("tm")
    chans = width // peers
    length = rows * peers
    vocab = embed_table.shape[0]

    w_part = w_in.reshape(chans, 3, peers, chans).transpose(2, 0, 1, 3).reshape(peers, chans, 3 * chans)
    cot_part = cotangent.reshape(rows, peers, chans).transpose(1, 2, 0)
    tok_part = narrow(token_ids).T.reshape(1, chans, -1)
    tok_part = jnp.broadcast_to(tok_part, (peers,) + tok_part.shape[1:])
    sent = jnp.concatenate([w_part, cot_part, tok_part], axis=2)
    got = lax.all_to_all(sent, "tm", split_axis=0, concat_axis=0, tiled=True)
    w_own = got[:, :, : 3 * chans].reshape(width, 3 * chans)
    upstream = widen(got[:, :, 3 * chans : 3 * chans + rows].transpose(1, 0, 2).reshape(chans, length))
    tokens = got[:, :, 3 * chans + rows :].reshape(peers, fields, rows)
    tokens = tokens.transpose(1, 0, 2).reshape(fields, length).astype(jnp.int32)
    row_index = tokens + field_offsets[:, None]

    codes = lax.broadcasted_iota(jnp.int32, (vocab, length), 0)
    counts = jnp.zeros((vocab, length), jnp.float32)
    for field in range(fields):
        counts = counts + jnp.where(codes == row_index[field][None, :], 1.0, 0.0)
    embedded = narrow(
        jnp.einsum("vr,vt->rt", embed_table, narrow(counts), preferred_element_type=jnp.float32)
    )
    proj = narrow(jnp.einsum("rc,rt->ct", w_own, embedded, preferred_element_type=jnp.float32))
    taps = lax.dynamic_index_in_dim(short_taps.reshape(3, 3, peers, chans), me, 2, keepdims=False)
    taps = taps.reshape(3, 3 * chans, 1)
    proj_wide = widen(proj)
    lags = (proj_wide, delayed(proj_wide, 1), delayed(proj_wide, 2))
    mixed = narrow(taps[0] * lags[0] + taps[1] * lags[1] + taps[2] * lags[2])
    values = mixed[:chans]
    first_gate = widen(mixed[chans : 2 * chans])
    second_gate = widen(mixed[2 * chans :])

    transform = Factored(2 * length)

    def spectra(*series):
        whole = transform.spectrum(jnp.concatenate(series, axis=0))
        return [
            tuple(part[i * chans : (i + 1) * chans] for part in whole) for i in range(len(series))
        ]

    def signals(*pairs):
        whole = transform.signal(tuple(jnp.concatenate(parts, axis=0) for parts in zip(*pairs)))
        return [whole[i * chans : (i + 1) * chans] for i in range(len(pairs))]

    grad_conv2 = narrow(upstream * second_gate)
    first_spec, second_spec, value_spec, grad_spec2 = spectra(
        filters[0], filters[1], values, grad_conv2
    )
    first_conv, grad_mix = signals(
        transform.product(value_spec, first_spec, False),
        transform.product(grad_spec2, second_spec, True),
    )
    first_conv = widen(narrow(first_conv))
    grad_mix = widen(narrow(grad_mix))
    first_mix = narrow(first_gate * first_conv)
    grad_gate1 = narrow(grad_mix * first_conv)
    grad_conv1 = narrow(grad_mix * first_gate)
    mix_spec, grad_spec1 = spectra(first_mix, grad_conv1)
    second_conv, grad_values, filter_one, filter_two = signals(
        transform.product(mix_spec, second_spec, False),
        transform.product(grad_spec1, first_spec, True),
        transform.product(grad_spec1, value_spec, True),
        transform.product(grad_spec2, mix_spec, True),
    )
    second_conv = widen(narrow(second_conv))
    mixer_out = narrow(second_gate * second_conv)
    grad_gate2 = narrow(upstream * second_conv)
    filter_grads = jnp.stack([filter_one, filter_two], axis=0)
    grad_mixed = jnp.concatenate([narrow(grad_values), grad_gate1, grad_gate2], axis=0)
    grad_wide = widen(grad_mixed)
    grad_proj = narrow(
        taps[0] * grad_wide + taps[1] * advanced(grad_wide, 1) + taps[2] * advanced(grad_wide, 2)
    )
    tap_terms = jnp.stack([jnp.sum(grad_wide * lag, axis=1) for lag in lags], axis=0)
    weight_terms = narrow(
        jnp.einsum("rt,ct->rc", embedded, grad_proj, preferred_element_type=jnp.float32)
    )

    weight_part = weight_terms.reshape(peers, chans, 3 * chans)
    mixer_part = mixer_out.reshape(chans, peers, rows).transpose(1, 0, 2)
    tap_part = narrow(tap_terms).reshape(1, chans, -1)
    tap_part = jnp.broadcast_to(tap_part, (peers,) + tap_part.shape[1:])
    back = lax.all_to_all(
        jnp.concatenate([weight_part, mixer_part, tap_part], axis=2),
        "tm",
        split_axis=0,
        concat_axis=0,
        tiled=True,
    )
    weight_grads = widen(
        back[:, :, : 3 * chans].reshape(peers, chans, 3, chans).transpose(1, 2, 0, 3)
    ).reshape(chans, 3 * width)
    mixer_rows = back[:, :, 3 * chans : 3 * chans + rows].reshape(width, rows).T
    tap_grads = widen(
        back[:, :, 3 * chans + rows :].reshape(peers, 3, 3, chans).transpose(1, 2, 0, 3)
    ).reshape(3, 3 * width)
    return (mixer_rows, weight_grads, tap_grads, filter_grads)


def solution(mesh):
    return jax.shard_map(
        local,
        mesh=mesh,
        in_specs=(
            P(("groups", "tm"), None),
            P("groups"),
            P(),
            P("tm", None),
            P(),
            P(None, "tm", None),
            P(("groups", "tm"), None),
        ),
        out_specs=(
            P(("groups", "tm"), None),
            P(("groups", "tm"), None),
            P("groups", None),
            P("groups", "tm", None),
        ),
        check_vma=False,
    )
```

```python
import math

import jax
import jax.numpy as jnp
import ml_dtypes
import numpy as np
from jax import lax
from jax.experimental import pallas as pl
from jax.experimental.pallas import tpu as pltpu
from jax.sharding import PartitionSpec as P

DENSE_LIMIT = 4096
CODES = 128
LANES = 128
VMEM = 56 << 20


def widen(array):
    return array.astype(jnp.float32)


def narrow(array):
    return array.astype(jnp.bfloat16)


def local(token_ids, field_offsets, embed_table, w_in, short_taps, filters, cotangent):
    peers = lax.axis_size("tm")
    rows, width = cotangent.shape
    dense = 2 * rows * peers <= DENSE_LIMIT
    fits = width == peers * LANES // 2 and rows == LANES and peers & (peers - 1) == 0
    pair = lax.axis_size("groups") == 2 and token_ids.shape[1] == 8
    plan = fast_local if dense and fits and pair else wide_local
    return plan(token_ids, field_offsets, embed_table, w_in, short_taps, filters, cotangent)


def basis(quarter):
    total = 8 * quarter
    k = np.arange(quarter)
    angle = np.outer(k, k) % (2 * quarter) * (np.pi / quarter)
    cos, sin = np.cos(angle), -np.sin(angle)
    forward = np.concatenate([cos, sin], axis=0)
    forward[quarter] = 1.0 - 2.0 * (k % 2)
    inverse = forward.T * (2.0 / total)
    inverse[:, 0] *= 0.5
    inverse[:, quarter] *= 0.5
    turn = np.arange(quarter + 8)
    turn[quarter:] = quarter
    twist = []
    for step in (1, 2, 3):
        twist += [np.cos(turn * step * (2 * np.pi / total)), np.sin(turn * step * (2 * np.pi / total))]
    twist = np.broadcast_to(np.stack(twist)[:, :, None], (6, quarter + 8, LANES))
    bf16 = ml_dtypes.bfloat16
    return (forward.astype(bf16), inverse.astype(bf16), twist.astype(np.float32))


def dot(left, right):
    return jnp.dot(left, right, preferred_element_type=jnp.float32)


def swap(value):
    return pltpu.roll(value, LANES // 2, 1)


def left_lanes(rows):
    return lax.broadcasted_iota(jnp.int32, (rows, LANES), 1) < LANES // 2


def pick_quarter(count):
    row = lax.broadcasted_iota(jnp.int32, (count, count), 0)
    col = lax.broadcasted_iota(jnp.int32, (count, count), 1)
    block = count // 4
    return narrow(jnp.where(col == 4 * (row % block) + row // block, 1.0, 0.0))


def spin(real, imag, twist, rows):
    re, im = [real[0]], [imag[0]]
    for p in (1, 2, 3):
        cos, sin = twist[2 * p - 2, rows, :], twist[2 * p - 1, rows, :]
        re.append(real[p] * cos + imag[p] * sin)
        im.append(imag[p] * cos - real[p] * sin)
    er, ei, fr, fi = re[0] + re[2], im[0] + im[2], re[0] - re[2], im[0] - im[2]
    gr, gi, hr, hi = re[1] + re[3], im[1] + im[3], re[1] - re[3], im[1] - im[3]
    return [er + gr, fr + hi, er - gr, fr - hi], [ei + gi, fi - hr, ei - gi, fi + hr]


def unspin(real, imag, twist, rows):
    er, ei, fr, fi = real[0] + real[2], imag[0] + imag[2], real[0] - real[2], imag[0] - imag[2]
    gr, gi, hr, hi = real[1] + real[3], imag[1] + imag[3], real[1] - real[3], imag[1] - imag[3]
    re, im = [er + gr, fr - hi, er - gr, fr + hi], [ei + gi, fi + hr, ei - gi, fi - hr]
    for p in (1, 2, 3):
        cos, sin = twist[2 * p - 2, rows, :], twist[2 * p - 1, rows, :]
        re[p], im[p] = re[p] * cos - im[p] * sin, im[p] * cos + re[p] * sin
    return re, im


def matmul_rows(left, right, out):
    rows = left.shape[0]
    chunk = min(256, rows)

    def body(step, carry):
        own = pl.ds(pl.multiple_of(step * chunk, chunk), chunk)
        out[own, :] = dot(left[own, :], right[...])
        return carry

    lax.fori_loop(0, rows // chunk, body, 0)


def lanes_of(p):
    return slice(p * LANES, (p + 1) * LANES)


def each_bin(bins, twist, visit):
    quarter = bins.shape[0] // 2
    last = pl.ds(quarter, 8)
    zero = jnp.zeros((8, LANES), jnp.float32)
    nyquist = [jnp.broadcast_to(bins[quarter : quarter + 1, lanes_of(p)], (8, LANES)) for p in range(4)]
    kept = visit(last, *spin(nyquist, [zero] * 4, twist, last), True)
    bins[quarter : quarter + 1, :] = jnp.zeros((1, bins.shape[1]), jnp.float32)
    chunk = 32

    def body(step, carry):
        start = pl.multiple_of(step * chunk, chunk)
        rows = pl.ds(start, chunk)
        lower = pl.ds(pl.multiple_of(quarter + start, chunk), chunk)
        real = [bins[rows, lanes_of(p)] for p in range(4)]
        imag = [bins[lower, lanes_of(p)] for p in range(4)]
        visit(rows, *spin(real, imag, twist, rows), False)
        return carry

    lax.fori_loop(0, quarter // chunk, body, 0)
    return kept


def put_back(packed, ends):
    quarter = packed.shape[0] // 2
    own = slice(quarter, quarter + 16)
    first = lax.broadcasted_iota(jnp.int32, (16, LANES), 0) == 0
    for p in range(4):
        here = widen(packed[own, lanes_of(p)])
        there = jnp.broadcast_to(ends[p][:1], (16, LANES))
        packed[own, lanes_of(p)] = narrow(jnp.where(first, there, here))


def keep(packed, rows, real, imag, twist, ends):
    re, im = unspin(real, imag, twist, rows)
    if ends:
        return re
    quarter = packed.shape[0] // 2
    lower = pl.ds(pl.multiple_of(rows.start + quarter, 16), rows.size)
    for p in range(4):
        packed[rows, lanes_of(p)] = narrow(re[p])
        packed[lower, lanes_of(p)] = narrow(im[p])
    return None


def sides(rows):
    return jnp.where(left_lanes(rows), 1.0, -1.0)


def filter_spectrum(filters, forward, twist, series, bins, spec_re, spec_im):
    length = filters.shape[2]
    both = filters.shape[0] * filters.shape[1]
    block = length // 4
    pick = pick_quarter(block)
    part = block // 4
    for b in range(4):
        chunk = filters[:, :, b * block : (b + 1) * block].reshape(both, block)
        turned = lax.dot_general(
            pick, chunk, (((1,), (1,)), ((), ())), preferred_element_type=jnp.float32
        )
        for p in range(4):
            series[b * part : (b + 1) * part, lanes_of(p)] = narrow(turned[p * part : (p + 1) * part])
    matmul_rows(forward, series, bins)

    def visit(rows, re, im, ends):
        sign = sides(rows.size)
        for m in range(4):
            spec_re[m, rows, :] = re[m]
            spec_im[m, rows, :] = im[m] * sign

    each_bin(bins, twist, visit)


def first_product(bins, twist, filt_re, filt_im, spec_re, spec_im, packed):
    def visit(rows, re, im, ends):
        out_re, out_im = [], []
        for m in range(4):
            spec_re[m, rows, :] = re[m]
            spec_im[m, rows, :] = im[m]
            fr, fi = filt_re[m, rows, :], filt_im[m, rows, :]
            out_re.append(re[m] * fr - im[m] * fi)
            out_im.append(re[m] * fi + im[m] * fr)
        return keep(packed, rows, out_re, out_im, twist, ends)

    put_back(packed, each_bin(bins, twist, visit))


def second_product(bins, twist, filt_re, filt_im, spec_re, spec_im, packed, lagged):
    def visit(rows, re, im, ends):
        out_re, out_im, lag_re, lag_im = [], [], [], []
        sign = sides(rows.size)
        for m in range(4):
            fr, fi = filt_re[m, rows, :], filt_im[m, rows, :]
            out_re.append(re[m] * fr + im[m] * fi)
            out_im.append(im[m] * fr - re[m] * fi)
            sr, si = spec_re[m, rows, :], spec_im[m, rows, :]
            lag_re.append(re[m] * sr + im[m] * si)
            lag_im.append((im[m] * sr - re[m] * si) * sign)
        conv = keep(packed, rows, out_re, out_im, twist, ends)
        lags = keep(lagged, rows, lag_re, lag_im, twist, ends)
        return (conv, lags)

    conv, lags = each_bin(bins, twist, visit)
    put_back(packed, conv)
    put_back(lagged, lags)


def shifted(value, step):
    rows = value.shape[0]
    row = lax.broadcasted_iota(jnp.int32, value.shape, 0)
    edge = 0 if step == 1 else rows - 1
    return jnp.where(row == edge, 0.0, pltpu.roll(value, step % rows, 0))


def remote(source, target, send_sems, recv_sems, d):
    return pltpu.make_async_remote_copy(
        src_ref=source,
        dst_ref=target,
        send_sem=send_sems.at[d],
        recv_sem=recv_sems.at[d],
        device_id=(lax.axis_index("groups"), lax.axis_index("tm") ^ d),
        device_id_type=pl.DeviceIdType.MESH,
    )


class Exchange:
    def __init__(self, send, got, sems, peers, same=False):
        self.send, self.got, self.sems, self.peers, self.same = send, got, sems, peers, same

    def copies(self):
        me = lax.axis_index("tm")
        for d in range(1, self.peers):
            source = self.send if self.same else self.send.at[me ^ d]
            yield remote(source, self.got.at[me], self.sems.at[0], self.sems.at[1], d)

    def own(self):
        me = lax.axis_index("tm")
        source = self.send if self.same else self.send.at[me]
        return pltpu.make_async_copy(source, self.got.at[me], self.sems.at[0, 0])

    def start(self):
        for copy in self.copies():
            copy.start()
        self.own().start()

    def wait_recv(self):
        self.own().wait()
        for copy in self.copies():
            copy.wait_recv()

    def wait_send(self):
        for copy in self.copies():
            copy.wait_send()


def window_kernel(
    tok_ref, offsets, taps_ref, w_hbm, cot_hbm, table_hbm, filters_hbm, forward_hbm, inverse_hbm, twist_hbm,
    mix_home, home, tap_home, lag_out,
    w_ref, cot_ref, table, filters, forward, inverse, twist,
    tok_own, tok_got, w_send, w_got, cot_send, cot_got, mix_back, back, tap_own,
    used, emb, w_own, proj, gates, first_gate, upstream,
    series, bins, filt_re, filt_im, spec_re, spec_im, packed, lagged, wave, grad_b, grad_a, grad_proj, lags_by_channel,
    load_sems, lag_sem, tok_sems, w_sems, relay_sems, cot_sems, mix_sems, out_sems, tap_sems,
):
    peers, _, _ = mix_home.shape
    rows, width = cot_ref.shape
    half = LANES // 2
    quarter = inverse.shape[0]
    block = rows // 4
    fields = tok_ref.shape[0]
    me = lax.axis_index("tm")
    others = range(1, peers)

    loads = [
        pltpu.make_async_copy(source, target, load_sems.at[i])
        for i, (source, target) in enumerate(
            [
                (w_hbm, w_ref), (cot_hbm, cot_ref), (table_hbm, table), (filters_hbm, filters),
                (forward_hbm, forward), (twist_hbm, twist), (inverse_hbm, inverse),
            ]
        )
    ]
    for load in loads:
        load.start()
    barrier = pltpu.get_barrier_semaphore()
    group = lax.axis_index("groups")
    for device in [(group, me ^ d) for d in others] + [(1 - group, me)]:
        pl.semaphore_signal(barrier, inc=1, device_id=device, device_id_type=pl.DeviceIdType.MESH)

    to_tok = Exchange(tok_own, tok_got, tok_sems, peers, same=True)
    to_w = Exchange(w_send.at[group], w_got.at[group], w_sems, peers)
    to_cot = Exchange(cot_send, cot_got, cot_sems, peers)
    to_mix = Exchange(mix_back, mix_home, mix_sems, peers)
    to_out = Exchange(back, home, out_sems, peers)
    to_tap = Exchange(tap_own, tap_home, tap_sems, peers, same=True)

    pick = pick_quarter(rows)
    tok_own[...] = lax.dot_general(
        narrow(tok_ref[...].astype(jnp.float32)), pick, (((1,), (1,)), ((), ())), preferred_element_type=jnp.float32
    )

    def fill(send, q, pairs):
        for side in range(2):
            mine = slice(side * half, (side + 1) * half)
            send[q + side] = jnp.concatenate(
                [jnp.concatenate([a[:, mine], b[:, mine]], axis=1) for a, b in pairs], axis=0
            )

    loads[0].wait()
    for q in range(0, peers, 2):
        value, gate1, gate2 = [w_ref[:, j * width + q * half : j * width + (q + 2) * half] for j in range(3)]
        for part in range(2):
            low, mid, high = part * half // 2, part * half // 2 + half // 4, (part + 1) * half // 2
            fill(w_send.at[part], q, [(value[low:high], gate2[low:high]), (gate1[low:mid], gate1[mid:high])])
    w_got[1 - group, me] = w_send[1 - group, me]
    pl.semaphore_wait(barrier, peers)
    to_tok.start()
    to_w.start()
    loads[1].wait()
    turned = narrow(dot(pick, cot_ref[...]))
    for q in range(0, peers, 2):
        steps = [turned[p * block : (p + 1) * block, q * half : (q + 2) * half] for p in range(4)]
        fill(cot_send, q, [(steps[0], steps[1]), (steps[2], steps[3])])
    to_cot.start()

    loads[2].wait()
    col = lax.broadcasted_iota(jnp.int32, (CODES, table.shape[0]), 1)
    col = col - lax.broadcasted_iota(jnp.int32, (CODES, table.shape[0]), 0)
    count = 4
    for field in range(0, fields, count):
        chosen = [narrow(jnp.where(col == offsets[field + s], 1.0, 0.0)) for s in range(count)]
        found = dot(jnp.concatenate(chosen, axis=0), table[...])
        used[field * CODES : (field + count) * CODES, :] = narrow(found)
    for load in loads[3:6]:
        load.wait()
    filter_spectrum(filters, forward, twist, series, bins, filt_re, filt_im)

    to_w.wait_recv()
    relays = []
    for d in others:
        half_block = w_got.at[group, me ^ d]
        relays.append(
            pltpu.make_async_remote_copy(
                src_ref=half_block,
                dst_ref=half_block,
                send_sem=relay_sems.at[0, d],
                recv_sem=relay_sems.at[1, d],
                device_id=(1 - group, me),
                device_id_type=pl.DeviceIdType.MESH,
            )
        )
    for relay in relays:
        relay.start()

    to_tok.wait_recv()
    lanes = lax.broadcasted_iota(jnp.int32, (rows, CODES), 1).astype(jnp.float32)

    def embed(i, carry):
        hot = []
        for s in range(2):
            steps = tok_got[2 * i + s].T
            hot.append(
                jnp.concatenate(
                    [
                        narrow(jnp.where(steps[:, field : field + 1] == lanes, 1.0, 0.0))
                        for field in range(fields)
                    ],
                    axis=1,
                )
            )
        summed = dot(jnp.concatenate(hot, axis=0), used[...])
        rounded = narrow(summed)
        for s in range(2):
            for p in range(4):
                start = s * rows + p * block
                emb[p, 2 * i + s] = rounded[start : start + block]
        return carry

    lax.fori_loop(0, peers // 2, embed, 0, unroll=2)
    loads[6].wait()

    for relay in relays:
        relay.wait_recv()
    near = left_lanes(half // 4)
    for peer in range(peers):
        for part in range(2):
            start = peer * half + part * half // 2
            own = slice(start, start + half // 2)
            w_own[own, :LANES] = w_got[part, peer, : half // 2]
            gate = widen(w_got[part, peer, half // 2 :])
            other = swap(gate)
            both = jnp.concatenate([jnp.where(near, gate, other), jnp.where(near, other, gate)], axis=0)
            w_own[own, LANES:] = narrow(both)
    place = pl.multiple_of(me // 2 * LANES, LANES)
    odd = me % 2 == 1
    near3 = left_lanes(3)
    own_taps = []
    for j in range(3):
        piece = taps_ref[:, pl.ds(pl.multiple_of(place + j * width, LANES), LANES)]
        own_taps.append(jnp.where(odd, swap(piece), piece))
    taps = jnp.concatenate(
        [jnp.where(near3, own_taps[0], swap(own_taps[2])), jnp.where(near3, own_taps[1], swap(own_taps[1]))], axis=1
    )
    tap = [taps[j : j + 1] for j in range(3)]

    for p in range(4):
        proj[p] = widen(narrow(dot(emb[p].reshape(quarter, width), w_own[...])))

    def back_by(p, steps):
        return proj[p - steps] if p >= steps else shifted(proj[p - steps + 4], 1)

    for p in range(4):
        mixed = widen(narrow(tap[0] * proj[p] + tap[1] * back_by(p, 1) + tap[2] * back_by(p, 2)))
        gates[p] = mixed[:, :LANES]
        first_gate[p] = mixed[:, LANES:]
    to_cot.wait_recv()
    left = left_lanes(quarter)
    for p in range(0, 4, 2):
        steps = widen(cot_got[:, p // 2 * block : (p // 2 + 1) * block, :].reshape(quarter, LANES))
        upstream[p] = jnp.where(left, 1.0, swap(steps))
        upstream[p + 1] = jnp.where(left, 1.0, steps)
    for p in range(4):
        series[:, lanes_of(p)] = narrow(gates[p] * upstream[p])

    matmul_rows(forward, series, bins)
    first_product(bins, twist, filt_re, filt_im, spec_re, spec_im, packed)
    matmul_rows(inverse, packed, wave)
    for p in range(4):
        out = widen(narrow(wave[:, lanes_of(p)]))
        flipped = swap(out)
        series[:, lanes_of(p)] = narrow(flipped * first_gate[p])
        grad_b[p] = widen(narrow(out * flipped))

    matmul_rows(forward, series, bins)
    second_product(bins, twist, filt_re, filt_im, spec_re, spec_im, packed, lagged)
    matmul_rows(inverse, packed, wave)
    mixed = []
    for p in range(4):
        out = widen(narrow(wave[:, lanes_of(p)]))
        mixed.append(gates[p] * out)
        grad_a[p] = widen(narrow(upstream[p] * out))
    for p in range(0, 4, 2):
        start = p // 2 * block
        both = narrow(jnp.where(left, swap(mixed[p]), mixed[p + 1]))
        mix_back[:, start : start + block, :] = both.reshape(peers, block, LANES)
    to_mix.start()

    def ahead(grad, p, steps):
        return grad[p + steps] if p + steps < 4 else shifted(grad[p + steps - 4], -1)

    sums = []
    for grad, own in ((grad_a, slice(0, LANES)), (grad_b, slice(LANES, 2 * LANES))):
        total = [jnp.zeros((1, LANES), jnp.float32)] * 3
        for p in range(4):
            here = grad[p]
            out = tap[0][:, own] * here + tap[1][:, own] * ahead(grad, p, 1) + tap[2][:, own] * ahead(grad, p, 2)
            grad_proj[own, p * quarter : (p + 1) * quarter] = narrow(out.T)
            for j in range(3):
                lag = proj[p - j, :, own] if p >= j else shifted(proj[p - j + 4, :, own], 1)
                total[j] = total[j] + jnp.sum(here * lag, axis=0, keepdims=True)
        sums += total
    tap_own[...] = jnp.concatenate(sums + [jnp.zeros((2, LANES), jnp.float32)], axis=0)
    to_tap.start()

    near = left_lanes(half // 2)
    count = 4
    sends = list(to_out.copies())
    for step in (1, 2, 3, 0):
        first = (me // count ^ step) * count
        own = pl.ds(pl.multiple_of(first * half, count * half), count * half)
        steps = emb[:, :, :, own].reshape(peers * rows, count * half)
        terms = dot(grad_proj[...], steps).T
        for s in range(count):
            here = terms[s * half : (s + 1) * half]
            back[first + s, :half, :] = narrow(here[:, :LANES])
            twin = here[:, LANES:]
            back[first + s, half:, :] = narrow(jnp.where(near, twin[: half // 2], twin[half // 2 :]))
        for d in range(max(1, step * count), (step + 1) * count):
            sends[d - 1].start()
    to_out.own().start()

    matmul_rows(inverse, lagged, wave)
    part = quarter // 4
    order = pick_quarter(quarter)
    for b in range(4):
        lags = jnp.concatenate(
            [wave[b * part : (b + 1) * part, lanes_of(p)].T for p in range(4)], axis=1
        )
        high = narrow(lags)
        rest = narrow(lags - widen(high))
        out = dot(high, order) + dot(rest, order)
        span = slice(b * quarter, (b + 1) * quarter)
        lags_by_channel[0, :, span] = out[:half]
        lags_by_channel[1, :, span] = out[half:]
    leave = pltpu.make_async_copy(lags_by_channel, lag_out, lag_sem)
    leave.start()

    for exchange in (to_mix, to_tap, to_out):
        exchange.wait_recv()
    for exchange in (to_tok, to_w, to_cot, to_mix, to_tap, to_out):
        exchange.wait_send()
    for relay in relays:
        relay.wait_send()
    leave.wait()


def unpack_kernel(
    mix_hbm, hbm, tap_hbm, lags, mixer_out, weight_out, tap_out, filter_out, mix_home, home, tap_home, sems
):
    peers, block, _ = mix_home.shape
    block = block // 2
    half = LANES // 2
    width = peers * half
    loads = [
        pltpu.make_async_copy(source, target, sems.at[i])
        for i, (source, target) in enumerate(
            [(mix_hbm, mix_home), (tap_hbm, tap_home), (hbm, home), (lags, filter_out)]
        )
    ]
    for load in loads:
        load.start()
    loads[0].wait()
    columns = []
    for q in range(0, peers, 2):
        one, two = mix_home[q], mix_home[q + 1]
        pieces = []
        for p in range(4):
            at = slice(p // 2 * block, (p // 2 + 1) * block)
            mine = slice(p % 2 * half, (p % 2 + 1) * half)
            pieces.append(jnp.concatenate([one[at, mine], two[at, mine]], axis=1))
        columns.append(jnp.concatenate(pieces, axis=0))
    mixer_out[...] = narrow(
        lax.dot_general(
            pick_quarter(4 * block),
            jnp.concatenate(columns, axis=1),
            (((0,), (0,)), ((), ())),
            preferred_element_type=jnp.float32,
        )
    )
    loads[1].wait()
    loads[2].wait()
    for q in range(0, peers, 2):
        start = q * half
        one, two = tap_home[q], tap_home[q + 1]
        for j, (row, side) in enumerate(((0, 0), (3, 0), (0, 1))):
            mine = slice(side * half, (side + 1) * half)
            tap_out[:, j * width + start : j * width + start + LANES] = jnp.concatenate(
                [one[row : row + 3, mine], two[row : row + 3, mine]], axis=1
            )
        one, two = home[q], home[q + 1]
        for side in range(2):
            mine = slice(side * half, (side + 1) * half)
            column = 2 * side * width + start
            weight_out[:, column : column + LANES] = widen(
                jnp.concatenate([one[:half, mine], two[:half, mine]], axis=1)
            )
            at = slice(side * half // 2, (side + 1) * half // 2)
            weight_out[at, width + start : width + start + LANES] = widen(
                jnp.concatenate([one[half:, mine], two[half:, mine]], axis=1)
            )
    loads[3].wait()


def fast_local(token_ids, field_offsets, embed_table, w_in, short_taps, filters, cotangent):
    rows, width = cotangent.shape
    fields = token_ids.shape[1]
    peers = lax.axis_size("tm")
    length = rows * peers
    quarter = length // 4
    forward, inverse, twist = basis(quarter)
    whole = pl.BlockSpec(memory_space=pltpu.VMEM)
    anywhere = pl.BlockSpec(memory_space=pl.ANY)
    f32, bf16 = jnp.float32, jnp.bfloat16
    half = LANES // 2
    sems = pltpu.SemaphoreType.DMA((2, peers))
    wide = 4 * LANES
    scratch = [
        pltpu.VMEM(w_in.shape, bf16),
        pltpu.VMEM(cotangent.shape, bf16),
        pltpu.VMEM(embed_table.shape, bf16),
        pltpu.VMEM(filters.shape, bf16),
        pltpu.VMEM(forward.shape, bf16),
        pltpu.VMEM(inverse.shape, bf16),
        pltpu.VMEM(twist.shape, f32),
        pltpu.VMEM((fields, rows), f32),
        pltpu.VMEM((peers, fields, rows), f32),
        pltpu.VMEM((2, peers, half // 2 + half // 4, LANES), bf16),
        pltpu.VMEM((2, peers, half // 2 + half // 4, LANES), bf16),
        pltpu.VMEM((peers, rows // 2, LANES), bf16),
        pltpu.VMEM((peers, rows // 2, LANES), bf16),
        pltpu.VMEM((peers, rows // 2, LANES), bf16),
        pltpu.VMEM((peers, half + half // 2, LANES), bf16),
        pltpu.VMEM((8, LANES), f32),
        pltpu.VMEM((fields * CODES, width), bf16),
        pltpu.VMEM((4, peers, rows // 4, width), bf16),
        pltpu.VMEM((width, 2 * LANES), bf16),
        pltpu.VMEM((4, quarter, 2 * LANES), f32),
        pltpu.VMEM((4, quarter, LANES), f32),
        pltpu.VMEM((4, quarter, LANES), f32),
        pltpu.VMEM((4, quarter, LANES), f32),
        pltpu.VMEM((quarter, wide), bf16),
        pltpu.VMEM((2 * quarter, wide), f32),
        pltpu.VMEM((4, quarter + 8, LANES), f32),
        pltpu.VMEM((4, quarter + 8, LANES), f32),
        pltpu.VMEM((4, quarter + 8, LANES), f32),
        pltpu.VMEM((4, quarter + 8, LANES), f32),
        pltpu.VMEM((2 * quarter, wide), bf16),
        pltpu.VMEM((2 * quarter, wide), bf16),
        pltpu.VMEM((quarter, wide), f32),
        pltpu.VMEM((4, quarter, LANES), f32),
        pltpu.VMEM((4, quarter, LANES), f32),
        pltpu.VMEM((2 * LANES, length), bf16),
        pltpu.VMEM(filters.shape, f32),
        pltpu.SemaphoreType.DMA((7,)),
        pltpu.SemaphoreType.DMA,
    ] + [sems] * 7
    homes = pl.pallas_call(
        window_kernel,
        out_shape=(
            jax.ShapeDtypeStruct((peers, rows // 2, LANES), bf16),
            jax.ShapeDtypeStruct((peers, half + half // 2, LANES), bf16),
            jax.ShapeDtypeStruct((peers, 8, LANES), f32),
            jax.ShapeDtypeStruct(filters.shape, f32),
        ),
        in_specs=[whole, pl.BlockSpec(memory_space=pltpu.SMEM), whole] + [anywhere] * 7,
        out_specs=(anywhere,) * 4,
        scratch_shapes=scratch,
        compiler_params=pltpu.CompilerParams(
            vmem_limit_bytes=VMEM, collective_id=0, has_side_effects=True
        ),
        name="window",
    )(
        token_ids.T,
        field_offsets,
        short_taps,
        w_in,
        cotangent,
        embed_table,
        filters,
        jnp.asarray(forward),
        jnp.asarray(inverse),
        jnp.asarray(twist),
    )
    return tuple(
        pl.pallas_call(
            unpack_kernel,
            out_shape=(
                jax.ShapeDtypeStruct((rows, width), bf16),
                jax.ShapeDtypeStruct((half, 3 * width), f32),
                jax.ShapeDtypeStruct((3, 3 * width), f32),
                jax.ShapeDtypeStruct(filters.shape, f32),
            ),
            in_specs=[anywhere] * 4,
            out_specs=(whole,) * 4,
            scratch_shapes=[pltpu.VMEM(home.shape, home.dtype) for home in homes[:3]]
            + [pltpu.SemaphoreType.DMA((4,))],
            compiler_params=pltpu.CompilerParams(vmem_limit_bytes=VMEM),
            name="unpack",
        )(*homes)
    )


def cis_tables(count_a, count_b, modulus):
    left = jnp.arange(count_a, dtype=jnp.int32)[:, None]
    right = jnp.arange(count_b, dtype=jnp.int32)[None, :]
    angle = 2.0 * math.pi / modulus * (left * right % modulus).astype(jnp.float32)
    return (jnp.cos(angle), jnp.sin(angle))


class Factored:
    def __init__(self, total):
        bits = total.bit_length() - 1
        first_len = 1 << (bits + 1) // 2
        second_len = total // first_len
        first_cos, first_sin = cis_tables(first_len, first_len // 2, first_len)
        second_cos, second_sin = cis_tables(second_len, second_len, second_len)
        self.total = total
        self.second_len = second_len
        self.twist_cos, self.twist_sin = cis_tables(first_len, second_len, total)
        self.first_both = jnp.concatenate([first_cos, -first_sin], axis=0)
        self.forward = jnp.block([[second_cos, -second_sin], [second_sin, second_cos]])
        self.inverse = jnp.block([[second_cos, second_sin], [-second_sin, second_cos]])

    def spectrum(self, series):
        series = widen(series)
        channels, length = series.shape
        rows_k = self.twist_cos.shape[0]
        half = self.first_both.shape[1]
        blocks = series.reshape(channels, half, length // half)
        part = jnp.einsum("ka,cab->ckb", self.first_both, blocks)
        part_re = part[:, :rows_k]
        part_im = part[:, rows_k:]
        turn_re = part_re * self.twist_cos + part_im * self.twist_sin
        turn_im = part_im * self.twist_cos - part_re * self.twist_sin
        turned = jnp.concatenate([turn_re, turn_im], axis=2)
        result = jnp.einsum("ckb,bm->ckm", turned, self.forward)
        return (result[:, :, : self.second_len], result[:, :, self.second_len :])

    def product(self, left, right, conjugate):
        left_re, left_im = left
        right_re, right_im = right
        if conjugate:
            right_im = -right_im
        return (left_re * right_re - left_im * right_im, left_re * right_im + left_im * right_re)

    def signal(self, pair):
        joined = jnp.concatenate(pair, axis=2)
        back = jnp.einsum("ckm,mb->ckb", joined, self.inverse)
        back_re = back[:, :, : self.second_len]
        back_im = back[:, :, self.second_len :]
        turn_re = back_re * self.twist_cos - back_im * self.twist_sin
        turn_im = back_im * self.twist_cos + back_re * self.twist_sin
        turned = jnp.concatenate([turn_re, turn_im], axis=1)
        blocks = jnp.einsum("ka,ckb->cab", self.first_both, turned)
        return blocks.reshape(joined.shape[0], -1) * (1.0 / self.total)


def delayed(array, steps):
    length = array.shape[1]
    return jnp.pad(array, ((0, 0), (steps, 0)))[:, :length]


def advanced(array, steps):
    return jnp.pad(array, ((0, 0), (0, steps)))[:, steps:]


def wide_local(token_ids, field_offsets, embed_table, w_in, short_taps, filters, cotangent):
    rows, width = cotangent.shape
    fields = token_ids.shape[1]
    peers = lax.axis_size("tm")
    me = lax.axis_index("tm")
    chans = width // peers
    length = rows * peers
    vocab = embed_table.shape[0]

    w_part = w_in.reshape(chans, 3, peers, chans).transpose(2, 0, 1, 3).reshape(peers, chans, 3 * chans)
    cot_part = cotangent.reshape(rows, peers, chans).transpose(1, 2, 0)
    tok_part = narrow(token_ids).T.reshape(1, chans, -1)
    tok_part = jnp.broadcast_to(tok_part, (peers,) + tok_part.shape[1:])
    sent = jnp.concatenate([w_part, cot_part, tok_part], axis=2)
    got = lax.all_to_all(sent, "tm", split_axis=0, concat_axis=0, tiled=True)
    w_own = got[:, :, : 3 * chans].reshape(width, 3 * chans)
    upstream = widen(got[:, :, 3 * chans : 3 * chans + rows].transpose(1, 0, 2).reshape(chans, length))
    tokens = got[:, :, 3 * chans + rows :].reshape(peers, fields, rows)
    tokens = tokens.transpose(1, 0, 2).reshape(fields, length).astype(jnp.int32)
    row_index = tokens + field_offsets[:, None]

    codes = lax.broadcasted_iota(jnp.int32, (vocab, length), 0)
    counts = jnp.zeros((vocab, length), jnp.float32)
    for field in range(fields):
        counts = counts + jnp.where(codes == row_index[field][None, :], 1.0, 0.0)
    embedded = narrow(
        jnp.einsum("vr,vt->rt", embed_table, narrow(counts), preferred_element_type=jnp.float32)
    )
    proj = narrow(jnp.einsum("rc,rt->ct", w_own, embedded, preferred_element_type=jnp.float32))
    taps = lax.dynamic_index_in_dim(short_taps.reshape(3, 3, peers, chans), me, 2, keepdims=False)
    taps = taps.reshape(3, 3 * chans, 1)
    proj_wide = widen(proj)
    lags = (proj_wide, delayed(proj_wide, 1), delayed(proj_wide, 2))
    mixed = narrow(taps[0] * lags[0] + taps[1] * lags[1] + taps[2] * lags[2])
    values = mixed[:chans]
    first_gate = widen(mixed[chans : 2 * chans])
    second_gate = widen(mixed[2 * chans :])

    transform = Factored(2 * length)

    def spectra(*series):
        whole = transform.spectrum(jnp.concatenate(series, axis=0))
        return [
            tuple(part[i * chans : (i + 1) * chans] for part in whole) for i in range(len(series))
        ]

    def signals(*pairs):
        whole = transform.signal(tuple(jnp.concatenate(parts, axis=0) for parts in zip(*pairs)))
        return [whole[i * chans : (i + 1) * chans] for i in range(len(pairs))]

    grad_conv2 = narrow(upstream * second_gate)
    first_spec, second_spec, value_spec, grad_spec2 = spectra(
        filters[0], filters[1], values, grad_conv2
    )
    first_conv, grad_mix = signals(
        transform.product(value_spec, first_spec, False),
        transform.product(grad_spec2, second_spec, True),
    )
    first_conv = widen(narrow(first_conv))
    grad_mix = widen(narrow(grad_mix))
    first_mix = narrow(first_gate * first_conv)
    grad_gate1 = narrow(grad_mix * first_conv)
    grad_conv1 = narrow(grad_mix * first_gate)
    mix_spec, grad_spec1 = spectra(first_mix, grad_conv1)
    second_conv, grad_values, filter_one, filter_two = signals(
        transform.product(mix_spec, second_spec, False),
        transform.product(grad_spec1, first_spec, True),
        transform.product(grad_spec1, value_spec, True),
        transform.product(grad_spec2, mix_spec, True),
    )
    second_conv = widen(narrow(second_conv))
    mixer_out = narrow(second_gate * second_conv)
    grad_gate2 = narrow(upstream * second_conv)
    filter_grads = jnp.stack([filter_one, filter_two], axis=0)
    grad_mixed = jnp.concatenate([narrow(grad_values), grad_gate1, grad_gate2], axis=0)
    grad_wide = widen(grad_mixed)
    grad_proj = narrow(
        taps[0] * grad_wide + taps[1] * advanced(grad_wide, 1) + taps[2] * advanced(grad_wide, 2)
    )
    tap_terms = jnp.stack([jnp.sum(grad_wide * lag, axis=1) for lag in lags], axis=0)
    weight_terms = narrow(
        jnp.einsum("rt,ct->rc", embedded, grad_proj, preferred_element_type=jnp.float32)
    )

    weight_part = weight_terms.reshape(peers, chans, 3 * chans)
    mixer_part = mixer_out.reshape(chans, peers, rows).transpose(1, 0, 2)
    tap_part = narrow(tap_terms).reshape(1, chans, -1)
    tap_part = jnp.broadcast_to(tap_part, (peers,) + tap_part.shape[1:])
    back = lax.all_to_all(
        jnp.concatenate([weight_part, mixer_part, tap_part], axis=2),
        "tm",
        split_axis=0,
        concat_axis=0,
        tiled=True,
    )
    weight_grads = widen(
        back[:, :, : 3 * chans].reshape(peers, chans, 3, chans).transpose(1, 2, 0, 3)
    ).reshape(chans, 3 * width)
    mixer_rows = back[:, :, 3 * chans : 3 * chans + rows].reshape(width, rows).T
    tap_grads = widen(
        back[:, :, 3 * chans + rows :].reshape(peers, 3, 3, chans).transpose(1, 2, 0, 3)
    ).reshape(3, 3 * width)
    return (mixer_rows, weight_grads, tap_grads, filter_grads)


def solution(mesh):
    return jax.shard_map(
        local,
        mesh=mesh,
        in_specs=(
            P(("groups", "tm"), None),
            P("groups"),
            P(),
            P("tm", None),
            P(),
            P(None, "tm", None),
            P(("groups", "tm"), None),
        ),
        out_specs=(
            P(("groups", "tm"), None),
            P(("groups", "tm"), None),
            P("groups", None),
            P("groups", "tm", None),
        ),
        check_vma=False,
    )
```

```python
import math

import jax
import jax.numpy as jnp
import ml_dtypes
import numpy as np
from jax import lax
from jax.experimental import pallas as pl
from jax.experimental.pallas import tpu as pltpu
from jax.sharding import PartitionSpec as P

DENSE_LIMIT = 4096
CODES = 128
LANES = 128
VMEM = 56 << 20


def widen(array):
    return array.astype(jnp.float32)


def narrow(array):
    return array.astype(jnp.bfloat16)


def local(token_ids, field_offsets, embed_table, w_in, short_taps, filters, cotangent):
    peers = lax.axis_size("tm")
    rows, width = cotangent.shape
    dense = 2 * rows * peers <= DENSE_LIMIT
    fits = width == peers * LANES // 2 and rows == LANES and peers & (peers - 1) == 0
    pair = lax.axis_size("groups") == 2 and token_ids.shape[1] == 8
    plan = fast_local if dense and fits and pair else wide_local
    return plan(token_ids, field_offsets, embed_table, w_in, short_taps, filters, cotangent)


def basis(quarter):
    total = 8 * quarter
    k = np.arange(quarter)
    angle = np.outer(k, k) % (2 * quarter) * (np.pi / quarter)
    cos, sin = np.cos(angle), -np.sin(angle)
    forward = np.concatenate([cos, sin], axis=0)
    forward[quarter] = 1.0 - 2.0 * (k % 2)
    inverse = forward.T * (2.0 / total)
    inverse[:, 0] *= 0.5
    inverse[:, quarter] *= 0.5
    turn = np.arange(quarter + 8)
    turn[quarter:] = quarter
    twist = []
    for step in (1, 2, 3):
        twist += [np.cos(turn * step * (2 * np.pi / total)), np.sin(turn * step * (2 * np.pi / total))]
    twist = np.broadcast_to(np.stack(twist)[:, :, None], (6, quarter + 8, LANES))
    bf16 = ml_dtypes.bfloat16
    return (forward.astype(bf16), inverse.astype(bf16), twist.astype(np.float32))


def dot(left, right):
    return jnp.dot(left, right, preferred_element_type=jnp.float32)


def swap(value):
    return pltpu.roll(value, LANES // 2, 1)


def left_lanes(rows):
    return lax.broadcasted_iota(jnp.int32, (rows, LANES), 1) < LANES // 2


def pick_quarter(count):
    row = lax.broadcasted_iota(jnp.int32, (count, count), 0)
    col = lax.broadcasted_iota(jnp.int32, (count, count), 1)
    block = count // 4
    return narrow(jnp.where(col == 4 * (row % block) + row // block, 1.0, 0.0))


def spin(real, imag, twist, rows):
    re, im = [real[0]], [imag[0]]
    for p in (1, 2, 3):
        cos, sin = twist[2 * p - 2, rows, :], twist[2 * p - 1, rows, :]
        re.append(real[p] * cos + imag[p] * sin)
        im.append(imag[p] * cos - real[p] * sin)
    er, ei, fr, fi = re[0] + re[2], im[0] + im[2], re[0] - re[2], im[0] - im[2]
    gr, gi, hr, hi = re[1] + re[3], im[1] + im[3], re[1] - re[3], im[1] - im[3]
    return [er + gr, fr + hi, er - gr, fr - hi], [ei + gi, fi - hr, ei - gi, fi + hr]


def unspin(real, imag, twist, rows):
    er, ei, fr, fi = real[0] + real[2], imag[0] + imag[2], real[0] - real[2], imag[0] - imag[2]
    gr, gi, hr, hi = real[1] + real[3], imag[1] + imag[3], real[1] - real[3], imag[1] - imag[3]
    re, im = [er + gr, fr - hi, er - gr, fr + hi], [ei + gi, fi + hr, ei - gi, fi - hr]
    for p in (1, 2, 3):
        cos, sin = twist[2 * p - 2, rows, :], twist[2 * p - 1, rows, :]
        re[p], im[p] = re[p] * cos - im[p] * sin, im[p] * cos + re[p] * sin
    return re, im


def matmul_rows(left, right, out):
    rows = left.shape[0]
    chunk = min(256, rows)

    def body(step, carry):
        own = pl.ds(pl.multiple_of(step * chunk, chunk), chunk)
        out[own, :] = dot(left[own, :], right[...])
        return carry

    lax.fori_loop(0, rows // chunk, body, 0)


def lanes_of(p):
    return slice(p * LANES, (p + 1) * LANES)


def each_bin(bins, twist, visit):
    quarter = bins.shape[0] // 2
    last = pl.ds(quarter, 8)
    zero = jnp.zeros((8, LANES), jnp.float32)
    nyquist = [jnp.broadcast_to(bins[quarter : quarter + 1, lanes_of(p)], (8, LANES)) for p in range(4)]
    kept = visit(last, *spin(nyquist, [zero] * 4, twist, last), True)
    bins[quarter : quarter + 1, :] = jnp.zeros((1, bins.shape[1]), jnp.float32)
    chunk = 32

    def body(step, carry):
        start = pl.multiple_of(step * chunk, chunk)
        rows = pl.ds(start, chunk)
        lower = pl.ds(pl.multiple_of(quarter + start, chunk), chunk)
        real = [bins[rows, lanes_of(p)] for p in range(4)]
        imag = [bins[lower, lanes_of(p)] for p in range(4)]
        visit(rows, *spin(real, imag, twist, rows), False)
        return carry

    lax.fori_loop(0, quarter // chunk, body, 0)
    return kept


def put_back(packed, ends):
    quarter = packed.shape[0] // 2
    own = slice(quarter, quarter + 16)
    first = lax.broadcasted_iota(jnp.int32, (16, LANES), 0) == 0
    for p in range(4):
        here = widen(packed[own, lanes_of(p)])
        there = jnp.broadcast_to(ends[p][:1], (16, LANES))
        packed[own, lanes_of(p)] = narrow(jnp.where(first, there, here))


def keep(packed, rows, real, imag, twist, ends):
    re, im = unspin(real, imag, twist, rows)
    if ends:
        return re
    quarter = packed.shape[0] // 2
    lower = pl.ds(pl.multiple_of(rows.start + quarter, 16), rows.size)
    for p in range(4):
        packed[rows, lanes_of(p)] = narrow(re[p])
        packed[lower, lanes_of(p)] = narrow(im[p])
    return None


def sides(rows):
    return jnp.where(left_lanes(rows), 1.0, -1.0)


def filter_spectrum(filters, forward, twist, series, bins, spec_re, spec_im):
    length = filters.shape[2]
    both = filters.shape[0] * filters.shape[1]
    block = length // 4
    pick = pick_quarter(block)
    part = block // 4
    for b in range(4):
        chunk = filters[:, :, b * block : (b + 1) * block].reshape(both, block)
        turned = lax.dot_general(
            pick, chunk, (((1,), (1,)), ((), ())), preferred_element_type=jnp.float32
        )
        for p in range(4):
            series[b * part : (b + 1) * part, lanes_of(p)] = narrow(turned[p * part : (p + 1) * part])
    matmul_rows(forward, series, bins)

    def visit(rows, re, im, ends):
        sign = sides(rows.size)
        for m in range(4):
            spec_re[m, rows, :] = re[m]
            spec_im[m, rows, :] = im[m] * sign

    each_bin(bins, twist, visit)


def first_product(bins, twist, filt_re, filt_im, spec_re, spec_im, packed):
    def visit(rows, re, im, ends):
        out_re, out_im = [], []
        for m in range(4):
            spec_re[m, rows, :] = re[m]
            spec_im[m, rows, :] = im[m]
            fr, fi = filt_re[m, rows, :], filt_im[m, rows, :]
            out_re.append(re[m] * fr - im[m] * fi)
            out_im.append(re[m] * fi + im[m] * fr)
        return keep(packed, rows, out_re, out_im, twist, ends)

    put_back(packed, each_bin(bins, twist, visit))


def second_product(bins, twist, filt_re, filt_im, spec_re, spec_im, packed, lagged):
    def visit(rows, re, im, ends):
        out_re, out_im, lag_re, lag_im = [], [], [], []
        sign = sides(rows.size)
        for m in range(4):
            fr, fi = filt_re[m, rows, :], filt_im[m, rows, :]
            out_re.append(re[m] * fr + im[m] * fi)
            out_im.append(im[m] * fr - re[m] * fi)
            sr, si = spec_re[m, rows, :], spec_im[m, rows, :]
            lag_re.append(re[m] * sr + im[m] * si)
            lag_im.append((im[m] * sr - re[m] * si) * sign)
        conv = keep(packed, rows, out_re, out_im, twist, ends)
        lags = keep(lagged, rows, lag_re, lag_im, twist, ends)
        return (conv, lags)

    conv, lags = each_bin(bins, twist, visit)
    put_back(packed, conv)
    put_back(lagged, lags)


def shifted(value, step):
    rows = value.shape[0]
    row = lax.broadcasted_iota(jnp.int32, value.shape, 0)
    edge = 0 if step == 1 else rows - 1
    return jnp.where(row == edge, 0.0, pltpu.roll(value, step % rows, 0))


def remote(source, target, send_sems, recv_sems, d):
    return pltpu.make_async_remote_copy(
        src_ref=source,
        dst_ref=target,
        send_sem=send_sems.at[d],
        recv_sem=recv_sems.at[d],
        device_id=(lax.axis_index("groups"), lax.axis_index("tm") ^ d),
        device_id_type=pl.DeviceIdType.MESH,
    )


class Exchange:
    def __init__(self, send, got, sems, peers, same=False):
        self.send, self.got, self.sems, self.peers, self.same = send, got, sems, peers, same

    def copies(self):
        me = lax.axis_index("tm")
        for d in range(1, self.peers):
            source = self.send if self.same else self.send.at[me ^ d]
            yield remote(source, self.got.at[me], self.sems.at[0], self.sems.at[1], d)

    def own(self):
        me = lax.axis_index("tm")
        source = self.send if self.same else self.send.at[me]
        return pltpu.make_async_copy(source, self.got.at[me], self.sems.at[0, 0])

    def start(self):
        for copy in self.copies():
            copy.start()
        self.own().start()

    def wait_recv(self):
        self.own().wait()
        for copy in self.copies():
            copy.wait_recv()

    def wait_send(self):
        for copy in self.copies():
            copy.wait_send()


def window_kernel(
    tok_ref, offsets, taps_ref, w_hbm, cot_hbm, table_hbm, filters_hbm, forward_hbm, inverse_hbm, twist_hbm,
    mix_home, home, tap_home, lag_out,
    w_ref, cot_ref, table, filters, forward, inverse, twist,
    tok_own, tok_got, w_send, w_got, cot_send, cot_got, mix_back, back, tap_own, tap_got,
    used, emb, w_own, proj, gates, first_gate, upstream,
    series, bins, filt_re, filt_im, spec_re, spec_im, packed, lagged, wave, grad_b, grad_a, grad_proj, lags_by_channel,
    load_sems, lag_sem, tap_sem, relay_sems, tok_sems, w_sems, cot_sems, mix_sems, out_sems, tap_sems,
):
    peers, _, _ = mix_home.shape
    rows, width = cot_ref.shape
    half = LANES // 2
    quarter = inverse.shape[0]
    block = rows // 4
    fields = tok_ref.shape[0]
    me = lax.axis_index("tm")
    others = range(1, peers)

    loads = [
        pltpu.make_async_copy(source, target, load_sems.at[i])
        for i, (source, target) in enumerate(
            [
                (w_hbm, w_ref), (cot_hbm, cot_ref), (table_hbm, table), (filters_hbm, filters),
                (forward_hbm, forward), (twist_hbm, twist), (inverse_hbm, inverse),
            ]
        )
    ]
    for load in loads:
        load.start()
    barrier = pltpu.get_barrier_semaphore()
    group = lax.axis_index("groups")
    for device in [(group, me ^ d) for d in others] + [(1 - group, me)]:
        pl.semaphore_signal(barrier, inc=1, device_id=device, device_id_type=pl.DeviceIdType.MESH)

    to_tok = Exchange(tok_own, tok_got, tok_sems, peers, same=True)
    to_w = Exchange(w_send.at[group], w_got.at[group], w_sems, peers)
    to_cot = Exchange(cot_send, cot_got, cot_sems, peers)
    to_mix = Exchange(mix_back, mix_home, mix_sems, peers)
    to_out = Exchange(back, home, out_sems, peers)
    core, chip = me % 2, me // 2
    to_tap = [
        remote(tap_own, tap_got.at[core, chip], tap_sems.at[0], tap_sems.at[1], d) for d in range(2, peers, 2)
    ]
    tap_pair = remote(tap_got.at[core], tap_got.at[core], tap_sems.at[0], tap_sems.at[1], 1)

    pick = pick_quarter(rows)
    tok_own[...] = lax.dot_general(
        narrow(tok_ref[...].astype(jnp.float32)), pick, (((1,), (1,)), ((), ())), preferred_element_type=jnp.float32
    )

    def fill(send, q, pairs):
        for side in range(2):
            mine = slice(side * half, (side + 1) * half)
            send[q + side] = jnp.concatenate(
                [jnp.concatenate([a[:, mine], b[:, mine]], axis=1) for a, b in pairs], axis=0
            )

    loads[0].wait()
    for q in range(0, peers, 2):
        value, gate1, gate2 = [w_ref[:, j * width + q * half : j * width + (q + 2) * half] for j in range(3)]
        for part in range(2):
            low, mid, high = part * half // 2, part * half // 2 + half // 4, (part + 1) * half // 2
            fill(w_send.at[part], q, [(value[low:high], gate2[low:high]), (gate1[low:mid], gate1[mid:high])])
    pl.semaphore_wait(barrier, peers)
    to_tok.start()
    to_w.start()
    loads[1].wait()
    turned = narrow(dot(pick, cot_ref[...]))
    for q in range(0, peers, 2):
        steps = [turned[p * block : (p + 1) * block, q * half : (q + 2) * half] for p in range(4)]
        fill(cot_send, q, [(steps[0], steps[1]), (steps[2], steps[3])])
    to_cot.start()

    loads[2].wait()
    col = lax.broadcasted_iota(jnp.int32, (CODES, table.shape[0]), 1)
    col = col - lax.broadcasted_iota(jnp.int32, (CODES, table.shape[0]), 0)
    count = 4
    for field in range(0, fields, count):
        chosen = [narrow(jnp.where(col == offsets[field + s], 1.0, 0.0)) for s in range(count)]
        found = dot(jnp.concatenate(chosen, axis=0), table[...])
        used[field * CODES : (field + count) * CODES, :] = narrow(found)
    for load in loads[3:6]:
        load.wait()
    filter_spectrum(filters, forward, twist, series, bins, filt_re, filt_im)

    to_tok.wait_recv()
    lanes = lax.broadcasted_iota(jnp.int32, (rows, CODES), 1).astype(jnp.float32)

    def embed(i, carry):
        hot = []
        for s in range(2):
            steps = tok_got[2 * i + s].T
            hot.append(
                jnp.concatenate(
                    [
                        narrow(jnp.where(steps[:, field : field + 1] == lanes, 1.0, 0.0))
                        for field in range(fields)
                    ],
                    axis=1,
                )
            )
        summed = dot(jnp.concatenate(hot, axis=0), used[...])
        rounded = narrow(summed)
        for s in range(2):
            for p in range(4):
                start = s * rows + p * block
                emb[p, 2 * i + s] = rounded[start : start + block]
        return carry

    ahead_of_w = 2
    lax.fori_loop(0, ahead_of_w, embed, 0, unroll=2)
    to_w.wait_recv()
    relay = pltpu.make_async_remote_copy(
        src_ref=w_got.at[group],
        dst_ref=w_got.at[group],
        send_sem=relay_sems.at[0],
        recv_sem=relay_sems.at[1],
        device_id=(1 - group, me),
        device_id_type=pl.DeviceIdType.MESH,
    )
    relay.start()
    lax.fori_loop(ahead_of_w, peers // 2, embed, 0, unroll=2)
    loads[6].wait()

    relay.wait_recv()
    near = left_lanes(half // 4)
    for peer in range(peers):
        for part in range(2):
            start = peer * half + part * half // 2
            own = slice(start, start + half // 2)
            w_own[own, :LANES] = w_got[part, peer, : half // 2]
            gate = widen(w_got[part, peer, half // 2 :])
            other = swap(gate)
            both = jnp.concatenate([jnp.where(near, gate, other), jnp.where(near, other, gate)], axis=0)
            w_own[own, LANES:] = narrow(both)
    place = pl.multiple_of(me // 2 * LANES, LANES)
    odd = me % 2 == 1
    near3 = left_lanes(3)
    own_taps = []
    for j in range(3):
        piece = taps_ref[:, pl.ds(pl.multiple_of(place + j * width, LANES), LANES)]
        own_taps.append(jnp.where(odd, swap(piece), piece))
    taps = jnp.concatenate(
        [jnp.where(near3, own_taps[0], swap(own_taps[2])), jnp.where(near3, own_taps[1], swap(own_taps[1]))], axis=1
    )
    tap = [taps[j : j + 1] for j in range(3)]

    for p in range(4):
        proj[p] = widen(narrow(dot(emb[p].reshape(quarter, width), w_own[...])))

    def back_by(p, steps):
        return proj[p - steps] if p >= steps else shifted(proj[p - steps + 4], 1)

    for p in range(4):
        mixed = widen(narrow(tap[0] * proj[p] + tap[1] * back_by(p, 1) + tap[2] * back_by(p, 2)))
        gates[p] = mixed[:, :LANES]
        first_gate[p] = mixed[:, LANES:]
    to_cot.wait_recv()
    left = left_lanes(quarter)
    for p in range(0, 4, 2):
        steps = widen(cot_got[:, p // 2 * block : (p // 2 + 1) * block, :].reshape(quarter, LANES))
        upstream[p] = jnp.where(left, 1.0, swap(steps))
        upstream[p + 1] = jnp.where(left, 1.0, steps)
    for p in range(4):
        series[:, lanes_of(p)] = narrow(gates[p] * upstream[p])

    matmul_rows(forward, series, bins)
    first_product(bins, twist, filt_re, filt_im, spec_re, spec_im, packed)
    matmul_rows(inverse, packed, wave)
    for p in range(4):
        out = widen(narrow(wave[:, lanes_of(p)]))
        flipped = swap(out)
        series[:, lanes_of(p)] = narrow(flipped * first_gate[p])
        grad_b[p] = widen(narrow(out * flipped))

    matmul_rows(forward, series, bins)
    second_product(bins, twist, filt_re, filt_im, spec_re, spec_im, packed, lagged)
    matmul_rows(inverse, packed, wave)
    mixed = []
    for p in range(4):
        out = widen(narrow(wave[:, lanes_of(p)]))
        mixed.append(gates[p] * out)
        grad_a[p] = widen(narrow(upstream[p] * out))
    for p in range(0, 4, 2):
        start = p // 2 * block
        both = narrow(jnp.where(left, swap(mixed[p]), mixed[p + 1]))
        mix_back[:, start : start + block, :] = both.reshape(peers, block, LANES)
    to_mix.start()

    def ahead(grad, p, steps):
        return grad[p + steps] if p + steps < 4 else shifted(grad[p + steps - 4], -1)

    sums = []
    for grad, own in ((grad_a, slice(0, LANES)), (grad_b, slice(LANES, 2 * LANES))):
        total = [jnp.zeros((1, LANES), jnp.float32)] * 3
        for p in range(4):
            here = grad[p]
            out = tap[0][:, own] * here + tap[1][:, own] * ahead(grad, p, 1) + tap[2][:, own] * ahead(grad, p, 2)
            grad_proj[own, p * quarter : (p + 1) * quarter] = narrow(out.T)
            for j in range(3):
                lag = proj[p - j, :, own] if p >= j else shifted(proj[p - j + 4, :, own], 1)
                total[j] = total[j] + jnp.sum(here * lag, axis=0, keepdims=True)
        sums += total
    tap_own[...] = jnp.concatenate(sums + [jnp.zeros((2, LANES), jnp.float32)], axis=0)
    tap_got[core, chip] = tap_own[...]
    for copy in to_tap:
        copy.start()

    near = left_lanes(half // 2)
    count = 4
    sends = list(to_out.copies())
    for step in (1, 2, 3, 0):
        first = (me // count ^ step) * count
        own = pl.ds(pl.multiple_of(first * half, count * half), count * half)
        steps = emb[:, :, :, own].reshape(peers * rows, count * half)
        terms = dot(grad_proj[...], steps).T
        for s in range(count):
            here = terms[s * half : (s + 1) * half]
            back[first + s, :half, :] = narrow(here[:, :LANES])
            twin = here[:, LANES:]
            back[first + s, half:, :] = narrow(jnp.where(near, twin[: half // 2], twin[half // 2 :]))
        for d in range(max(1, step * count), (step + 1) * count):
            sends[d - 1].start()
    to_out.own().start()

    matmul_rows(inverse, lagged, wave)
    part = quarter // 4
    order = pick_quarter(quarter)
    for b in range(4):
        lags = jnp.concatenate(
            [wave[b * part : (b + 1) * part, lanes_of(p)].T for p in range(4)], axis=1
        )
        high = narrow(lags)
        rest = narrow(lags - widen(high))
        out = dot(high, order) + dot(rest, order)
        span = slice(b * quarter, (b + 1) * quarter)
        lags_by_channel[0, :, span] = out[:half]
        lags_by_channel[1, :, span] = out[half:]
    leave = pltpu.make_async_copy(lags_by_channel, lag_out, lag_sem)
    leave.start()

    for copy in to_tap:
        copy.wait_recv()
    tap_pair.start()
    tap_pair.wait_recv()
    tap_leave = pltpu.make_async_copy(tap_got, tap_home, tap_sem)
    tap_leave.start()
    for exchange in (to_mix, to_out):
        exchange.wait_recv()
    for exchange in (to_tok, to_w, to_cot, to_mix, to_out):
        exchange.wait_send()
    for copy in to_tap + [tap_pair]:
        copy.wait_send()
    tap_leave.wait()
    relay.wait_send()
    leave.wait()


def unpack_kernel(
    mix_hbm, hbm, tap_hbm, lags, mixer_out, weight_out, tap_out, filter_out, mix_home, home, tap_home, sems
):
    peers, block, _ = mix_home.shape
    block = block // 2
    half = LANES // 2
    width = peers * half
    loads = [
        pltpu.make_async_copy(source, target, sems.at[i])
        for i, (source, target) in enumerate(
            [(mix_hbm, mix_home), (tap_hbm, tap_home), (hbm, home), (lags, filter_out)]
        )
    ]
    for load in loads:
        load.start()
    loads[0].wait()
    columns = []
    for q in range(0, peers, 2):
        one, two = mix_home[q], mix_home[q + 1]
        pieces = []
        for p in range(4):
            at = slice(p // 2 * block, (p // 2 + 1) * block)
            mine = slice(p % 2 * half, (p % 2 + 1) * half)
            pieces.append(jnp.concatenate([one[at, mine], two[at, mine]], axis=1))
        columns.append(jnp.concatenate(pieces, axis=0))
    mixer_out[...] = narrow(
        lax.dot_general(
            pick_quarter(4 * block),
            jnp.concatenate(columns, axis=1),
            (((0,), (0,)), ((), ())),
            preferred_element_type=jnp.float32,
        )
    )
    loads[1].wait()
    loads[2].wait()
    for q in range(0, peers, 2):
        start = q * half
        one, two = tap_home[0, q // 2], tap_home[1, q // 2]
        for j, (row, side) in enumerate(((0, 0), (3, 0), (0, 1))):
            mine = slice(side * half, (side + 1) * half)
            tap_out[:, j * width + start : j * width + start + LANES] = jnp.concatenate(
                [one[row : row + 3, mine], two[row : row + 3, mine]], axis=1
            )
        one, two = home[q], home[q + 1]
        for side in range(2):
            mine = slice(side * half, (side + 1) * half)
            column = 2 * side * width + start
            weight_out[:, column : column + LANES] = widen(
                jnp.concatenate([one[:half, mine], two[:half, mine]], axis=1)
            )
            at = slice(side * half // 2, (side + 1) * half // 2)
            weight_out[at, width + start : width + start + LANES] = widen(
                jnp.concatenate([one[half:, mine], two[half:, mine]], axis=1)
            )
    loads[3].wait()


def fast_local(token_ids, field_offsets, embed_table, w_in, short_taps, filters, cotangent):
    rows, width = cotangent.shape
    fields = token_ids.shape[1]
    peers = lax.axis_size("tm")
    length = rows * peers
    quarter = length // 4
    forward, inverse, twist = basis(quarter)
    whole = pl.BlockSpec(memory_space=pltpu.VMEM)
    anywhere = pl.BlockSpec(memory_space=pl.ANY)
    f32, bf16 = jnp.float32, jnp.bfloat16
    half = LANES // 2
    sems = pltpu.SemaphoreType.DMA((2, peers))
    wide = 4 * LANES
    scratch = [
        pltpu.VMEM(w_in.shape, bf16),
        pltpu.VMEM(cotangent.shape, bf16),
        pltpu.VMEM(embed_table.shape, bf16),
        pltpu.VMEM(filters.shape, bf16),
        pltpu.VMEM(forward.shape, bf16),
        pltpu.VMEM(inverse.shape, bf16),
        pltpu.VMEM(twist.shape, f32),
        pltpu.VMEM((fields, rows), f32),
        pltpu.VMEM((peers, fields, rows), f32),
        pltpu.VMEM((2, peers, half // 2 + half // 4, LANES), bf16),
        pltpu.VMEM((2, peers, half // 2 + half // 4, LANES), bf16),
        pltpu.VMEM((peers, rows // 2, LANES), bf16),
        pltpu.VMEM((peers, rows // 2, LANES), bf16),
        pltpu.VMEM((peers, rows // 2, LANES), bf16),
        pltpu.VMEM((peers, half + half // 2, LANES), bf16),
        pltpu.VMEM((8, LANES), f32),
        pltpu.VMEM((2, peers // 2, 8, LANES), f32),
        pltpu.VMEM((fields * CODES, width), bf16),
        pltpu.VMEM((4, peers, rows // 4, width), bf16),
        pltpu.VMEM((width, 2 * LANES), bf16),
        pltpu.VMEM((4, quarter, 2 * LANES), f32),
        pltpu.VMEM((4, quarter, LANES), f32),
        pltpu.VMEM((4, quarter, LANES), f32),
        pltpu.VMEM((4, quarter, LANES), f32),
        pltpu.VMEM((quarter, wide), bf16),
        pltpu.VMEM((2 * quarter, wide), f32),
        pltpu.VMEM((4, quarter + 8, LANES), f32),
        pltpu.VMEM((4, quarter + 8, LANES), f32),
        pltpu.VMEM((4, quarter + 8, LANES), f32),
        pltpu.VMEM((4, quarter + 8, LANES), f32),
        pltpu.VMEM((2 * quarter, wide), bf16),
        pltpu.VMEM((2 * quarter, wide), bf16),
        pltpu.VMEM((quarter, wide), f32),
        pltpu.VMEM((4, quarter, LANES), f32),
        pltpu.VMEM((4, quarter, LANES), f32),
        pltpu.VMEM((2 * LANES, length), bf16),
        pltpu.VMEM(filters.shape, f32),
        pltpu.SemaphoreType.DMA((7,)),
        pltpu.SemaphoreType.DMA,
        pltpu.SemaphoreType.DMA,
        pltpu.SemaphoreType.DMA((2,)),
    ] + [sems] * 6
    homes = pl.pallas_call(
        window_kernel,
        out_shape=(
            jax.ShapeDtypeStruct((peers, rows // 2, LANES), bf16),
            jax.ShapeDtypeStruct((peers, half + half // 2, LANES), bf16),
            jax.ShapeDtypeStruct((2, peers // 2, 8, LANES), f32),
            jax.ShapeDtypeStruct(filters.shape, f32),
        ),
        in_specs=[whole, pl.BlockSpec(memory_space=pltpu.SMEM), whole] + [anywhere] * 7,
        out_specs=(anywhere,) * 4,
        scratch_shapes=scratch,
        compiler_params=pltpu.CompilerParams(
            vmem_limit_bytes=VMEM, collective_id=0, has_side_effects=True
        ),
        name="window",
    )(
        token_ids.T,
        field_offsets,
        short_taps,
        w_in,
        cotangent,
        embed_table,
        filters,
        jnp.asarray(forward),
        jnp.asarray(inverse),
        jnp.asarray(twist),
    )
    return tuple(
        pl.pallas_call(
            unpack_kernel,
            out_shape=(
                jax.ShapeDtypeStruct((rows, width), bf16),
                jax.ShapeDtypeStruct((half, 3 * width), f32),
                jax.ShapeDtypeStruct((3, 3 * width), f32),
                jax.ShapeDtypeStruct(filters.shape, f32),
            ),
            in_specs=[anywhere] * 4,
            out_specs=(whole,) * 4,
            scratch_shapes=[pltpu.VMEM(home.shape, home.dtype) for home in homes[:3]]
            + [pltpu.SemaphoreType.DMA((4,))],
            compiler_params=pltpu.CompilerParams(vmem_limit_bytes=VMEM),
            name="unpack",
        )(*homes)
    )


def cis_tables(count_a, count_b, modulus):
    left = jnp.arange(count_a, dtype=jnp.int32)[:, None]
    right = jnp.arange(count_b, dtype=jnp.int32)[None, :]
    angle = 2.0 * math.pi / modulus * (left * right % modulus).astype(jnp.float32)
    return (jnp.cos(angle), jnp.sin(angle))


class Factored:
    def __init__(self, total):
        bits = total.bit_length() - 1
        first_len = 1 << (bits + 1) // 2
        second_len = total // first_len
        first_cos, first_sin = cis_tables(first_len, first_len // 2, first_len)
        second_cos, second_sin = cis_tables(second_len, second_len, second_len)
        self.total = total
        self.second_len = second_len
        self.twist_cos, self.twist_sin = cis_tables(first_len, second_len, total)
        self.first_both = jnp.concatenate([first_cos, -first_sin], axis=0)
        self.forward = jnp.block([[second_cos, -second_sin], [second_sin, second_cos]])
        self.inverse = jnp.block([[second_cos, second_sin], [-second_sin, second_cos]])

    def spectrum(self, series):
        series = widen(series)
        channels, length = series.shape
        rows_k = self.twist_cos.shape[0]
        half = self.first_both.shape[1]
        blocks = series.reshape(channels, half, length // half)
        part = jnp.einsum("ka,cab->ckb", self.first_both, blocks)
        part_re = part[:, :rows_k]
        part_im = part[:, rows_k:]
        turn_re = part_re * self.twist_cos + part_im * self.twist_sin
        turn_im = part_im * self.twist_cos - part_re * self.twist_sin
        turned = jnp.concatenate([turn_re, turn_im], axis=2)
        result = jnp.einsum("ckb,bm->ckm", turned, self.forward)
        return (result[:, :, : self.second_len], result[:, :, self.second_len :])

    def product(self, left, right, conjugate):
        left_re, left_im = left
        right_re, right_im = right
        if conjugate:
            right_im = -right_im
        return (left_re * right_re - left_im * right_im, left_re * right_im + left_im * right_re)

    def signal(self, pair):
        joined = jnp.concatenate(pair, axis=2)
        back = jnp.einsum("ckm,mb->ckb", joined, self.inverse)
        back_re = back[:, :, : self.second_len]
        back_im = back[:, :, self.second_len :]
        turn_re = back_re * self.twist_cos - back_im * self.twist_sin
        turn_im = back_im * self.twist_cos + back_re * self.twist_sin
        turned = jnp.concatenate([turn_re, turn_im], axis=1)
        blocks = jnp.einsum("ka,ckb->cab", self.first_both, turned)
        return blocks.reshape(joined.shape[0], -1) * (1.0 / self.total)


def delayed(array, steps):
    length = array.shape[1]
    return jnp.pad(array, ((0, 0), (steps, 0)))[:, :length]


def advanced(array, steps):
    return jnp.pad(array, ((0, 0), (0, steps)))[:, steps:]


def wide_local(token_ids, field_offsets, embed_table, w_in, short_taps, filters, cotangent):
    rows, width = cotangent.shape
    fields = token_ids.shape[1]
    peers = lax.axis_size("tm")
    me = lax.axis_index("tm")
    chans = width // peers
    length = rows * peers
    vocab = embed_table.shape[0]

    w_part = w_in.reshape(chans, 3, peers, chans).transpose(2, 0, 1, 3).reshape(peers, chans, 3 * chans)
    cot_part = cotangent.reshape(rows, peers, chans).transpose(1, 2, 0)
    tok_part = narrow(token_ids).T.reshape(1, chans, -1)
    tok_part = jnp.broadcast_to(tok_part, (peers,) + tok_part.shape[1:])
    sent = jnp.concatenate([w_part, cot_part, tok_part], axis=2)
    got = lax.all_to_all(sent, "tm", split_axis=0, concat_axis=0, tiled=True)
    w_own = got[:, :, : 3 * chans].reshape(width, 3 * chans)
    upstream = widen(got[:, :, 3 * chans : 3 * chans + rows].transpose(1, 0, 2).reshape(chans, length))
    tokens = got[:, :, 3 * chans + rows :].reshape(peers, fields, rows)
    tokens = tokens.transpose(1, 0, 2).reshape(fields, length).astype(jnp.int32)
    row_index = tokens + field_offsets[:, None]

    codes = lax.broadcasted_iota(jnp.int32, (vocab, length), 0)
    counts = jnp.zeros((vocab, length), jnp.float32)
    for field in range(fields):
        counts = counts + jnp.where(codes == row_index[field][None, :], 1.0, 0.0)
    embedded = narrow(
        jnp.einsum("vr,vt->rt", embed_table, narrow(counts), preferred_element_type=jnp.float32)
    )
    proj = narrow(jnp.einsum("rc,rt->ct", w_own, embedded, preferred_element_type=jnp.float32))
    taps = lax.dynamic_index_in_dim(short_taps.reshape(3, 3, peers, chans), me, 2, keepdims=False)
    taps = taps.reshape(3, 3 * chans, 1)
    proj_wide = widen(proj)
    lags = (proj_wide, delayed(proj_wide, 1), delayed(proj_wide, 2))
    mixed = narrow(taps[0] * lags[0] + taps[1] * lags[1] + taps[2] * lags[2])
    values = mixed[:chans]
    first_gate = widen(mixed[chans : 2 * chans])
    second_gate = widen(mixed[2 * chans :])

    transform = Factored(2 * length)

    def spectra(*series):
        whole = transform.spectrum(jnp.concatenate(series, axis=0))
        return [
            tuple(part[i * chans : (i + 1) * chans] for part in whole) for i in range(len(series))
        ]

    def signals(*pairs):
        whole = transform.signal(tuple(jnp.concatenate(parts, axis=0) for parts in zip(*pairs)))
        return [whole[i * chans : (i + 1) * chans] for i in range(len(pairs))]

    grad_conv2 = narrow(upstream * second_gate)
    first_spec, second_spec, value_spec, grad_spec2 = spectra(
        filters[0], filters[1], values, grad_conv2
    )
    first_conv, grad_mix = signals(
        transform.product(value_spec, first_spec, False),
        transform.product(grad_spec2, second_spec, True),
    )
    first_conv = widen(narrow(first_conv))
    grad_mix = widen(narrow(grad_mix))
    first_mix = narrow(first_gate * first_conv)
    grad_gate1 = narrow(grad_mix * first_conv)
    grad_conv1 = narrow(grad_mix * first_gate)
    mix_spec, grad_spec1 = spectra(first_mix, grad_conv1)
    second_conv, grad_values, filter_one, filter_two = signals(
        transform.product(mix_spec, second_spec, False),
        transform.product(grad_spec1, first_spec, True),
        transform.product(grad_spec1, value_spec, True),
        transform.product(grad_spec2, mix_spec, True),
    )
    second_conv = widen(narrow(second_conv))
    mixer_out = narrow(second_gate * second_conv)
    grad_gate2 = narrow(upstream * second_conv)
    filter_grads = jnp.stack([filter_one, filter_two], axis=0)
    grad_mixed = jnp.concatenate([narrow(grad_values), grad_gate1, grad_gate2], axis=0)
    grad_wide = widen(grad_mixed)
    grad_proj = narrow(
        taps[0] * grad_wide + taps[1] * advanced(grad_wide, 1) + taps[2] * advanced(grad_wide, 2)
    )
    tap_terms = jnp.stack([jnp.sum(grad_wide * lag, axis=1) for lag in lags], axis=0)
    weight_terms = narrow(
        jnp.einsum("rt,ct->rc", embedded, grad_proj, preferred_element_type=jnp.float32)
    )

    weight_part = weight_terms.reshape(peers, chans, 3 * chans)
    mixer_part = mixer_out.reshape(chans, peers, rows).transpose(1, 0, 2)
    tap_part = narrow(tap_terms).reshape(1, chans, -1)
    tap_part = jnp.broadcast_to(tap_part, (peers,) + tap_part.shape[1:])
    back = lax.all_to_all(
        jnp.concatenate([weight_part, mixer_part, tap_part], axis=2),
        "tm",
        split_axis=0,
        concat_axis=0,
        tiled=True,
    )
    weight_grads = widen(
        back[:, :, : 3 * chans].reshape(peers, chans, 3, chans).transpose(1, 2, 0, 3)
    ).reshape(chans, 3 * width)
    mixer_rows = back[:, :, 3 * chans : 3 * chans + rows].reshape(width, rows).T
    tap_grads = widen(
        back[:, :, 3 * chans + rows :].reshape(peers, 3, 3, chans).transpose(1, 2, 0, 3)
    ).reshape(3, 3 * width)
    return (mixer_rows, weight_grads, tap_grads, filter_grads)


def solution(mesh):
    return jax.shard_map(
        local,
        mesh=mesh,
        in_specs=(
            P(("groups", "tm"), None),
            P("groups"),
            P(),
            P("tm", None),
            P(),
            P(None, "tm", None),
            P(("groups", "tm"), None),
        ),
        out_specs=(
            P(("groups", "tm"), None),
            P(("groups", "tm"), None),
            P("groups", None),
            P("groups", "tm", None),
        ),
        check_vma=False,
    )
```

```python
import math

import jax
import jax.numpy as jnp
import ml_dtypes
import numpy as np
from jax import lax
from jax.experimental import pallas as pl
from jax.experimental.pallas import tpu as pltpu
from jax.sharding import PartitionSpec as P

DENSE_LIMIT = 4096
CODES = 128
LANES = 128
VMEM = 56 << 20


def widen(array):
    return array.astype(jnp.float32)


def narrow(array):
    return array.astype(jnp.bfloat16)


def local(token_ids, field_offsets, embed_table, w_in, short_taps, filters, cotangent):
    peers = lax.axis_size("tm")
    rows, width = cotangent.shape
    dense = 2 * rows * peers <= DENSE_LIMIT
    fits = width == peers * LANES // 2 and rows == LANES and peers & (peers - 1) == 0
    pair = lax.axis_size("groups") == 2 and token_ids.shape[1] == 8
    plan = fast_local if dense and fits and pair else wide_local
    return plan(token_ids, field_offsets, embed_table, w_in, short_taps, filters, cotangent)


def basis(quarter):
    total = 8 * quarter
    k = np.arange(quarter)
    angle = np.outer(k, k) % (2 * quarter) * (np.pi / quarter)
    cos, sin = np.cos(angle), -np.sin(angle)
    forward = np.concatenate([cos, sin], axis=0)
    forward[quarter] = 1.0 - 2.0 * (k % 2)
    inverse = forward.T * (2.0 / total)
    inverse[:, 0] *= 0.5
    inverse[:, quarter] *= 0.5
    turn = np.arange(quarter + 8)
    turn[quarter:] = quarter
    twist = []
    for step in (1, 2, 3):
        twist += [np.cos(turn * step * (2 * np.pi / total)), np.sin(turn * step * (2 * np.pi / total))]
    twist = np.broadcast_to(np.stack(twist)[:, :, None], (6, quarter + 8, LANES))
    bf16 = ml_dtypes.bfloat16
    return (forward.astype(bf16), inverse.astype(bf16), twist.astype(np.float32))


def dot(left, right):
    return jnp.dot(left, right, preferred_element_type=jnp.float32)


def swap(value):
    return pltpu.roll(value, LANES // 2, 1)


def left_lanes(rows):
    return lax.broadcasted_iota(jnp.int32, (rows, LANES), 1) < LANES // 2


def pick_quarter(count):
    row = lax.broadcasted_iota(jnp.int32, (count, count), 0)
    col = lax.broadcasted_iota(jnp.int32, (count, count), 1)
    block = count // 4
    return narrow(jnp.where(col == 4 * (row % block) + row // block, 1.0, 0.0))


def spin(real, imag, twist, rows):
    re, im = [real[0]], [imag[0]]
    for p in (1, 2, 3):
        cos, sin = twist[2 * p - 2, rows, :], twist[2 * p - 1, rows, :]
        re.append(real[p] * cos + imag[p] * sin)
        im.append(imag[p] * cos - real[p] * sin)
    er, ei, fr, fi = re[0] + re[2], im[0] + im[2], re[0] - re[2], im[0] - im[2]
    gr, gi, hr, hi = re[1] + re[3], im[1] + im[3], re[1] - re[3], im[1] - im[3]
    return [er + gr, fr + hi, er - gr, fr - hi], [ei + gi, fi - hr, ei - gi, fi + hr]


def unspin(real, imag, twist, rows):
    er, ei, fr, fi = real[0] + real[2], imag[0] + imag[2], real[0] - real[2], imag[0] - imag[2]
    gr, gi, hr, hi = real[1] + real[3], imag[1] + imag[3], real[1] - real[3], imag[1] - imag[3]
    re, im = [er + gr, fr - hi, er - gr, fr + hi], [ei + gi, fi + hr, ei - gi, fi - hr]
    for p in (1, 2, 3):
        cos, sin = twist[2 * p - 2, rows, :], twist[2 * p - 1, rows, :]
        re[p], im[p] = re[p] * cos - im[p] * sin, im[p] * cos + re[p] * sin
    return re, im


def matmul_rows(left, right, out):
    rows = left.shape[0]
    chunk = min(256, rows)

    def body(step, carry):
        own = pl.ds(pl.multiple_of(step * chunk, chunk), chunk)
        out[own, :] = dot(left[own, :], right[...])
        return carry

    lax.fori_loop(0, rows // chunk, body, 0, unroll=True)


def lanes_of(p):
    return slice(p * LANES, (p + 1) * LANES)


def each_bin(bins, twist, visit):
    quarter = bins.shape[0] // 2
    last = pl.ds(quarter, 8)
    zero = jnp.zeros((8, LANES), jnp.float32)
    nyquist = [jnp.broadcast_to(bins[quarter : quarter + 1, lanes_of(p)], (8, LANES)) for p in range(4)]
    kept = visit(last, *spin(nyquist, [zero] * 4, twist, last), True)
    bins[quarter : quarter + 1, :] = jnp.zeros((1, bins.shape[1]), jnp.float32)
    chunk = 32

    def body(step, carry):
        start = pl.multiple_of(step * chunk, chunk)
        rows = pl.ds(start, chunk)
        lower = pl.ds(pl.multiple_of(quarter + start, chunk), chunk)
        real = [bins[rows, lanes_of(p)] for p in range(4)]
        imag = [bins[lower, lanes_of(p)] for p in range(4)]
        visit(rows, *spin(real, imag, twist, rows), False)
        return carry

    lax.fori_loop(0, quarter // chunk, body, 0, unroll=4)
    return kept


def put_back(packed, ends):
    quarter = packed.shape[0] // 2
    own = slice(quarter, quarter + 16)
    first = lax.broadcasted_iota(jnp.int32, (16, LANES), 0) == 0
    for p in range(4):
        here = widen(packed[own, lanes_of(p)])
        there = jnp.broadcast_to(ends[p][:1], (16, LANES))
        packed[own, lanes_of(p)] = narrow(jnp.where(first, there, here))


def keep(packed, rows, real, imag, twist, ends):
    re, im = unspin(real, imag, twist, rows)
    if ends:
        return re
    quarter = packed.shape[0] // 2
    lower = pl.ds(pl.multiple_of(rows.start + quarter, 16), rows.size)
    for p in range(4):
        packed[rows, lanes_of(p)] = narrow(re[p])
        packed[lower, lanes_of(p)] = narrow(im[p])
    return None


def sides(rows):
    return jnp.where(left_lanes(rows), 1.0, -1.0)


def filter_spectrum(filters, forward, twist, series, bins, spec_re, spec_im):
    length = filters.shape[2]
    both = filters.shape[0] * filters.shape[1]
    block = length // 4
    pick = pick_quarter(block)
    part = block // 4
    for b in range(4):
        chunk = filters[:, :, b * block : (b + 1) * block].reshape(both, block)
        turned = lax.dot_general(
            pick, chunk, (((1,), (1,)), ((), ())), preferred_element_type=jnp.float32
        )
        for p in range(4):
            series[b * part : (b + 1) * part, lanes_of(p)] = narrow(turned[p * part : (p + 1) * part])
    matmul_rows(forward, series, bins)

    def visit(rows, re, im, ends):
        sign = sides(rows.size)
        for m in range(4):
            spec_re[m, rows, :] = re[m]
            spec_im[m, rows, :] = im[m] * sign

    each_bin(bins, twist, visit)


def first_product(bins, twist, filt_re, filt_im, spec_re, spec_im, packed):
    def visit(rows, re, im, ends):
        out_re, out_im = [], []
        for m in range(4):
            spec_re[m, rows, :] = re[m]
            spec_im[m, rows, :] = im[m]
            fr, fi = filt_re[m, rows, :], filt_im[m, rows, :]
            out_re.append(re[m] * fr - im[m] * fi)
            out_im.append(re[m] * fi + im[m] * fr)
        return keep(packed, rows, out_re, out_im, twist, ends)

    put_back(packed, each_bin(bins, twist, visit))


def second_product(bins, twist, filt_re, filt_im, spec_re, spec_im, packed, lagged):
    def visit(rows, re, im, ends):
        out_re, out_im, lag_re, lag_im = [], [], [], []
        sign = sides(rows.size)
        for m in range(4):
            fr, fi = filt_re[m, rows, :], filt_im[m, rows, :]
            out_re.append(re[m] * fr + im[m] * fi)
            out_im.append(im[m] * fr - re[m] * fi)
            sr, si = spec_re[m, rows, :], spec_im[m, rows, :]
            lag_re.append(re[m] * sr + im[m] * si)
            lag_im.append((im[m] * sr - re[m] * si) * sign)
        conv = keep(packed, rows, out_re, out_im, twist, ends)
        lags = keep(lagged, rows, lag_re, lag_im, twist, ends)
        return (conv, lags)

    conv, lags = each_bin(bins, twist, visit)
    put_back(packed, conv)
    put_back(lagged, lags)


def shifted(value, step):
    rows = value.shape[0]
    row = lax.broadcasted_iota(jnp.int32, value.shape, 0)
    edge = 0 if step == 1 else rows - 1
    return jnp.where(row == edge, 0.0, pltpu.roll(value, step % rows, 0))


def remote(source, target, send_sems, recv_sems, d):
    return pltpu.make_async_remote_copy(
        src_ref=source,
        dst_ref=target,
        send_sem=send_sems.at[d],
        recv_sem=recv_sems.at[d],
        device_id=(lax.axis_index("groups"), lax.axis_index("tm") ^ d),
        device_id_type=pl.DeviceIdType.MESH,
    )


class Exchange:
    def __init__(self, send, got, sems, peers, same=False):
        self.send, self.got, self.sems, self.peers, self.same = send, got, sems, peers, same

    def copies(self):
        me = lax.axis_index("tm")
        for d in range(1, self.peers):
            source = self.send if self.same else self.send.at[me ^ d]
            yield remote(source, self.got.at[me], self.sems.at[0], self.sems.at[1], d)

    def own(self):
        me = lax.axis_index("tm")
        source = self.send if self.same else self.send.at[me]
        return pltpu.make_async_copy(source, self.got.at[me], self.sems.at[0, 0])

    def start(self):
        for copy in self.copies():
            copy.start()
        self.own().start()

    def wait_recv(self):
        self.own().wait()
        for copy in self.copies():
            copy.wait_recv()

    def wait_send(self):
        for copy in self.copies():
            copy.wait_send()


def window_kernel(
    tok_ref, offsets, taps_ref, w_hbm, cot_hbm, table_hbm, filters_hbm, forward_hbm, inverse_hbm, twist_hbm,
    mix_home, home, tap_home, lag_out,
    w_ref, cot_ref, table, filters, forward, inverse, twist,
    tok_own, tok_got, w_send, w_got, cot_send, cot_got, mix_back, back, tap_own, tap_got,
    used, emb, w_own, proj, gates, first_gate, upstream,
    series, bins, filt_re, filt_im, spec_re, spec_im, packed, lagged, wave, grad_b, grad_a, grad_proj, lags_by_channel,
    load_sems, lag_sem, tap_sem, relay_sems, tok_sems, w_sems, cot_sems, mix_sems, out_sems, tap_sems,
):
    peers, _, _ = mix_home.shape
    rows, width = cot_ref.shape
    half = LANES // 2
    quarter = inverse.shape[0]
    block = rows // 4
    fields = tok_ref.shape[0]
    me = lax.axis_index("tm")
    others = range(1, peers)

    loads = [
        pltpu.make_async_copy(source, target, load_sems.at[i])
        for i, (source, target) in enumerate(
            [
                (w_hbm, w_ref), (cot_hbm, cot_ref), (table_hbm, table), (filters_hbm, filters),
                (forward_hbm, forward), (twist_hbm, twist), (inverse_hbm, inverse),
            ]
        )
    ]
    for load in loads:
        load.start()
    barrier = pltpu.get_barrier_semaphore()
    group = lax.axis_index("groups")
    for device in [(group, me ^ d) for d in others] + [(1 - group, me)]:
        pl.semaphore_signal(barrier, inc=1, device_id=device, device_id_type=pl.DeviceIdType.MESH)

    to_tok = Exchange(tok_own, tok_got, tok_sems, peers, same=True)
    to_w = Exchange(w_send.at[group], w_got.at[group], w_sems, peers)
    to_cot = Exchange(cot_send, cot_got, cot_sems, peers)
    to_mix = Exchange(mix_back, mix_home, mix_sems, peers)
    to_out = Exchange(back, home, out_sems, peers)
    core, chip = me % 2, me // 2
    to_tap = [
        remote(tap_own, tap_got.at[core, chip], tap_sems.at[0], tap_sems.at[1], d) for d in range(2, peers, 2)
    ]
    tap_pair = remote(tap_got.at[core], tap_got.at[core], tap_sems.at[0], tap_sems.at[1], 1)

    pick = pick_quarter(rows)
    tok_own[...] = lax.dot_general(
        narrow(tok_ref[...].astype(jnp.float32)), pick, (((1,), (1,)), ((), ())), preferred_element_type=jnp.float32
    )

    def fill(send, q, pairs):
        for side in range(2):
            mine = slice(side * half, (side + 1) * half)
            send[q + side] = jnp.concatenate(
                [jnp.concatenate([a[:, mine], b[:, mine]], axis=1) for a, b in pairs], axis=0
            )

    loads[0].wait()
    for q in range(0, peers, 2):
        value, gate1, gate2 = [w_ref[:, j * width + q * half : j * width + (q + 2) * half] for j in range(3)]
        for part in range(2):
            low, mid, high = part * half // 2, part * half // 2 + half // 4, (part + 1) * half // 2
            fill(w_send.at[part], q, [(value[low:high], gate2[low:high]), (gate1[low:mid], gate1[mid:high])])
    pl.semaphore_wait(barrier, peers)
    to_tok.start()
    to_w.start()
    loads[1].wait()
    turned = narrow(dot(pick, cot_ref[...]))
    for q in range(0, peers, 2):
        steps = [turned[p * block : (p + 1) * block, q * half : (q + 2) * half] for p in range(4)]
        fill(cot_send, q, [(steps[0], steps[1]), (steps[2], steps[3])])
    to_cot.start()

    loads[2].wait()
    col = lax.broadcasted_iota(jnp.int32, (CODES, table.shape[0]), 1)
    col = col - lax.broadcasted_iota(jnp.int32, (CODES, table.shape[0]), 0)
    count = 4
    for field in range(0, fields, count):
        chosen = [narrow(jnp.where(col == offsets[field + s], 1.0, 0.0)) for s in range(count)]
        found = dot(jnp.concatenate(chosen, axis=0), table[...])
        used[field * CODES : (field + count) * CODES, :] = narrow(found)
    for load in loads[3:6]:
        load.wait()
    filter_spectrum(filters, forward, twist, series, bins, filt_re, filt_im)

    to_tok.wait_recv()
    lanes = lax.broadcasted_iota(jnp.int32, (rows, CODES), 1).astype(jnp.float32)

    def embed(i, carry):
        hot = []
        for s in range(2):
            steps = tok_got[2 * i + s].T
            hot.append(
                jnp.concatenate(
                    [
                        narrow(jnp.where(steps[:, field : field + 1] == lanes, 1.0, 0.0))
                        for field in range(fields)
                    ],
                    axis=1,
                )
            )
        summed = dot(jnp.concatenate(hot, axis=0), used[...])
        rounded = narrow(summed)
        for s in range(2):
            for p in range(4):
                start = s * rows + p * block
                emb[p, 2 * i + s] = rounded[start : start + block]
        return carry

    ahead_of_w = 2
    lax.fori_loop(0, ahead_of_w, embed, 0, unroll=2)
    to_w.wait_recv()
    relay = pltpu.make_async_remote_copy(
        src_ref=w_got.at[group],
        dst_ref=w_got.at[group],
        send_sem=relay_sems.at[0],
        recv_sem=relay_sems.at[1],
        device_id=(1 - group, me),
        device_id_type=pl.DeviceIdType.MESH,
    )
    relay.start()
    lax.fori_loop(ahead_of_w, peers // 2, embed, 0, unroll=2)
    loads[6].wait()

    relay.wait_recv()
    near = left_lanes(half // 4)
    for peer in range(peers):
        for part in range(2):
            start = peer * half + part * half // 2
            own = slice(start, start + half // 2)
            w_own[own, :LANES] = w_got[part, peer, : half // 2]
            gate = widen(w_got[part, peer, half // 2 :])
            other = swap(gate)
            both = jnp.concatenate([jnp.where(near, gate, other), jnp.where(near, other, gate)], axis=0)
            w_own[own, LANES:] = narrow(both)
    place = pl.multiple_of(me // 2 * LANES, LANES)
    odd = me % 2 == 1
    near3 = left_lanes(3)
    own_taps = []
    for j in range(3):
        piece = taps_ref[:, pl.ds(pl.multiple_of(place + j * width, LANES), LANES)]
        own_taps.append(jnp.where(odd, swap(piece), piece))
    taps = jnp.concatenate(
        [jnp.where(near3, own_taps[0], swap(own_taps[2])), jnp.where(near3, own_taps[1], swap(own_taps[1]))], axis=1
    )
    tap = [taps[j : j + 1] for j in range(3)]

    for p in range(4):
        proj[p] = widen(narrow(dot(emb[p].reshape(quarter, width), w_own[...])))

    def back_by(p, steps):
        return proj[p - steps] if p >= steps else shifted(proj[p - steps + 4], 1)

    for p in range(4):
        mixed = widen(narrow(tap[0] * proj[p] + tap[1] * back_by(p, 1) + tap[2] * back_by(p, 2)))
        gates[p] = mixed[:, :LANES]
        first_gate[p] = mixed[:, LANES:]
    to_cot.wait_recv()
    left = left_lanes(quarter)
    for p in range(0, 4, 2):
        steps = widen(cot_got[:, p // 2 * block : (p // 2 + 1) * block, :].reshape(quarter, LANES))
        upstream[p] = jnp.where(left, 1.0, swap(steps))
        upstream[p + 1] = jnp.where(left, 1.0, steps)
    for p in range(4):
        series[:, lanes_of(p)] = narrow(gates[p] * upstream[p])

    matmul_rows(forward, series, bins)
    first_product(bins, twist, filt_re, filt_im, spec_re, spec_im, packed)
    matmul_rows(inverse, packed, wave)
    for p in range(4):
        out = widen(narrow(wave[:, lanes_of(p)]))
        flipped = swap(out)
        series[:, lanes_of(p)] = narrow(flipped * first_gate[p])
        grad_b[p] = widen(narrow(out * flipped))

    matmul_rows(forward, series, bins)
    second_product(bins, twist, filt_re, filt_im, spec_re, spec_im, packed, lagged)
    matmul_rows(inverse, packed, wave)
    mixed = []
    for p in range(4):
        out = widen(narrow(wave[:, lanes_of(p)]))
        mixed.append(gates[p] * out)
        grad_a[p] = widen(narrow(upstream[p] * out))
    for p in range(0, 4, 2):
        start = p // 2 * block
        both = narrow(jnp.where(left, swap(mixed[p]), mixed[p + 1]))
        mix_back[:, start : start + block, :] = both.reshape(peers, block, LANES)
    to_mix.start()

    def ahead(grad, p, steps):
        return grad[p + steps] if p + steps < 4 else shifted(grad[p + steps - 4], -1)

    sums = []
    for grad, own in ((grad_a, slice(0, LANES)), (grad_b, slice(LANES, 2 * LANES))):
        total = [jnp.zeros((1, LANES), jnp.float32)] * 3
        for p in range(4):
            here = grad[p]
            out = tap[0][:, own] * here + tap[1][:, own] * ahead(grad, p, 1) + tap[2][:, own] * ahead(grad, p, 2)
            grad_proj[own, p * quarter : (p + 1) * quarter] = narrow(out.T)
            for j in range(3):
                lag = proj[p - j, :, own] if p >= j else shifted(proj[p - j + 4, :, own], 1)
                total[j] = total[j] + jnp.sum(here * lag, axis=0, keepdims=True)
        sums += total
    tap_own[...] = jnp.concatenate(sums + [jnp.zeros((2, LANES), jnp.float32)], axis=0)
    tap_got[core, chip] = tap_own[...]
    for copy in to_tap:
        copy.start()

    near = left_lanes(half // 2)
    count = 4
    sends = list(to_out.copies())
    for step in (1, 2, 3, 0):
        first = (me // count ^ step) * count
        own = pl.ds(pl.multiple_of(first * half, count * half), count * half)
        steps = emb[:, :, :, own].reshape(peers * rows, count * half)
        terms = dot(grad_proj[...], steps).T
        for s in range(count):
            here = terms[s * half : (s + 1) * half]
            back[first + s, :half, :] = narrow(here[:, :LANES])
            twin = here[:, LANES:]
            back[first + s, half:, :] = narrow(jnp.where(near, twin[: half // 2], twin[half // 2 :]))
        for d in range(max(1, step * count), (step + 1) * count):
            sends[d - 1].start()
    to_out.own().start()

    matmul_rows(inverse, lagged, wave)
    part = quarter // 4
    order = pick_quarter(quarter)
    for b in range(4):
        lags = jnp.concatenate(
            [wave[b * part : (b + 1) * part, lanes_of(p)].T for p in range(4)], axis=1
        )
        high = narrow(lags)
        rest = narrow(lags - widen(high))
        out = dot(high, order) + dot(rest, order)
        span = slice(b * quarter, (b + 1) * quarter)
        lags_by_channel[0, :, span] = out[:half]
        lags_by_channel[1, :, span] = out[half:]
    leave = pltpu.make_async_copy(lags_by_channel, lag_out, lag_sem)
    leave.start()

    for copy in to_tap:
        copy.wait_recv()
    tap_pair.start()
    tap_pair.wait_recv()
    tap_leave = pltpu.make_async_copy(tap_got, tap_home, tap_sem)
    tap_leave.start()
    for exchange in (to_mix, to_out):
        exchange.wait_recv()
    for exchange in (to_tok, to_w, to_cot, to_mix, to_out):
        exchange.wait_send()
    for copy in to_tap + [tap_pair]:
        copy.wait_send()
    tap_leave.wait()
    relay.wait_send()
    leave.wait()


def unpack_kernel(
    mix_hbm, hbm, tap_hbm, lags, mixer_out, weight_out, tap_out, filter_out, mix_home, home, tap_home, sems
):
    peers, block, _ = mix_home.shape
    block = block // 2
    half = LANES // 2
    width = peers * half
    loads = [
        pltpu.make_async_copy(source, target, sems.at[i])
        for i, (source, target) in enumerate(
            [(mix_hbm, mix_home), (tap_hbm, tap_home), (hbm, home), (lags, filter_out)]
        )
    ]
    for load in loads:
        load.start()
    loads[0].wait()
    columns = []
    for q in range(0, peers, 2):
        one, two = mix_home[q], mix_home[q + 1]
        pieces = []
        for p in range(4):
            at = slice(p // 2 * block, (p // 2 + 1) * block)
            mine = slice(p % 2 * half, (p % 2 + 1) * half)
            pieces.append(jnp.concatenate([one[at, mine], two[at, mine]], axis=1))
        columns.append(jnp.concatenate(pieces, axis=0))
    mixer_out[...] = narrow(
        lax.dot_general(
            pick_quarter(4 * block),
            jnp.concatenate(columns, axis=1),
            (((0,), (0,)), ((), ())),
            preferred_element_type=jnp.float32,
        )
    )
    loads[1].wait()
    loads[2].wait()
    for q in range(0, peers, 2):
        start = q * half
        one, two = tap_home[0, q // 2], tap_home[1, q // 2]
        for j, (row, side) in enumerate(((0, 0), (3, 0), (0, 1))):
            mine = slice(side * half, (side + 1) * half)
            tap_out[:, j * width + start : j * width + start + LANES] = jnp.concatenate(
                [one[row : row + 3, mine], two[row : row + 3, mine]], axis=1
            )
        one, two = home[q], home[q + 1]
        for side in range(2):
            mine = slice(side * half, (side + 1) * half)
            column = 2 * side * width + start
            weight_out[:, column : column + LANES] = widen(
                jnp.concatenate([one[:half, mine], two[:half, mine]], axis=1)
            )
            at = slice(side * half // 2, (side + 1) * half // 2)
            weight_out[at, width + start : width + start + LANES] = widen(
                jnp.concatenate([one[half:, mine], two[half:, mine]], axis=1)
            )
    loads[3].wait()


def fast_local(token_ids, field_offsets, embed_table, w_in, short_taps, filters, cotangent):
    rows, width = cotangent.shape
    fields = token_ids.shape[1]
    peers = lax.axis_size("tm")
    length = rows * peers
    quarter = length // 4
    forward, inverse, twist = basis(quarter)
    whole = pl.BlockSpec(memory_space=pltpu.VMEM)
    anywhere = pl.BlockSpec(memory_space=pl.ANY)
    f32, bf16 = jnp.float32, jnp.bfloat16
    half = LANES // 2
    sems = pltpu.SemaphoreType.DMA((2, peers))
    wide = 4 * LANES
    scratch = [
        pltpu.VMEM(w_in.shape, bf16),
        pltpu.VMEM(cotangent.shape, bf16),
        pltpu.VMEM(embed_table.shape, bf16),
        pltpu.VMEM(filters.shape, bf16),
        pltpu.VMEM(forward.shape, bf16),
        pltpu.VMEM(inverse.shape, bf16),
        pltpu.VMEM(twist.shape, f32),
        pltpu.VMEM((fields, rows), f32),
        pltpu.VMEM((peers, fields, rows), f32),
        pltpu.VMEM((2, peers, half // 2 + half // 4, LANES), bf16),
        pltpu.VMEM((2, peers, half // 2 + half // 4, LANES), bf16),
        pltpu.VMEM((peers, rows // 2, LANES), bf16),
        pltpu.VMEM((peers, rows // 2, LANES), bf16),
        pltpu.VMEM((peers, rows // 2, LANES), bf16),
        pltpu.VMEM((peers, half + half // 2, LANES), bf16),
        pltpu.VMEM((8, LANES), f32),
        pltpu.VMEM((2, peers // 2, 8, LANES), f32),
        pltpu.VMEM((fields * CODES, width), bf16),
        pltpu.VMEM((4, peers, rows // 4, width), bf16),
        pltpu.VMEM((width, 2 * LANES), bf16),
        pltpu.VMEM((4, quarter, 2 * LANES), f32),
        pltpu.VMEM((4, quarter, LANES), f32),
        pltpu.VMEM((4, quarter, LANES), f32),
        pltpu.VMEM((4, quarter, LANES), f32),
        pltpu.VMEM((quarter, wide), bf16),
        pltpu.VMEM((2 * quarter, wide), f32),
        pltpu.VMEM((4, quarter + 8, LANES), f32),
        pltpu.VMEM((4, quarter + 8, LANES), f32),
        pltpu.VMEM((4, quarter + 8, LANES), f32),
        pltpu.VMEM((4, quarter + 8, LANES), f32),
        pltpu.VMEM((2 * quarter, wide), bf16),
        pltpu.VMEM((2 * quarter, wide), bf16),
        pltpu.VMEM((quarter, wide), f32),
        pltpu.VMEM((4, quarter, LANES), f32),
        pltpu.VMEM((4, quarter, LANES), f32),
        pltpu.VMEM((2 * LANES, length), bf16),
        pltpu.VMEM(filters.shape, f32),
        pltpu.SemaphoreType.DMA((7,)),
        pltpu.SemaphoreType.DMA,
        pltpu.SemaphoreType.DMA,
        pltpu.SemaphoreType.DMA((2,)),
    ] + [sems] * 6
    homes = pl.pallas_call(
        window_kernel,
        out_shape=(
            jax.ShapeDtypeStruct((peers, rows // 2, LANES), bf16),
            jax.ShapeDtypeStruct((peers, half + half // 2, LANES), bf16),
            jax.ShapeDtypeStruct((2, peers // 2, 8, LANES), f32),
            jax.ShapeDtypeStruct(filters.shape, f32),
        ),
        in_specs=[whole, pl.BlockSpec(memory_space=pltpu.SMEM), whole] + [anywhere] * 7,
        out_specs=(anywhere,) * 4,
        scratch_shapes=scratch,
        compiler_params=pltpu.CompilerParams(
            vmem_limit_bytes=VMEM, collective_id=0, has_side_effects=True
        ),
        name="window",
    )(
        token_ids.T,
        field_offsets,
        short_taps,
        w_in,
        cotangent,
        embed_table,
        filters,
        jnp.asarray(forward),
        jnp.asarray(inverse),
        jnp.asarray(twist),
    )
    return tuple(
        pl.pallas_call(
            unpack_kernel,
            out_shape=(
                jax.ShapeDtypeStruct((rows, width), bf16),
                jax.ShapeDtypeStruct((half, 3 * width), f32),
                jax.ShapeDtypeStruct((3, 3 * width), f32),
                jax.ShapeDtypeStruct(filters.shape, f32),
            ),
            in_specs=[anywhere] * 4,
            out_specs=(whole,) * 4,
            scratch_shapes=[pltpu.VMEM(home.shape, home.dtype) for home in homes[:3]]
            + [pltpu.SemaphoreType.DMA((4,))],
            compiler_params=pltpu.CompilerParams(vmem_limit_bytes=VMEM),
            name="unpack",
        )(*homes)
    )


def cis_tables(count_a, count_b, modulus):
    left = jnp.arange(count_a, dtype=jnp.int32)[:, None]
    right = jnp.arange(count_b, dtype=jnp.int32)[None, :]
    angle = 2.0 * math.pi / modulus * (left * right % modulus).astype(jnp.float32)
    return (jnp.cos(angle), jnp.sin(angle))


class Factored:
    def __init__(self, total):
        bits = total.bit_length() - 1
        first_len = 1 << (bits + 1) // 2
        second_len = total // first_len
        first_cos, first_sin = cis_tables(first_len, first_len // 2, first_len)
        second_cos, second_sin = cis_tables(second_len, second_len, second_len)
        self.total = total
        self.second_len = second_len
        self.twist_cos, self.twist_sin = cis_tables(first_len, second_len, total)
        self.first_both = jnp.concatenate([first_cos, -first_sin], axis=0)
        self.forward = jnp.block([[second_cos, -second_sin], [second_sin, second_cos]])
        self.inverse = jnp.block([[second_cos, second_sin], [-second_sin, second_cos]])

    def spectrum(self, series):
        series = widen(series)
        channels, length = series.shape
        rows_k = self.twist_cos.shape[0]
        half = self.first_both.shape[1]
        blocks = series.reshape(channels, half, length // half)
        part = jnp.einsum("ka,cab->ckb", self.first_both, blocks)
        part_re = part[:, :rows_k]
        part_im = part[:, rows_k:]
        turn_re = part_re * self.twist_cos + part_im * self.twist_sin
        turn_im = part_im * self.twist_cos - part_re * self.twist_sin
        turned = jnp.concatenate([turn_re, turn_im], axis=2)
        result = jnp.einsum("ckb,bm->ckm", turned, self.forward)
        return (result[:, :, : self.second_len], result[:, :, self.second_len :])

    def product(self, left, right, conjugate):
        left_re, left_im = left
        right_re, right_im = right
        if conjugate:
            right_im = -right_im
        return (left_re * right_re - left_im * right_im, left_re * right_im + left_im * right_re)

    def signal(self, pair):
        joined = jnp.concatenate(pair, axis=2)
        back = jnp.einsum("ckm,mb->ckb", joined, self.inverse)
        back_re = back[:, :, : self.second_len]
        back_im = back[:, :, self.second_len :]
        turn_re = back_re * self.twist_cos - back_im * self.twist_sin
        turn_im = back_im * self.twist_cos + back_re * self.twist_sin
        turned = jnp.concatenate([turn_re, turn_im], axis=1)
        blocks = jnp.einsum("ka,ckb->cab", self.first_both, turned)
        return blocks.reshape(joined.shape[0], -1) * (1.0 / self.total)


def delayed(array, steps):
    length = array.shape[1]
    return jnp.pad(array, ((0, 0), (steps, 0)))[:, :length]


def advanced(array, steps):
    return jnp.pad(array, ((0, 0), (0, steps)))[:, steps:]


def wide_local(token_ids, field_offsets, embed_table, w_in, short_taps, filters, cotangent):
    rows, width = cotangent.shape
    fields = token_ids.shape[1]
    peers = lax.axis_size("tm")
    me = lax.axis_index("tm")
    chans = width // peers
    length = rows * peers
    vocab = embed_table.shape[0]

    w_part = w_in.reshape(chans, 3, peers, chans).transpose(2, 0, 1, 3).reshape(peers, chans, 3 * chans)
    cot_part = cotangent.reshape(rows, peers, chans).transpose(1, 2, 0)
    tok_part = narrow(token_ids).T.reshape(1, chans, -1)
    tok_part = jnp.broadcast_to(tok_part, (peers,) + tok_part.shape[1:])
    sent = jnp.concatenate([w_part, cot_part, tok_part], axis=2)
    got = lax.all_to_all(sent, "tm", split_axis=0, concat_axis=0, tiled=True)
    w_own = got[:, :, : 3 * chans].reshape(width, 3 * chans)
    upstream = widen(got[:, :, 3 * chans : 3 * chans + rows].transpose(1, 0, 2).reshape(chans, length))
    tokens = got[:, :, 3 * chans + rows :].reshape(peers, fields, rows)
    tokens = tokens.transpose(1, 0, 2).reshape(fields, length).astype(jnp.int32)
    row_index = tokens + field_offsets[:, None]

    codes = lax.broadcasted_iota(jnp.int32, (vocab, length), 0)
    counts = jnp.zeros((vocab, length), jnp.float32)
    for field in range(fields):
        counts = counts + jnp.where(codes == row_index[field][None, :], 1.0, 0.0)
    embedded = narrow(
        jnp.einsum("vr,vt->rt", embed_table, narrow(counts), preferred_element_type=jnp.float32)
    )
    proj = narrow(jnp.einsum("rc,rt->ct", w_own, embedded, preferred_element_type=jnp.float32))
    taps = lax.dynamic_index_in_dim(short_taps.reshape(3, 3, peers, chans), me, 2, keepdims=False)
    taps = taps.reshape(3, 3 * chans, 1)
    proj_wide = widen(proj)
    lags = (proj_wide, delayed(proj_wide, 1), delayed(proj_wide, 2))
    mixed = narrow(taps[0] * lags[0] + taps[1] * lags[1] + taps[2] * lags[2])
    values = mixed[:chans]
    first_gate = widen(mixed[chans : 2 * chans])
    second_gate = widen(mixed[2 * chans :])

    transform = Factored(2 * length)

    def spectra(*series):
        whole = transform.spectrum(jnp.concatenate(series, axis=0))
        return [
            tuple(part[i * chans : (i + 1) * chans] for part in whole) for i in range(len(series))
        ]

    def signals(*pairs):
        whole = transform.signal(tuple(jnp.concatenate(parts, axis=0) for parts in zip(*pairs)))
        return [whole[i * chans : (i + 1) * chans] for i in range(len(pairs))]

    grad_conv2 = narrow(upstream * second_gate)
    first_spec, second_spec, value_spec, grad_spec2 = spectra(
        filters[0], filters[1], values, grad_conv2
    )
    first_conv, grad_mix = signals(
        transform.product(value_spec, first_spec, False),
        transform.product(grad_spec2, second_spec, True),
    )
    first_conv = widen(narrow(first_conv))
    grad_mix = widen(narrow(grad_mix))
    first_mix = narrow(first_gate * first_conv)
    grad_gate1 = narrow(grad_mix * first_conv)
    grad_conv1 = narrow(grad_mix * first_gate)
    mix_spec, grad_spec1 = spectra(first_mix, grad_conv1)
    second_conv, grad_values, filter_one, filter_two = signals(
        transform.product(mix_spec, second_spec, False),
        transform.product(grad_spec1, first_spec, True),
        transform.product(grad_spec1, value_spec, True),
        transform.product(grad_spec2, mix_spec, True),
    )
    second_conv = widen(narrow(second_conv))
    mixer_out = narrow(second_gate * second_conv)
    grad_gate2 = narrow(upstream * second_conv)
    filter_grads = jnp.stack([filter_one, filter_two], axis=0)
    grad_mixed = jnp.concatenate([narrow(grad_values), grad_gate1, grad_gate2], axis=0)
    grad_wide = widen(grad_mixed)
    grad_proj = narrow(
        taps[0] * grad_wide + taps[1] * advanced(grad_wide, 1) + taps[2] * advanced(grad_wide, 2)
    )
    tap_terms = jnp.stack([jnp.sum(grad_wide * lag, axis=1) for lag in lags], axis=0)
    weight_terms = narrow(
        jnp.einsum("rt,ct->rc", embedded, grad_proj, preferred_element_type=jnp.float32)
    )

    weight_part = weight_terms.reshape(peers, chans, 3 * chans)
    mixer_part = mixer_out.reshape(chans, peers, rows).transpose(1, 0, 2)
    tap_part = narrow(tap_terms).reshape(1, chans, -1)
    tap_part = jnp.broadcast_to(tap_part, (peers,) + tap_part.shape[1:])
    back = lax.all_to_all(
        jnp.concatenate([weight_part, mixer_part, tap_part], axis=2),
        "tm",
        split_axis=0,
        concat_axis=0,
        tiled=True,
    )
    weight_grads = widen(
        back[:, :, : 3 * chans].reshape(peers, chans, 3, chans).transpose(1, 2, 0, 3)
    ).reshape(chans, 3 * width)
    mixer_rows = back[:, :, 3 * chans : 3 * chans + rows].reshape(width, rows).T
    tap_grads = widen(
        back[:, :, 3 * chans + rows :].reshape(peers, 3, 3, chans).transpose(1, 2, 0, 3)
    ).reshape(3, 3 * width)
    return (mixer_rows, weight_grads, tap_grads, filter_grads)


def solution(mesh):
    return jax.shard_map(
        local,
        mesh=mesh,
        in_specs=(
            P(("groups", "tm"), None),
            P("groups"),
            P(),
            P("tm", None),
            P(),
            P(None, "tm", None),
            P(("groups", "tm"), None),
        ),
        out_specs=(
            P(("groups", "tm"), None),
            P(("groups", "tm"), None),
            P("groups", None),
            P("groups", "tm", None),
        ),
        check_vma=False,
    )
```

```python
import math

import jax
import jax.numpy as jnp
import ml_dtypes
import numpy as np
from jax import lax
from jax.experimental import pallas as pl
from jax.experimental.pallas import tpu as pltpu
from jax.sharding import PartitionSpec as P

DENSE_LIMIT = 4096
CODES = 128
LANES = 128
VMEM = 56 << 20


def widen(array):
    return array.astype(jnp.float32)


def narrow(array):
    return array.astype(jnp.bfloat16)


def local(token_ids, field_offsets, embed_table, w_in, short_taps, filters, cotangent):
    peers = lax.axis_size("tm")
    rows, width = cotangent.shape
    dense = 2 * rows * peers <= DENSE_LIMIT
    fits = width == peers * LANES // 2 and rows == LANES and peers & (peers - 1) == 0
    pair = lax.axis_size("groups") == 2 and token_ids.shape[1] == 8
    plan = fast_local if dense and fits and pair else wide_local
    return plan(token_ids, field_offsets, embed_table, w_in, short_taps, filters, cotangent)


def basis(quarter):
    total = 8 * quarter
    k = np.arange(quarter)
    angle = np.outer(k, k) % (2 * quarter) * (np.pi / quarter)
    cos, sin = np.cos(angle), -np.sin(angle)
    forward = np.concatenate([cos, sin], axis=0)
    forward[quarter] = 1.0 - 2.0 * (k % 2)
    inverse = forward.T * (2.0 / total)
    inverse[:, 0] *= 0.5
    inverse[:, quarter] *= 0.5
    turn = np.arange(quarter + 8)
    turn[quarter:] = quarter
    twist = []
    for step in (1, 2, 3):
        twist += [np.cos(turn * step * (2 * np.pi / total)), np.sin(turn * step * (2 * np.pi / total))]
    twist = np.broadcast_to(np.stack(twist)[:, :, None], (6, quarter + 8, LANES))
    bf16 = ml_dtypes.bfloat16
    return (forward.astype(bf16), inverse.astype(bf16), twist.astype(np.float32))


def dot(left, right):
    return jnp.dot(left, right, preferred_element_type=jnp.float32)


def swap(value):
    return pltpu.roll(value, LANES // 2, 1)


def left_lanes(rows):
    return lax.broadcasted_iota(jnp.int32, (rows, LANES), 1) < LANES // 2


def pick_quarter(count):
    row = lax.broadcasted_iota(jnp.int32, (count, count), 0)
    col = lax.broadcasted_iota(jnp.int32, (count, count), 1)
    block = count // 4
    return narrow(jnp.where(col == 4 * (row % block) + row // block, 1.0, 0.0))


def spin(real, imag, twist, rows):
    re, im = [real[0]], [imag[0]]
    for p in (1, 2, 3):
        cos, sin = twist[2 * p - 2, rows, :], twist[2 * p - 1, rows, :]
        re.append(real[p] * cos + imag[p] * sin)
        im.append(imag[p] * cos - real[p] * sin)
    er, ei, fr, fi = re[0] + re[2], im[0] + im[2], re[0] - re[2], im[0] - im[2]
    gr, gi, hr, hi = re[1] + re[3], im[1] + im[3], re[1] - re[3], im[1] - im[3]
    return [er + gr, fr + hi, er - gr, fr - hi], [ei + gi, fi - hr, ei - gi, fi + hr]


def unspin(real, imag, twist, rows):
    er, ei, fr, fi = real[0] + real[2], imag[0] + imag[2], real[0] - real[2], imag[0] - imag[2]
    gr, gi, hr, hi = real[1] + real[3], imag[1] + imag[3], real[1] - real[3], imag[1] - imag[3]
    re, im = [er + gr, fr - hi, er - gr, fr + hi], [ei + gi, fi + hr, ei - gi, fi - hr]
    for p in (1, 2, 3):
        cos, sin = twist[2 * p - 2, rows, :], twist[2 * p - 1, rows, :]
        re[p], im[p] = re[p] * cos - im[p] * sin, im[p] * cos + re[p] * sin
    return re, im


def matmul_rows(left, right, out):
    rows = left.shape[0]
    chunk = min(256, rows)

    def body(step, carry):
        own = pl.ds(pl.multiple_of(step * chunk, chunk), chunk)
        out[own, :] = dot(left[own, :], right[...])
        return carry

    lax.fori_loop(0, rows // chunk, body, 0, unroll=True)


def lanes_of(p):
    return slice(p * LANES, (p + 1) * LANES)


def each_bin(bins, twist, visit):
    quarter = bins.shape[0] // 2
    last = pl.ds(quarter, 8)
    zero = jnp.zeros((8, LANES), jnp.float32)
    nyquist = [jnp.broadcast_to(bins[quarter : quarter + 1, lanes_of(p)], (8, LANES)) for p in range(4)]
    kept = visit(last, *spin(nyquist, [zero] * 4, twist, last), True)
    bins[quarter : quarter + 1, :] = jnp.zeros((1, bins.shape[1]), jnp.float32)
    chunk = 32

    def body(step, carry):
        start = pl.multiple_of(step * chunk, chunk)
        rows = pl.ds(start, chunk)
        lower = pl.ds(pl.multiple_of(quarter + start, chunk), chunk)
        real = [bins[rows, lanes_of(p)] for p in range(4)]
        imag = [bins[lower, lanes_of(p)] for p in range(4)]
        visit(rows, *spin(real, imag, twist, rows), False)
        return carry

    lax.fori_loop(0, quarter // chunk, body, 0, unroll=4)
    return kept


def put_back(packed, ends):
    quarter = packed.shape[0] // 2
    own = slice(quarter, quarter + 16)
    first = lax.broadcasted_iota(jnp.int32, (16, LANES), 0) == 0
    for p in range(4):
        here = widen(packed[own, lanes_of(p)])
        there = jnp.broadcast_to(ends[p][:1], (16, LANES))
        packed[own, lanes_of(p)] = narrow(jnp.where(first, there, here))


def keep(packed, rows, real, imag, twist, ends):
    re, im = unspin(real, imag, twist, rows)
    if ends:
        return re
    quarter = packed.shape[0] // 2
    lower = pl.ds(pl.multiple_of(rows.start + quarter, 16), rows.size)
    for p in range(4):
        packed[rows, lanes_of(p)] = narrow(re[p])
        packed[lower, lanes_of(p)] = narrow(im[p])
    return None


def sides(rows):
    return jnp.where(left_lanes(rows), 1.0, -1.0)


def filter_spectrum(filters, forward, twist, series, bins, spec_re, spec_im):
    length = filters.shape[2]
    both = filters.shape[0] * filters.shape[1]
    block = length // 4
    pick = pick_quarter(block)
    part = block // 4
    for b in range(4):
        chunk = filters[:, :, b * block : (b + 1) * block].reshape(both, block)
        turned = lax.dot_general(
            pick, chunk, (((1,), (1,)), ((), ())), preferred_element_type=jnp.float32
        )
        for p in range(4):
            series[b * part : (b + 1) * part, lanes_of(p)] = narrow(turned[p * part : (p + 1) * part])
    matmul_rows(forward, series, bins)

    def visit(rows, re, im, ends):
        sign = sides(rows.size)
        for m in range(4):
            spec_re[m, rows, :] = re[m]
            spec_im[m, rows, :] = im[m] * sign

    each_bin(bins, twist, visit)


def first_product(bins, twist, filt_re, filt_im, spec_re, spec_im, packed):
    def visit(rows, re, im, ends):
        out_re, out_im = [], []
        for m in range(4):
            spec_re[m, rows, :] = re[m]
            spec_im[m, rows, :] = im[m]
            fr, fi = filt_re[m, rows, :], filt_im[m, rows, :]
            out_re.append(re[m] * fr - im[m] * fi)
            out_im.append(re[m] * fi + im[m] * fr)
        return keep(packed, rows, out_re, out_im, twist, ends)

    put_back(packed, each_bin(bins, twist, visit))


def second_product(bins, twist, filt_re, filt_im, spec_re, spec_im, packed, lagged):
    def visit(rows, re, im, ends):
        out_re, out_im, lag_re, lag_im = [], [], [], []
        sign = sides(rows.size)
        for m in range(4):
            fr, fi = filt_re[m, rows, :], filt_im[m, rows, :]
            out_re.append(re[m] * fr + im[m] * fi)
            out_im.append(im[m] * fr - re[m] * fi)
            sr, si = spec_re[m, rows, :], spec_im[m, rows, :]
            lag_re.append(re[m] * sr + im[m] * si)
            lag_im.append((im[m] * sr - re[m] * si) * sign)
        conv = keep(packed, rows, out_re, out_im, twist, ends)
        lags = keep(lagged, rows, lag_re, lag_im, twist, ends)
        return (conv, lags)

    conv, lags = each_bin(bins, twist, visit)
    put_back(packed, conv)
    put_back(lagged, lags)


def shifted(value, step):
    rows = value.shape[0]
    row = lax.broadcasted_iota(jnp.int32, value.shape, 0)
    edge = 0 if step == 1 else rows - 1
    return jnp.where(row == edge, 0.0, pltpu.roll(value, step % rows, 0))


def remote(source, target, send_sems, recv_sems, d):
    return pltpu.make_async_remote_copy(
        src_ref=source,
        dst_ref=target,
        send_sem=send_sems.at[d],
        recv_sem=recv_sems.at[d],
        device_id=(lax.axis_index("groups"), lax.axis_index("tm") ^ d),
        device_id_type=pl.DeviceIdType.MESH,
    )


class Exchange:
    def __init__(self, send, got, sems, peers, same=False):
        self.send, self.got, self.sems, self.peers, self.same = send, got, sems, peers, same

    def copies(self):
        me = lax.axis_index("tm")
        for d in range(1, self.peers):
            source = self.send if self.same else self.send.at[me ^ d]
            yield remote(source, self.got.at[me], self.sems.at[0], self.sems.at[1], d)

    def own(self):
        me = lax.axis_index("tm")
        source = self.send if self.same else self.send.at[me]
        return pltpu.make_async_copy(source, self.got.at[me], self.sems.at[0, 0])

    def start(self):
        for copy in self.copies():
            copy.start()
        self.own().start()

    def wait_recv(self):
        self.own().wait()
        for copy in self.copies():
            copy.wait_recv()

    def wait_send(self):
        for copy in self.copies():
            copy.wait_send()


def window_kernel(
    tok_ref, offsets, taps_ref, w_hbm, cot_hbm, table_hbm, filters_hbm, forward_hbm, inverse_hbm, twist_hbm,
    mix_home, home, tap_home, lag_out,
    w_ref, cot_ref, table, filters, forward, inverse, twist,
    tok_own, tok_got, w_send, w_got, cot_send, cot_got, mix_back, back, tap_own, tap_got,
    used, emb, w_own, proj, gates, first_gate, upstream,
    series, bins, filt_re, filt_im, spec_re, spec_im, packed, lagged, wave, grad_b, grad_a, grad_proj, lags_by_channel,
    load_sems, lag_sem, tap_sem, relay_sems, tok_sems, w_sems, cot_sems, mix_sems, out_sems, tap_sems,
):
    peers, _, _ = mix_home.shape
    rows, width = cot_ref.shape
    half = LANES // 2
    quarter = inverse.shape[0]
    block = rows // 4
    fields = tok_ref.shape[0]
    me = lax.axis_index("tm")
    others = range(1, peers)

    loads = [
        pltpu.make_async_copy(source, target, load_sems.at[i])
        for i, (source, target) in enumerate(
            [
                (w_hbm, w_ref), (cot_hbm, cot_ref), (table_hbm, table), (filters_hbm, filters),
                (forward_hbm, forward), (twist_hbm, twist), (inverse_hbm, inverse),
            ]
        )
    ]
    for load in loads:
        load.start()
    barrier = pltpu.get_barrier_semaphore()
    group = lax.axis_index("groups")
    for device in [(group, me ^ d) for d in others] + [(1 - group, me)]:
        pl.semaphore_signal(barrier, inc=1, device_id=device, device_id_type=pl.DeviceIdType.MESH)

    to_tok = Exchange(tok_own, tok_got, tok_sems, peers, same=True)
    to_w = Exchange(w_send.at[group], w_got.at[group], w_sems, peers)
    to_cot = Exchange(cot_send, cot_got, cot_sems, peers)
    to_mix = Exchange(mix_back, mix_home, mix_sems, peers)
    to_out = Exchange(back, home, out_sems, peers)
    core, chip = me % 2, me // 2
    to_tap = [
        remote(tap_own, tap_got.at[core, chip], tap_sems.at[0], tap_sems.at[1], d) for d in range(2, peers, 2)
    ]
    tap_pair = remote(tap_got.at[core], tap_got.at[core], tap_sems.at[0], tap_sems.at[1], 1)

    pick = pick_quarter(rows)
    tok_own[...] = lax.dot_general(
        narrow(tok_ref[...].astype(jnp.float32)), pick, (((1,), (1,)), ((), ())), preferred_element_type=jnp.float32
    )

    def fill(send, q, pairs):
        for side in range(2):
            mine = slice(side * half, (side + 1) * half)
            send[q + side] = jnp.concatenate(
                [jnp.concatenate([a[:, mine], b[:, mine]], axis=1) for a, b in pairs], axis=0
            )

    loads[0].wait()
    for q in range(0, peers, 2):
        value, gate1, gate2 = [w_ref[:, j * width + q * half : j * width + (q + 2) * half] for j in range(3)]
        for part in range(2):
            low, mid, high = part * half // 2, part * half // 2 + half // 4, (part + 1) * half // 2
            fill(w_send.at[part], q, [(value[low:high], gate2[low:high]), (gate1[low:mid], gate1[mid:high])])
    pl.semaphore_wait(barrier, peers)
    to_tok.start()
    to_w.start()
    loads[1].wait()
    turned = narrow(dot(pick, cot_ref[...]))
    for q in range(0, peers, 2):
        steps = [turned[p * block : (p + 1) * block, q * half : (q + 2) * half] for p in range(4)]
        fill(cot_send, q, [(steps[0], steps[1]), (steps[2], steps[3])])
    to_cot.start()

    loads[2].wait()
    col = lax.broadcasted_iota(jnp.int32, (CODES, table.shape[0]), 1)
    col = col - lax.broadcasted_iota(jnp.int32, (CODES, table.shape[0]), 0)
    count = 4
    for field in range(0, fields, count):
        chosen = [narrow(jnp.where(col == offsets[field + s], 1.0, 0.0)) for s in range(count)]
        found = dot(jnp.concatenate(chosen, axis=0), table[...])
        used[field * CODES : (field + count) * CODES, :] = narrow(found)
    for load in loads[3:6]:
        load.wait()
    filter_spectrum(filters, forward, twist, series, bins, filt_re, filt_im)

    to_tok.wait_recv()
    lanes = lax.broadcasted_iota(jnp.int32, (rows, CODES), 1).astype(jnp.float32)

    def embed(i, carry):
        hot = []
        for s in range(2):
            steps = tok_got[2 * i + s].T
            hot.append(
                jnp.concatenate(
                    [
                        narrow(jnp.where(steps[:, field : field + 1] == lanes, 1.0, 0.0))
                        for field in range(fields)
                    ],
                    axis=1,
                )
            )
        summed = dot(jnp.concatenate(hot, axis=0), used[...])
        rounded = narrow(summed)
        for s in range(2):
            for p in range(4):
                start = s * rows + p * block
                emb[p, 2 * i + s] = rounded[start : start + block]
        return carry

    ahead_of_w = 2
    lax.fori_loop(0, ahead_of_w, embed, 0, unroll=2)
    to_w.wait_recv()
    relay = pltpu.make_async_remote_copy(
        src_ref=w_got.at[group],
        dst_ref=w_got.at[group],
        send_sem=relay_sems.at[0],
        recv_sem=relay_sems.at[1],
        device_id=(1 - group, me),
        device_id_type=pl.DeviceIdType.MESH,
    )
    relay.start()
    lax.fori_loop(ahead_of_w, peers // 2, embed, 0, unroll=3)
    loads[6].wait()

    relay.wait_recv()
    near = left_lanes(half // 4)
    for peer in range(peers):
        for part in range(2):
            start = peer * half + part * half // 2
            own = slice(start, start + half // 2)
            w_own[own, :LANES] = w_got[part, peer, : half // 2]
            gate = widen(w_got[part, peer, half // 2 :])
            other = swap(gate)
            both = jnp.concatenate([jnp.where(near, gate, other), jnp.where(near, other, gate)], axis=0)
            w_own[own, LANES:] = narrow(both)
    place = pl.multiple_of(me // 2 * LANES, LANES)
    odd = me % 2 == 1
    near3 = left_lanes(3)
    own_taps = []
    for j in range(3):
        piece = taps_ref[:, pl.ds(pl.multiple_of(place + j * width, LANES), LANES)]
        own_taps.append(jnp.where(odd, swap(piece), piece))
    taps = jnp.concatenate(
        [jnp.where(near3, own_taps[0], swap(own_taps[2])), jnp.where(near3, own_taps[1], swap(own_taps[1]))], axis=1
    )
    tap = [taps[j : j + 1] for j in range(3)]

    for p in range(4):
        proj[p] = widen(narrow(dot(emb[p].reshape(quarter, width), w_own[...])))

    def back_by(p, steps):
        return proj[p - steps] if p >= steps else shifted(proj[p - steps + 4], 1)

    for p in range(4):
        mixed = widen(narrow(tap[0] * proj[p] + tap[1] * back_by(p, 1) + tap[2] * back_by(p, 2)))
        gates[p] = mixed[:, :LANES]
        first_gate[p] = mixed[:, LANES:]
    to_cot.wait_recv()
    left = left_lanes(quarter)
    for p in range(0, 4, 2):
        steps = widen(cot_got[:, p // 2 * block : (p // 2 + 1) * block, :].reshape(quarter, LANES))
        upstream[p] = jnp.where(left, 1.0, swap(steps))
        upstream[p + 1] = jnp.where(left, 1.0, steps)
    for p in range(4):
        series[:, lanes_of(p)] = narrow(gates[p] * upstream[p])

    matmul_rows(forward, series, bins)
    first_product(bins, twist, filt_re, filt_im, spec_re, spec_im, packed)
    matmul_rows(inverse, packed, wave)
    for p in range(4):
        out = widen(narrow(wave[:, lanes_of(p)]))
        flipped = swap(out)
        series[:, lanes_of(p)] = narrow(flipped * first_gate[p])
        grad_b[p] = widen(narrow(out * flipped))

    matmul_rows(forward, series, bins)
    second_product(bins, twist, filt_re, filt_im, spec_re, spec_im, packed, lagged)
    matmul_rows(inverse, packed, wave)
    mixed = []
    for p in range(4):
        out = widen(narrow(wave[:, lanes_of(p)]))
        mixed.append(gates[p] * out)
        grad_a[p] = widen(narrow(upstream[p] * out))
    for p in range(0, 4, 2):
        start = p // 2 * block
        both = narrow(jnp.where(left, swap(mixed[p]), mixed[p + 1]))
        mix_back[:, start : start + block, :] = both.reshape(peers, block, LANES)
    to_mix.start()

    def ahead(grad, p, steps):
        return grad[p + steps] if p + steps < 4 else shifted(grad[p + steps - 4], -1)

    sums = []
    for grad, own in ((grad_a, slice(0, LANES)), (grad_b, slice(LANES, 2 * LANES))):
        total = [jnp.zeros((1, LANES), jnp.float32)] * 3
        for p in range(4):
            here = grad[p]
            out = tap[0][:, own] * here + tap[1][:, own] * ahead(grad, p, 1) + tap[2][:, own] * ahead(grad, p, 2)
            grad_proj[own, p * quarter : (p + 1) * quarter] = narrow(out.T)
            for j in range(3):
                lag = proj[p - j, :, own] if p >= j else shifted(proj[p - j + 4, :, own], 1)
                total[j] = total[j] + jnp.sum(here * lag, axis=0, keepdims=True)
        sums += total
    tap_own[...] = jnp.concatenate(sums + [jnp.zeros((2, LANES), jnp.float32)], axis=0)
    tap_got[core, chip] = tap_own[...]
    for copy in to_tap:
        copy.start()

    near = left_lanes(half // 2)
    count = 4
    sends = list(to_out.copies())
    for step in (1, 2, 3, 0):
        first = (me // count ^ step) * count
        own = pl.ds(pl.multiple_of(first * half, count * half), count * half)
        steps = emb[:, :, :, own].reshape(peers * rows, count * half)
        terms = dot(grad_proj[...], steps).T
        for s in range(count):
            here = terms[s * half : (s + 1) * half]
            back[first + s, :half, :] = narrow(here[:, :LANES])
            twin = here[:, LANES:]
            back[first + s, half:, :] = narrow(jnp.where(near, twin[: half // 2], twin[half // 2 :]))
        for d in range(max(1, step * count), (step + 1) * count):
            sends[d - 1].start()
    to_out.own().start()

    matmul_rows(inverse, lagged, wave)
    part = quarter // 4
    order = pick_quarter(quarter)
    for b in range(4):
        lags = jnp.concatenate(
            [wave[b * part : (b + 1) * part, lanes_of(p)].T for p in range(4)], axis=1
        )
        high = narrow(lags)
        rest = narrow(lags - widen(high))
        out = dot(high, order) + dot(rest, order)
        span = slice(b * quarter, (b + 1) * quarter)
        lags_by_channel[0, :, span] = out[:half]
        lags_by_channel[1, :, span] = out[half:]
    leave = pltpu.make_async_copy(lags_by_channel, lag_out, lag_sem)
    leave.start()

    for copy in to_tap:
        copy.wait_recv()
    tap_pair.start()
    tap_pair.wait_recv()
    tap_leave = pltpu.make_async_copy(tap_got, tap_home, tap_sem)
    tap_leave.start()
    for exchange in (to_mix, to_out):
        exchange.wait_recv()
    for exchange in (to_tok, to_w, to_cot, to_mix, to_out):
        exchange.wait_send()
    for copy in to_tap + [tap_pair]:
        copy.wait_send()
    tap_leave.wait()
    relay.wait_send()
    leave.wait()


def unpack_kernel(
    mix_hbm, hbm, tap_hbm, lags, mixer_out, weight_out, tap_out, filter_out, mix_home, home, tap_home, sems
):
    peers, block, _ = mix_home.shape
    block = block // 2
    half = LANES // 2
    width = peers * half
    loads = [
        pltpu.make_async_copy(source, target, sems.at[i])
        for i, (source, target) in enumerate(
            [(mix_hbm, mix_home), (tap_hbm, tap_home), (hbm, home), (lags, filter_out)]
        )
    ]
    for load in loads:
        load.start()
    loads[0].wait()
    columns = []
    for q in range(0, peers, 2):
        one, two = mix_home[q], mix_home[q + 1]
        pieces = []
        for p in range(4):
            at = slice(p // 2 * block, (p // 2 + 1) * block)
            mine = slice(p % 2 * half, (p % 2 + 1) * half)
            pieces.append(jnp.concatenate([one[at, mine], two[at, mine]], axis=1))
        columns.append(jnp.concatenate(pieces, axis=0))
    mixer_out[...] = narrow(
        lax.dot_general(
            pick_quarter(4 * block),
            jnp.concatenate(columns, axis=1),
            (((0,), (0,)), ((), ())),
            preferred_element_type=jnp.float32,
        )
    )
    loads[1].wait()
    loads[2].wait()
    for q in range(0, peers, 2):
        start = q * half
        one, two = tap_home[0, q // 2], tap_home[1, q // 2]
        for j, (row, side) in enumerate(((0, 0), (3, 0), (0, 1))):
            mine = slice(side * half, (side + 1) * half)
            tap_out[:, j * width + start : j * width + start + LANES] = jnp.concatenate(
                [one[row : row + 3, mine], two[row : row + 3, mine]], axis=1
            )
        one, two = home[q], home[q + 1]
        for side in range(2):
            mine = slice(side * half, (side + 1) * half)
            column = 2 * side * width + start
            weight_out[:, column : column + LANES] = widen(
                jnp.concatenate([one[:half, mine], two[:half, mine]], axis=1)
            )
            at = slice(side * half // 2, (side + 1) * half // 2)
            weight_out[at, width + start : width + start + LANES] = widen(
                jnp.concatenate([one[half:, mine], two[half:, mine]], axis=1)
            )
    loads[3].wait()


def fast_local(token_ids, field_offsets, embed_table, w_in, short_taps, filters, cotangent):
    rows, width = cotangent.shape
    fields = token_ids.shape[1]
    peers = lax.axis_size("tm")
    length = rows * peers
    quarter = length // 4
    forward, inverse, twist = basis(quarter)
    whole = pl.BlockSpec(memory_space=pltpu.VMEM)
    anywhere = pl.BlockSpec(memory_space=pl.ANY)
    f32, bf16 = jnp.float32, jnp.bfloat16
    half = LANES // 2
    sems = pltpu.SemaphoreType.DMA((2, peers))
    wide = 4 * LANES
    scratch = [
        pltpu.VMEM(w_in.shape, bf16),
        pltpu.VMEM(cotangent.shape, bf16),
        pltpu.VMEM(embed_table.shape, bf16),
        pltpu.VMEM(filters.shape, bf16),
        pltpu.VMEM(forward.shape, bf16),
        pltpu.VMEM(inverse.shape, bf16),
        pltpu.VMEM(twist.shape, f32),
        pltpu.VMEM((fields, rows), f32),
        pltpu.VMEM((peers, fields, rows), f32),
        pltpu.VMEM((2, peers, half // 2 + half // 4, LANES), bf16),
        pltpu.VMEM((2, peers, half // 2 + half // 4, LANES), bf16),
        pltpu.VMEM((peers, rows // 2, LANES), bf16),
        pltpu.VMEM((peers, rows // 2, LANES), bf16),
        pltpu.VMEM((peers, rows // 2, LANES), bf16),
        pltpu.VMEM((peers, half + half // 2, LANES), bf16),
        pltpu.VMEM((8, LANES), f32),
        pltpu.VMEM((2, peers // 2, 8, LANES), f32),
        pltpu.VMEM((fields * CODES, width), bf16),
        pltpu.VMEM((4, peers, rows // 4, width), bf16),
        pltpu.VMEM((width, 2 * LANES), bf16),
        pltpu.VMEM((4, quarter, 2 * LANES), f32),
        pltpu.VMEM((4, quarter, LANES), f32),
        pltpu.VMEM((4, quarter, LANES), f32),
        pltpu.VMEM((4, quarter, LANES), f32),
        pltpu.VMEM((quarter, wide), bf16),
        pltpu.VMEM((2 * quarter, wide), f32),
        pltpu.VMEM((4, quarter + 8, LANES), f32),
        pltpu.VMEM((4, quarter + 8, LANES), f32),
        pltpu.VMEM((4, quarter + 8, LANES), f32),
        pltpu.VMEM((4, quarter + 8, LANES), f32),
        pltpu.VMEM((2 * quarter, wide), bf16),
        pltpu.VMEM((2 * quarter, wide), bf16),
        pltpu.VMEM((quarter, wide), f32),
        pltpu.VMEM((4, quarter, LANES), f32),
        pltpu.VMEM((4, quarter, LANES), f32),
        pltpu.VMEM((2 * LANES, length), bf16),
        pltpu.VMEM(filters.shape, f32),
        pltpu.SemaphoreType.DMA((7,)),
        pltpu.SemaphoreType.DMA,
        pltpu.SemaphoreType.DMA,
        pltpu.SemaphoreType.DMA((2,)),
    ] + [sems] * 6
    homes = pl.pallas_call(
        window_kernel,
        out_shape=(
            jax.ShapeDtypeStruct((peers, rows // 2, LANES), bf16),
            jax.ShapeDtypeStruct((peers, half + half // 2, LANES), bf16),
            jax.ShapeDtypeStruct((2, peers // 2, 8, LANES), f32),
            jax.ShapeDtypeStruct(filters.shape, f32),
        ),
        in_specs=[whole, pl.BlockSpec(memory_space=pltpu.SMEM), whole] + [anywhere] * 7,
        out_specs=(anywhere,) * 4,
        scratch_shapes=scratch,
        compiler_params=pltpu.CompilerParams(
            vmem_limit_bytes=VMEM, collective_id=0, has_side_effects=True
        ),
        name="window",
    )(
        token_ids.T,
        field_offsets,
        short_taps,
        w_in,
        cotangent,
        embed_table,
        filters,
        jnp.asarray(forward),
        jnp.asarray(inverse),
        jnp.asarray(twist),
    )
    return tuple(
        pl.pallas_call(
            unpack_kernel,
            out_shape=(
                jax.ShapeDtypeStruct((rows, width), bf16),
                jax.ShapeDtypeStruct((half, 3 * width), f32),
                jax.ShapeDtypeStruct((3, 3 * width), f32),
                jax.ShapeDtypeStruct(filters.shape, f32),
            ),
            in_specs=[anywhere] * 4,
            out_specs=(whole,) * 4,
            scratch_shapes=[pltpu.VMEM(home.shape, home.dtype) for home in homes[:3]]
            + [pltpu.SemaphoreType.DMA((4,))],
            compiler_params=pltpu.CompilerParams(vmem_limit_bytes=VMEM),
            name="unpack",
        )(*homes)
    )


def cis_tables(count_a, count_b, modulus):
    left = jnp.arange(count_a, dtype=jnp.int32)[:, None]
    right = jnp.arange(count_b, dtype=jnp.int32)[None, :]
    angle = 2.0 * math.pi / modulus * (left * right % modulus).astype(jnp.float32)
    return (jnp.cos(angle), jnp.sin(angle))


class Factored:
    def __init__(self, total):
        bits = total.bit_length() - 1
        first_len = 1 << (bits + 1) // 2
        second_len = total // first_len
        first_cos, first_sin = cis_tables(first_len, first_len // 2, first_len)
        second_cos, second_sin = cis_tables(second_len, second_len, second_len)
        self.total = total
        self.second_len = second_len
        self.twist_cos, self.twist_sin = cis_tables(first_len, second_len, total)
        self.first_both = jnp.concatenate([first_cos, -first_sin], axis=0)
        self.forward = jnp.block([[second_cos, -second_sin], [second_sin, second_cos]])
        self.inverse = jnp.block([[second_cos, second_sin], [-second_sin, second_cos]])

    def spectrum(self, series):
        series = widen(series)
        channels, length = series.shape
        rows_k = self.twist_cos.shape[0]
        half = self.first_both.shape[1]
        blocks = series.reshape(channels, half, length // half)
        part = jnp.einsum("ka,cab->ckb", self.first_both, blocks)
        part_re = part[:, :rows_k]
        part_im = part[:, rows_k:]
        turn_re = part_re * self.twist_cos + part_im * self.twist_sin
        turn_im = part_im * self.twist_cos - part_re * self.twist_sin
        turned = jnp.concatenate([turn_re, turn_im], axis=2)
        result = jnp.einsum("ckb,bm->ckm", turned, self.forward)
        return (result[:, :, : self.second_len], result[:, :, self.second_len :])

    def product(self, left, right, conjugate):
        left_re, left_im = left
        right_re, right_im = right
        if conjugate:
            right_im = -right_im
        return (left_re * right_re - left_im * right_im, left_re * right_im + left_im * right_re)

    def signal(self, pair):
        joined = jnp.concatenate(pair, axis=2)
        back = jnp.einsum("ckm,mb->ckb", joined, self.inverse)
        back_re = back[:, :, : self.second_len]
        back_im = back[:, :, self.second_len :]
        turn_re = back_re * self.twist_cos - back_im * self.twist_sin
        turn_im = back_im * self.twist_cos + back_re * self.twist_sin
        turned = jnp.concatenate([turn_re, turn_im], axis=1)
        blocks = jnp.einsum("ka,ckb->cab", self.first_both, turned)
        return blocks.reshape(joined.shape[0], -1) * (1.0 / self.total)


def delayed(array, steps):
    length = array.shape[1]
    return jnp.pad(array, ((0, 0), (steps, 0)))[:, :length]


def advanced(array, steps):
    return jnp.pad(array, ((0, 0), (0, steps)))[:, steps:]


def wide_local(token_ids, field_offsets, embed_table, w_in, short_taps, filters, cotangent):
    rows, width = cotangent.shape
    fields = token_ids.shape[1]
    peers = lax.axis_size("tm")
    me = lax.axis_index("tm")
    chans = width // peers
    length = rows * peers
    vocab = embed_table.shape[0]

    w_part = w_in.reshape(chans, 3, peers, chans).transpose(2, 0, 1, 3).reshape(peers, chans, 3 * chans)
    cot_part = cotangent.reshape(rows, peers, chans).transpose(1, 2, 0)
    tok_part = narrow(token_ids).T.reshape(1, chans, -1)
    tok_part = jnp.broadcast_to(tok_part, (peers,) + tok_part.shape[1:])
    sent = jnp.concatenate([w_part, cot_part, tok_part], axis=2)
    got = lax.all_to_all(sent, "tm", split_axis=0, concat_axis=0, tiled=True)
    w_own = got[:, :, : 3 * chans].reshape(width, 3 * chans)
    upstream = widen(got[:, :, 3 * chans : 3 * chans + rows].transpose(1, 0, 2).reshape(chans, length))
    tokens = got[:, :, 3 * chans + rows :].reshape(peers, fields, rows)
    tokens = tokens.transpose(1, 0, 2).reshape(fields, length).astype(jnp.int32)
    row_index = tokens + field_offsets[:, None]

    codes = lax.broadcasted_iota(jnp.int32, (vocab, length), 0)
    counts = jnp.zeros((vocab, length), jnp.float32)
    for field in range(fields):
        counts = counts + jnp.where(codes == row_index[field][None, :], 1.0, 0.0)
    embedded = narrow(
        jnp.einsum("vr,vt->rt", embed_table, narrow(counts), preferred_element_type=jnp.float32)
    )
    proj = narrow(jnp.einsum("rc,rt->ct", w_own, embedded, preferred_element_type=jnp.float32))
    taps = lax.dynamic_index_in_dim(short_taps.reshape(3, 3, peers, chans), me, 2, keepdims=False)
    taps = taps.reshape(3, 3 * chans, 1)
    proj_wide = widen(proj)
    lags = (proj_wide, delayed(proj_wide, 1), delayed(proj_wide, 2))
    mixed = narrow(taps[0] * lags[0] + taps[1] * lags[1] + taps[2] * lags[2])
    values = mixed[:chans]
    first_gate = widen(mixed[chans : 2 * chans])
    second_gate = widen(mixed[2 * chans :])

    transform = Factored(2 * length)

    def spectra(*series):
        whole = transform.spectrum(jnp.concatenate(series, axis=0))
        return [
            tuple(part[i * chans : (i + 1) * chans] for part in whole) for i in range(len(series))
        ]

    def signals(*pairs):
        whole = transform.signal(tuple(jnp.concatenate(parts, axis=0) for parts in zip(*pairs)))
        return [whole[i * chans : (i + 1) * chans] for i in range(len(pairs))]

    grad_conv2 = narrow(upstream * second_gate)
    first_spec, second_spec, value_spec, grad_spec2 = spectra(
        filters[0], filters[1], values, grad_conv2
    )
    first_conv, grad_mix = signals(
        transform.product(value_spec, first_spec, False),
        transform.product(grad_spec2, second_spec, True),
    )
    first_conv = widen(narrow(first_conv))
    grad_mix = widen(narrow(grad_mix))
    first_mix = narrow(first_gate * first_conv)
    grad_gate1 = narrow(grad_mix * first_conv)
    grad_conv1 = narrow(grad_mix * first_gate)
    mix_spec, grad_spec1 = spectra(first_mix, grad_conv1)
    second_conv, grad_values, filter_one, filter_two = signals(
        transform.product(mix_spec, second_spec, False),
        transform.product(grad_spec1, first_spec, True),
        transform.product(grad_spec1, value_spec, True),
        transform.product(grad_spec2, mix_spec, True),
    )
    second_conv = widen(narrow(second_conv))
    mixer_out = narrow(second_gate * second_conv)
    grad_gate2 = narrow(upstream * second_conv)
    filter_grads = jnp.stack([filter_one, filter_two], axis=0)
    grad_mixed = jnp.concatenate([narrow(grad_values), grad_gate1, grad_gate2], axis=0)
    grad_wide = widen(grad_mixed)
    grad_proj = narrow(
        taps[0] * grad_wide + taps[1] * advanced(grad_wide, 1) + taps[2] * advanced(grad_wide, 2)
    )
    tap_terms = jnp.stack([jnp.sum(grad_wide * lag, axis=1) for lag in lags], axis=0)
    weight_terms = narrow(
        jnp.einsum("rt,ct->rc", embedded, grad_proj, preferred_element_type=jnp.float32)
    )

    weight_part = weight_terms.reshape(peers, chans, 3 * chans)
    mixer_part = mixer_out.reshape(chans, peers, rows).transpose(1, 0, 2)
    tap_part = narrow(tap_terms).reshape(1, chans, -1)
    tap_part = jnp.broadcast_to(tap_part, (peers,) + tap_part.shape[1:])
    back = lax.all_to_all(
        jnp.concatenate([weight_part, mixer_part, tap_part], axis=2),
        "tm",
        split_axis=0,
        concat_axis=0,
        tiled=True,
    )
    weight_grads = widen(
        back[:, :, : 3 * chans].reshape(peers, chans, 3, chans).transpose(1, 2, 0, 3)
    ).reshape(chans, 3 * width)
    mixer_rows = back[:, :, 3 * chans : 3 * chans + rows].reshape(width, rows).T
    tap_grads = widen(
        back[:, :, 3 * chans + rows :].reshape(peers, 3, 3, chans).transpose(1, 2, 0, 3)
    ).reshape(3, 3 * width)
    return (mixer_rows, weight_grads, tap_grads, filter_grads)


def solution(mesh):
    return jax.shard_map(
        local,
        mesh=mesh,
        in_specs=(
            P(("groups", "tm"), None),
            P("groups"),
            P(),
            P("tm", None),
            P(),
            P(None, "tm", None),
            P(("groups", "tm"), None),
        ),
        out_specs=(
            P(("groups", "tm"), None),
            P(("groups", "tm"), None),
            P("groups", None),
            P("groups", "tm", None),
        ),
        check_vma=False,
    )
```
